128 devices in a mesh: ulysses: 4 (over z_lo, core), blk: 32 (over x, z_hi, y).
Axes of the slice: x: 4, y: 4, z: 4 (z_hi: 2, z_lo: 2; z = z_hi * 2 + z_lo), core: 2. Of those that a mesh axis runs over, the one named last changes fastest.
Arguments:
- tokens: bfloat16 [16384, 768], P(('blk', 'ulysses')), may hold values from -6 to 6
- cotangent: bfloat16 [16384, 768], P(('blk', 'ulysses')), may hold values from -6 to 6
- segments: int32 [16384], P('blk'), may hold values from 0 to 31, never falling along the last dimension, each value on 1 to 1024 neighbouring positions
- first_gain: bfloat16 [768], P(('ulysses', 'blk')), may hold values from 0.5 to 1.5
- first_shift: bfloat16 [768], P(('ulysses', 'blk')), may hold values from -1.5 to 1.5
- input_weight: bfloat16 [768, 2304], P(('ulysses', 'blk')), may hold values from -0.21875 to 0.21875
- query_bias: bfloat16 [768], P(('ulysses', 'blk')), may hold values from -2.5 to 2.5
- value_bias: bfloat16 [768], P(('ulysses', 'blk')), may hold values from -0.25 to 0.25
- output_weight: bfloat16 [768, 768], P(('ulysses', 'blk')), may hold values from -3.5 to 3.5
- output_bias: bfloat16 [768], P(('ulysses', 'blk')), may hold values from -1.5 to 1.5
- second_gain: bfloat16 [768], P(('ulysses', 'blk')), may hold values from 0.5 to 1.5
- second_shift: bfloat16 [768], P(('ulysses', 'blk')), may hold values from -1.5 to 1.5
- expand_weight: bfloat16 [768, 3072], P(('ulysses', 'blk')), may hold values from -0.21875 to 0.21875
- expand_bias: bfloat16 [3072], P(('ulysses', 'blk')), may hold values from -1.5 to 1.5
- reduce_weight: bfloat16 [3072, 768], P(('ulysses', 'blk')), may hold values from -0.15625 to 0.15625
- reduce_bias: bfloat16 [768], P(('ulysses', 'blk')), may hold values from -1.5 to 1.5
Outputs:
- layer_out: bfloat16 [16384, 768], P(('blk', 'ulysses'))
- grad_input: float32 [16384, 768], P(('blk', 'ulysses'))
- first_gain_grad: float32 [768], P(('ulysses', 'blk'))
- first_shift_grad: float32 [768], P(('ulysses', 'blk'))
- input_weight_grad: float32 [768, 2304], P(('ulysses', 'blk'))
- query_bias_grad: float32 [768], P(('ulysses', 'blk'))
- value_bias_grad: float32 [768], P(('ulysses', 'blk'))
- output_weight_grad: float32 [768, 768], P(('ulysses', 'blk'))
- output_bias_grad: float32 [768], P(('ulysses', 'blk'))
- second_gain_grad: float32 [768], P(('ulysses', 'blk'))
- second_shift_grad: float32 [768], P(('ulysses', 'blk'))
- expand_weight_grad: float32 [768, 3072], P(('ulysses', 'blk'))
- expand_bias_grad: float32 [3072], P(('ulysses', 'blk'))
- reduce_weight_grad: float32 [3072, 768], P(('ulysses', 'blk'))
- reduce_bias_grad: float32 [768], P(('ulysses', 'blk'))
The draws below stay inside these ranges and needn't reach their ends.
Inputs may be any that keep to these rules, and one draw needn't show every extreme that they name: `segments`: document numbers never fall along the sequence; each document holds 1 to 1024 tokens, one of them exactly 1024.
All inputs are finite; a program needn't handle non-finite values.
Results may differ from the reference program's by a relative error of at most 0.015.
Values may be sent and summed in bfloat16 or wider, within the bound.
No kernel may reach another device: no remote copies, remote signals or barrier semaphores. Data moves between devices by JAX's collectives and lax.ppermute only.
A program may use at most 128 MiB of HBM per device.

```python
import math
from functools import partial
import jax
import jax.numpy as jnp
import numpy as np
from jax import lax

D = 768
H = 12
HD = 64
FF = 3072
SEQ = 16384
DOC_MOST = 1024
QB = 512
DEVICES = 128


def level_of(rng, shape, split, smallest, high):
    factor_of, own = 1.0, jax.random.fold_in(rng, 6)
    for position, shards_of in split:
        steps = jnp.exp(jax.random.uniform(jax.random.fold_in(own, position), (shards_of,), jnp.float32, smallest / len(split), high / len(split)))
        factor_of = factor_of * jnp.repeat(steps, shape[position] // shards_of).reshape([-1 if axis == position else 1 for axis in range(len(shape))])
    return factor_of


def split_up(number_of, total, most, slope):
    weights = [(1 << 20) // math.isqrt(standing ** slope) + 1 for standing in range(2, number_of + 1)]
    spare, counts = total - most - (number_of - 1), [1] * (number_of - 1)
    while spare > 0:
        candidates = [i for i in range(number_of - 1) if counts[i] < most]
        whole, left = sum([weights[i] for i in candidates]), spare
        for i in candidates:
            extra = min(most - counts[i], max(1, left * weights[i] // whole), spare)
            counts[i] = counts[i] + extra
            spare = spare - extra
    return np.array([most] + counts)


def ragged_sizes(rng, amount, total, bound, slope):
    if amount == 2:
        one = jax.random.randint(rng, (), max(1, total - bound), min(bound, total - 1) + 1)
        return jnp.stack([one, total - one])
    tallies = jnp.asarray(split_up(amount, total, bound, slope), jnp.int32)
    pairs = (amount - 1) // 2
    source_of, sink = tallies[1:1 + 2 * pairs:2], tallies[2:2 + 2 * pairs:2]
    slack = jnp.minimum(source_of - 1, bound - sink)
    passed = jax.random.randint(jax.random.fold_in(rng, 1), (pairs,), 0, 1 << 20) % (slack + 1)
    tallies = tallies.at[1:1 + 2 * pairs:2].set(source_of - passed).at[2:2 + 2 * pairs:2].set(sink + passed)
    return tallies[jax.random.permutation(jax.random.fold_in(rng, 2), amount)]


def gaussian(key, dims, spread, bound, shards=(), kind=jnp.bfloat16):
    drawn = spread * jax.random.normal(key, dims, jnp.float32)
    if shards:
        drawn = drawn * level_of(key, dims, shards, -0.22, 0.18)
    return jnp.clip(drawn, -bound, bound).astype(kind)


def setup_inputs(seed: int = 0) -> dict:
    arg_keys = jax.random.split(jax.random.key(seed), 17)
    tokens = gaussian(arg_keys[0], (SEQ, D), 1.0, 6.0, ((0, 128),))
    cotangent = gaussian(arg_keys[1], (SEQ, D), 1.0, 6.0, ((0, 128),))
    segments = jnp.searchsorted(jnp.cumsum(ragged_sizes(arg_keys[2], DEVICES // 4, SEQ, DOC_MOST, 1)), jnp.arange(SEQ), side="right").astype(jnp.int32)
    first_gain = jnp.clip(1.0 + 0.1 * jax.random.normal(arg_keys[3], (D,), jnp.float32), 0.5, 1.5).astype(jnp.bfloat16)
    first_shift = gaussian(arg_keys[4], (D,), 0.3, 1.5, ((0, 128),))
    input_weight = gaussian(arg_keys[5], (D, 3 * D), D ** -0.5, 0.21875, ((0, 128),))
    query_bias = gaussian(arg_keys[6], (D,), 0.5, 2.5, ((0, 128),))
    value_bias = gaussian(arg_keys[7], (D,), 0.05, 0.25, ((0, 128),))
    output_weight = gaussian(arg_keys[8], (D, D), (max(1, 4 * D // DOC_MOST)) ** -0.5, 3.5, ((0, 128),))
    output_bias = gaussian(arg_keys[9], (D,), 0.3, 1.5, ((0, 128),))
    second_gain = jnp.clip(1.0 + 0.1 * jax.random.normal(arg_keys[10], (D,), jnp.float32), 0.5, 1.5).astype(jnp.bfloat16)
    second_shift = gaussian(arg_keys[11], (D,), 0.3, 1.5, ((0, 128),))
    expand_weight = gaussian(arg_keys[12], (D, FF), D ** -0.5, 0.21875, ((0, 128),))
    expand_bias = gaussian(arg_keys[13], (FF,), 0.3, 1.5, ((0, 128),))
    reduce_weight = gaussian(arg_keys[14], (FF, D), (FF // 2) ** -0.5, 0.15625, ((0, 128),))
    reduce_bias = gaussian(arg_keys[15], (D,), 0.3, 1.5, ((0, 128),))
    return {"tokens": tokens, "cotangent": cotangent, "segments": segments, "first_gain": first_gain, "first_shift": first_shift, "input_weight": input_weight, "query_bias": query_bias, "value_bias": value_bias, "output_weight": output_weight, "output_bias": output_bias, "second_gain": second_gain, "second_shift": second_shift, "expand_weight": expand_weight, "expand_bias": expand_bias, "reduce_weight": reduce_weight, "reduce_bias": reduce_bias}


@jax.custom_vjp
def low(v):
    return lax.optimization_barrier(v.astype(jnp.bfloat16)).astype(jnp.float32)

@jax.custom_vjp
def low_back(v):
    return v

def low_keep(v):
    return (low(v), None)

def low_pass(kept, grad):
    return (grad,)

def back_keep(v):
    return (v, None)

def back_low(kept, grad):
    return (low(grad),)
low.defvjp(low_keep, low_pass)
low_back.defvjp(back_keep, back_low)

def layer_norm(values, gain, shift):
    centered = values - lax.optimization_barrier(jnp.mean(values, -1, keepdims=True))
    scale = lax.rsqrt(lax.optimization_barrier(jnp.mean(centered * centered, -1, keepdims=True)) + 1e-05)
    return centered * scale * gain + shift

def smooth_gate(hidden):
    return 0.5 * hidden * (1.0 + jnp.tanh(0.7978845608 * (hidden + 0.044715 * hidden * hidden * hidden)))

def attend_block(inputs):
    query, keys, vals, seg_query, seg_keys, pos_query, pos_keys = inputs
    scores = low_back(0.125 * jnp.einsum('qhd,khd->hqk', query, keys, precision=lax.Precision.HIGHEST))
    allowed = (seg_query[:, None] == seg_keys[None, :]) & (pos_keys[None, :] <= pos_query[:, None])
    scores = jnp.where(allowed[None], scores, -1e+30)
    top = lax.optimization_barrier(jnp.max(scores, -1, keepdims=True))
    expo = jnp.exp(scores - top)
    probs = low(expo / lax.optimization_barrier(jnp.sum(expo, -1, keepdims=True)))
    return jnp.einsum('hqk,khd->qhd', probs, vals, precision=lax.Precision.HIGHEST)

def attention(query, keys, vals, segments):
    count = SEQ // QB
    reach = DOC_MOST // QB
    padding = jnp.zeros((DOC_MOST, H, HD), jnp.float32)
    keys_pad = jnp.concatenate([padding, keys], 0)
    vals_pad = jnp.concatenate([padding, vals], 0)
    seg_pad = jnp.concatenate([jnp.full((DOC_MOST,), -1, jnp.int32), segments.astype(jnp.int32)], 0)
    pos_pad = jnp.arange(SEQ + DOC_MOST, dtype=jnp.int32) - DOC_MOST

    def windows(whole):
        pieces = whole.reshape((count + reach, QB) + whole.shape[1:])
        return jnp.concatenate([pieces[offset:offset + count] for offset in range(reach + 1)], axis=1)
    result = lax.map(jax.checkpoint(attend_block), (query.reshape(count, QB, H, HD), windows(keys_pad), windows(vals_pad), segments.astype(jnp.int32).reshape(count, QB), windows(seg_pad), jnp.arange(SEQ, dtype=jnp.int32).reshape(count, QB), windows(pos_pad)))
    return result.reshape(SEQ, H, HD)

def forward(segments, values, first_gain, first_shift, input_weight, query_bias, value_bias, output_weight, output_bias, second_gain, second_shift, expand_weight, expand_bias, reduce_weight, reduce_bias):
    highest = lax.Precision.HIGHEST
    lowered_one = low(layer_norm(values, first_gain, first_shift))
    mixed = jnp.dot(lowered_one, input_weight, precision=highest)
    mixed = mixed + jnp.concatenate([query_bias, jnp.zeros_like(query_bias), value_bias])
    parts = low(low_back(mixed)).reshape(SEQ, 3, H, HD)
    attended = attention(parts[:, 0], parts[:, 1], parts[:, 2], segments)
    attended = low(low_back(attended)).reshape(SEQ, D)
    branch = low_back(jnp.dot(attended, output_weight, precision=highest) + output_bias)
    middle = values + branch
    lowered_two = low(layer_norm(middle, second_gain, second_shift))
    hidden = low_back(jnp.dot(lowered_two, expand_weight, precision=highest) + expand_bias)
    active = low(smooth_gate(hidden))
    return middle + low_back(jnp.dot(active, reduce_weight, precision=highest) + reduce_bias)

def reference(tokens, cotangent, segments, first_gain, first_shift, input_weight, query_bias, value_bias, output_weight, output_bias, second_gain, second_shift, expand_weight, expand_bias, reduce_weight, reduce_bias):
    params = [first_gain, first_shift, input_weight, query_bias, value_bias, output_weight, output_bias, second_gain, second_shift, expand_weight, expand_bias, reduce_weight, reduce_bias]
    params = [item.astype(jnp.float32) for item in params]
    result, pullback = jax.vjp(partial(forward, segments), tokens.astype(jnp.float32), *params)
    grads = pullback(cotangent.astype(jnp.float32))
    return (result.astype(jnp.bfloat16), grads[0], grads[1], grads[2], grads[3], grads[4], grads[5], grads[6], grads[7], grads[8], grads[9], grads[10], grads[11], grads[12], grads[13])
```

```python
import jax
import jax.numpy as jnp
from jax import lax
from jax.sharding import Mesh
from jax.sharding import PartitionSpec as P

HD = 64
CHIPS = ("zl", "x", "zh", "y")
BF = jnp.bfloat16
F32 = jnp.float32


def chip_shift(value, distance):
    def at(place):
        place = place % 64
        zl, rest = place % 2, place // 2
        y, rest = rest % 4, rest // 4
        zh, x = rest % 2, rest // 2
        return ((zl * 4 + x) * 2 + zh) * 4 + y

    return lax.ppermute(value, CHIPS, [(at(t), at(t + distance)) for t in range(64)])


def swap(value):
    return lax.ppermute(value, "c", [(0, 1), (1, 0)])


def ring_shift(value, axis, distance):
    if axis == "z":
        place = [0, 2, 1, 3]
        return lax.ppermute(
            value, ("zl", "zh"), [(place[i], place[(i + distance) % 4]) for i in range(4)]
        )
    return lax.ppermute(value, axis, [(i, (i + distance) % 4) for i in range(4)])


def ring_place(axis):
    if axis == "z":
        return lax.axis_index("zh") * 2 + lax.axis_index("zl")
    return lax.axis_index(axis)


def gather_ring(value, axis):
    me = ring_place(axis)
    out = jnp.zeros((4,) + value.shape, value.dtype)
    pieces = [(ring_shift(value, axis, d), (me - d) % 4) for d in (1, 3, 2)]
    out = lax.dynamic_update_index_in_dim(out, value, me, 0)
    for piece, index in pieces:
        out = lax.dynamic_update_index_in_dim(out, piece, index, 0)
    return out


def scatter_ring(value, axis):
    me = ring_place(axis)
    total = lax.dynamic_index_in_dim(value, me, 0, keepdims=False).astype(F32)
    sent = [
        ring_shift(lax.dynamic_index_in_dim(value, (me + d) % 4, 0, keepdims=False), axis, d)
        for d in (1, 3, 2)
    ]
    for piece in sent:
        total = total + piece.astype(F32)
    return total


def norm_forward(values, gain, shift):
    centered = values - jnp.mean(values, -1, keepdims=True)
    scale = lax.rsqrt(jnp.mean(centered * centered, -1, keepdims=True) + 1e-05)
    unit = centered * scale
    return unit * gain + shift, unit, scale


def norm_backward(grad_out, unit, scale, gain):
    scaled = grad_out * gain
    return scale * (
        scaled
        - jnp.mean(scaled, -1, keepdims=True)
        - unit * jnp.mean(scaled * unit, -1, keepdims=True)
    )


def smooth_gate(hidden):
    return (
        0.5
        * hidden
        * (1.0 + jnp.tanh(0.7978845608 * (hidden + 0.044715 * hidden * hidden * hidden)))
    )


def dot(left, right):
    return jnp.dot(left, right, preferred_element_type=F32)


def outer_sum(left, right):
    return lax.dot_general(left, right, (((0,), (0,)), ((), ())), preferred_element_type=F32)


def back_project(left, weight):
    return lax.dot_general(left, weight, (((1,), (1,)), ((), ())), preferred_element_type=F32)


def pick(value, index, axis):
    return lax.dynamic_index_in_dim(value, index, axis, keepdims=False)


def by_core(core, mine, other, axis):
    first = jnp.where(core == 0, mine, other)
    second = jnp.where(core == 0, other, mine)
    return jnp.stack([first, second], axis)


def local(
    tokens,
    cotangent,
    segments,
    first_gain,
    first_shift,
    input_weight,
    query_bias,
    value_bias,
    output_weight,
    output_bias,
    second_gain,
    second_shift,
    expand_weight,
    expand_bias,
    reduce_weight,
    reduce_bias,
):
    core = lax.axis_index("c")
    zl = lax.axis_index("zl")
    chip = ((lax.axis_index("x") * 2 + lax.axis_index("zh")) * 4 + lax.axis_index("y")) * 2 + zl
    seg_own = lax.dynamic_slice_in_dim(segments, (zl * 2 + core) * 128, 128).astype(BF)
    seg_rows = jnp.pad(seg_own[None], ((0, 7), (0, 640)))
    ext = jnp.concatenate([tokens, seg_rows], 0)
    halo = [chip_shift(ext, d) for d in (4, 3, 2, 1)]
    small = jnp.concatenate(
        [
            jnp.stack(
                [
                    first_gain,
                    first_shift,
                    query_bias,
                    value_bias,
                    output_bias,
                    second_gain,
                    second_shift,
                    reduce_bias,
                ],
                1,
            ),
            expand_bias.reshape(6, 4),
            jnp.zeros((6, 116), BF),
        ],
        1,
    )
    in_halves = input_weight.reshape(6, 6, 2, 192)
    up_halves = expand_weight.reshape(6, 2, 2, 768)

    def half(which):
        return jnp.concatenate(
            [
                pick(in_halves, which, 2).reshape(6, 1152),
                small,
                pick(up_halves, which, 2).reshape(6, 1536),
            ],
            1,
        )

    mine = half(core)
    other = swap(half(1 - core))
    pack = jnp.concatenate([mine, other, output_weight], 1)
    pack = gather_ring(pack, "y").reshape(24, 6400)
    in_part = jnp.concatenate([pack[:, :1280], pack[:, 2816:4096], pack[:, 5632:]], 1)
    up_part = jnp.concatenate([pack[:, 1280:2816], pack[:, 4096:5632]], 1)
    in_all = gather_ring(gather_ring(in_part, "z"), "x")
    up_all = gather_ring(gather_ring(up_part, "x"), "z")
    down_all = gather_ring(gather_ring(gather_ring(reduce_weight, "z"), "x"), "y")

    in_all = in_all.reshape(4, 2, 2, 24, 3328)
    halves = by_core(core, in_all[..., :1280], in_all[..., 1280:2560], 0)
    in_rows = halves.transpose(3, 0, 1, 2, 4, 5).reshape(768, 1280)
    weight_in = in_rows[:, :1152]
    vectors = in_rows[:, 1152:1168].T
    weight_out = in_all[..., 2560:].transpose(2, 0, 1, 3, 4).reshape(384, 768)
    up_all = up_all.reshape(2, 2, 4, 24, 3072)
    halves = by_core(core, up_all[..., :1536], up_all[..., 1536:], 0)
    weight_up = halves.transpose(2, 0, 3, 1, 4, 5).reshape(768, 1536)
    weight_down = (
        down_all.reshape(4, 4, 2, 2, 24, 768).transpose(3, 1, 2, 0, 4, 5).reshape(1536, 768)
    )
    bias_up_all = in_rows[:, 1160:1164].reshape(2, 2, 768)
    bias_up = pick(bias_up_all, core, 1).reshape(1536)
    gain_one, shift_one = vectors[0], vectors[1]
    bias_query = pick(vectors[2].reshape(2, 2, 192), core, 1).reshape(384)
    bias_value = pick(vectors[3].reshape(2, 2, 192), core, 1).reshape(384)
    bias_out, gain_two, shift_two, bias_down = vectors[4], vectors[5], vectors[6], vectors[7]

    chunks = jnp.stack(halo + [ext], 0)
    chunks = jnp.concatenate([chunks, swap(chunks)], 0)
    seg_keys = chunks[:, 128, :128].reshape(1280).astype(jnp.int32)
    values = chunks[:, :128].reshape(1280, 768).astype(F32)
    normed_one, unit_one, scale_one = norm_forward(values, gain_one, shift_one)
    lowered_one = normed_one.astype(BF)
    starts = chip * 256 - jnp.arange(4, -1, -1, dtype=jnp.int32) * 256
    spots = jnp.concatenate([starts + core * 128, starts + (1 - core) * 128])
    pos_keys = (spots[:, None] + jnp.arange(128, dtype=jnp.int32)[None]).reshape(1280)

    def own(rows):
        return jnp.concatenate([rows[512:640], rows[1152:]], 0)

    weight_kv = weight_in[:, 384:]
    query = dot(own(lowered_one), weight_in[:, :384]) + bias_query.astype(F32)
    query = query.astype(BF).reshape(256, 6, HD)
    pair = dot(lowered_one, weight_kv) + jnp.concatenate(
        [jnp.zeros_like(bias_value), bias_value]
    ).astype(F32)
    pair = pair.astype(BF).reshape(1280, 2, 6, HD)
    keys, vals = pair[:, 0], pair[:, 1]
    allowed = (
        (own(seg_keys)[:, None] == seg_keys[None, :])
        & (pos_keys[None, :] <= own(pos_keys)[:, None])
        & (pos_keys[None, :] >= 0)
    )
    scores = jnp.einsum("qhd,khd->hqk", query, keys, preferred_element_type=F32) * 0.125
    scores = jnp.where(allowed[None], scores, -1e30)
    top = jnp.max(scores, -1, keepdims=True)
    expo = jnp.exp(scores - top)
    probs = expo / jnp.sum(expo, -1, keepdims=True)
    probs_low = probs.astype(BF)
    attended = jnp.einsum("hqk,khd->qhd", probs_low, vals, preferred_element_type=F32)
    attended = attended.astype(BF).reshape(256, 384)

    def share(part):
        return part[:128] + swap(part[128:])

    def both(rows):
        return jnp.concatenate([rows, swap(rows)], 0)

    own_values = values[512:640]
    branch = share(dot(attended, weight_out)) + bias_out.astype(F32)
    middle = own_values + branch
    normed_two, unit_two, scale_two = norm_forward(middle, gain_two, shift_two)
    lowered_two = both(normed_two.astype(BF))
    hidden = dot(lowered_two, weight_up) + bias_up.astype(F32)
    active = smooth_gate(hidden).astype(BF)
    layer_out = (middle + share(dot(active, weight_down)) + bias_down.astype(F32)).astype(BF)

    grad = both(cotangent)
    down_grad = outer_sum(active, grad)
    grad_active = back_project(grad, weight_down)
    grad_hidden = jax.vjp(smooth_gate, hidden)[1](grad_active)[0].astype(BF)
    up_grad = outer_sum(lowered_two, grad_hidden)
    up_bias_grad = jnp.sum(grad_hidden.astype(F32), 0)
    grad_two = share(back_project(grad_hidden, weight_up))
    gain_two_grad = jnp.sum(grad_two * unit_two, 0)
    shift_two_grad = jnp.sum(grad_two, 0)
    own_grad = cotangent.astype(F32)
    grad_middle = own_grad + norm_backward(grad_two, unit_two, scale_two, gain_two)
    own_branch = grad_middle.astype(BF)
    grad_branch = both(own_branch)
    out_grad = outer_sum(attended, grad_branch)
    grad_attended = back_project(grad_branch, weight_out).astype(BF).reshape(256, 6, HD)

    grad_probs = jnp.einsum("qhd,khd->hqk", grad_attended, vals, preferred_element_type=F32)
    inner = jnp.sum(probs * grad_probs, -1, keepdims=True)
    grad_scores = (probs * (grad_probs - inner)).astype(BF)
    grad_query = 0.125 * jnp.einsum(
        "hqk,khd->qhd", grad_scores, keys, preferred_element_type=F32
    )
    grad_keys = 0.125 * jnp.einsum(
        "hqk,qhd->khd", grad_scores, query, preferred_element_type=F32
    )
    grad_vals = jnp.einsum("hqk,qhd->khd", probs_low, grad_attended, preferred_element_type=F32)
    grad_query = grad_query.astype(BF).reshape(256, 384)
    grad_pair = jnp.concatenate(
        [grad_keys.reshape(1280, 384), grad_vals.reshape(1280, 384)], 1
    ).astype(BF)
    in_grad = jnp.concatenate(
        [outer_sum(own(lowered_one), grad_query), outer_sum(lowered_one, grad_pair)], 1
    )
    from_query = back_project(grad_query, weight_in[:, :384])
    from_pair = back_project(grad_pair, weight_kv)
    grad_one = jnp.concatenate(
        [
            from_pair[:512],
            from_pair[512:640] + from_query[:128],
            from_pair[640:1152],
            from_pair[1152:] + from_query[128:],
        ],
        0,
    )
    gain_one_grad = jnp.sum(grad_one * unit_one, 0)
    shift_one_grad = jnp.sum(grad_one, 0)
    low_one = grad_one.astype(BF)
    mine_one = (grad_one[:640] + swap(low_one[640:]).astype(F32)).reshape(5, 128, 768)
    total_one = mine_one[4]
    for i, d in enumerate((4, 3, 2, 1)):
        total_one = total_one + chip_shift(mine_one[i].astype(BF), -d).astype(F32)
    grad_input = grad_middle + norm_backward(
        total_one, unit_one[512:640], scale_one[512:640], gain_one
    )

    def widened(vector):
        rows = vector.reshape(2, vector.shape[0] // 2)
        zeros = jnp.zeros_like(rows)
        return by_core(core, rows, zeros, 1).reshape(-1)

    query_sum = jnp.sum(grad_query.astype(F32), 0)
    value_sum = jnp.sum(grad_pair[:, 384:].astype(F32), 0)
    columns = jnp.stack(
        [
            gain_one_grad,
            shift_one_grad,
            widened(query_sum),
            widened(value_sum),
            jnp.sum(own_branch.astype(F32), 0),
            gain_two_grad,
            shift_two_grad,
            jnp.sum(own_grad, 0),
        ],
        1,
    )
    columns = jnp.concatenate(
        [columns, widened(up_bias_grad).reshape(768, 4), jnp.zeros((768, 116), F32)], 1
    ).astype(BF)
    in_grad = jnp.concatenate([in_grad.astype(BF), columns], 1)

    def core_rows(rows, cols):
        rows = rows.reshape(2, 2, 4, 2, 24, cols)
        return pick(rows, core, 1), pick(rows, 1 - core, 1)

    in_send = jnp.concatenate(
        [*core_rows(in_grad, 1280), out_grad.astype(BF).reshape(2, 4, 2, 24, 768)], -1
    ).transpose(1, 2, 0, 3, 4)
    in_sum = scatter_ring(in_send.reshape(4, 4, 24, 3328), "x").astype(BF)
    in_sum = scatter_ring(in_sum, "z").astype(BF)
    up_send = jnp.concatenate(core_rows(up_grad.astype(BF), 1536), -1).transpose(2, 0, 1, 3, 4)
    up_sum = scatter_ring(up_send.reshape(4, 4, 24, 3072), "z").astype(BF)
    up_sum = scatter_ring(up_sum, "x").astype(BF)
    down_send = down_grad.astype(BF).reshape(2, 4, 2, 4, 24, 768).transpose(3, 1, 2, 0, 4, 5)
    down_sum = scatter_ring(down_send.reshape(4, 16, 24, 768), "y").astype(BF)
    down_sum = scatter_ring(down_sum.reshape(4, 4, 24, 768), "x").astype(BF)
    reduce_weight_grad = scatter_ring(down_sum, "z")
    pack = jnp.concatenate(
        [in_sum[:, :1280], up_sum[:, :1536], in_sum[:, 1280:2560], up_sum[:, 1536:], in_sum[:, 2560:]],
        1,
    )
    pack = scatter_ring(pack.reshape(4, 6, 6400), "y")
    mine = pack[:, :2816]
    other = swap(pack[:, 2816:5632].astype(BF)).astype(F32)
    sums = mine[:, 1152:1280] + other[:, 1152:1280]
    input_weight_grad = by_core(
        core, mine[:, :1152].reshape(6, 6, 192), other[:, :1152].reshape(6, 6, 192), 2
    ).reshape(6, 2304)
    expand_weight_grad = by_core(
        core, mine[:, 1280:].reshape(6, 2, 768), other[:, 1280:].reshape(6, 2, 768), 2
    ).reshape(6, 3072)
    output_weight_grad = pack[:, 5632:]
    return (
        layer_out,
        grad_input,
        sums[:, 0],
        sums[:, 1],
        input_weight_grad,
        sums[:, 2],
        sums[:, 3],
        output_weight_grad,
        sums[:, 4],
        sums[:, 5],
        sums[:, 6],
        expand_weight_grad,
        sums[:, 8:12].reshape(24),
        reduce_weight_grad,
        sums[:, 7],
    )


def solution(mesh):
    fine = Mesh(mesh.devices.reshape(2, 2, 4, 2, 4), ("zl", "c", "x", "zh", "y"))
    token = P(("x", "zh", "y", "zl", "c"))
    param = P(("zl", "c", "x", "zh", "y"))
    return jax.shard_map(
        local,
        mesh=fine,
        in_specs=(token, token, P(("x", "zh", "y"))) + (param,) * 13,
        out_specs=(token, token) + (param,) * 13,
        check_vma=False,
    )
```

```python
import jax
import jax.numpy as jnp
from jax import lax
from jax.experimental import pallas as pl
from jax.experimental.pallas import tpu as pltpu
from jax.sharding import Mesh
from jax.sharding import PartitionSpec as P

CHIPS = ("zl", "x", "zh", "y")
BF = jnp.bfloat16
F32 = jnp.float32
I32 = jnp.int32
SMEM = pl.BlockSpec(memory_space=pltpu.SMEM)
VMEM = pl.BlockSpec(memory_space=pltpu.VMEM)
ANY = pl.BlockSpec(memory_space=pl.ANY)


def chip_shift(value, distance):
    def at(place):
        place = place % 64
        zl, rest = place % 2, place // 2
        y, rest = rest % 4, rest // 4
        zh, x = rest % 2, rest // 2
        return ((zl * 4 + x) * 2 + zh) * 4 + y

    return lax.ppermute(value, CHIPS, [(at(t), at(t + distance)) for t in range(64)])


def swap(value):
    return lax.ppermute(value, "c", [(0, 1), (1, 0)])


def ring_shift(value, axis, distance):
    if axis == "z":
        place = [0, 2, 1, 3]
        return lax.ppermute(
            value, ("zl", "zh"), [(place[i], place[(i + distance) % 4]) for i in range(4)]
        )
    return lax.ppermute(value, axis, [(i, (i + distance) % 4) for i in range(4)])


def trade(value, axis, step):
    def at(core, place):
        if axis == "z":
            return ((place % 2) * 2 + core) * 2 + place // 2
        return core * 4 + place

    pairs = []
    for core in range(2):
        flip = 1 if core == step else 3
        pairs += [(at(core, m), at(core, m ^ flip)) for m in range(4)]
    return lax.ppermute(value, ("zl", "c", "zh") if axis == "z" else ("c", axis), pairs)


def around(value, axis):
    pair = jnp.stack([value, trade(value, axis, 0)])
    return pair, trade(pair, axis, 1)


def around_once(value, axis):
    after = ring_shift(value, axis, 1), ring_shift(value, axis, 3), ring_shift(value, axis, 2)
    return (value, after[0], after[2], after[1])


def spread_once(blocks, axis):
    got = (
        ring_shift(blocks[1], axis, 1),
        ring_shift(blocks[3], axis, 3),
        ring_shift(blocks[2], axis, 2),
    )
    return (blocks[0], got[0], got[2], got[1])


def shape(dims, kind):
    return jax.ShapeDtypeStruct(dims, kind)


def run(body, outs, specs, args, scratch=(), out_specs=None, us=1.0, vmem=24):
    return pl.pallas_call(
        body,
        out_shape=tuple(outs),
        in_specs=list(specs),
        out_specs=tuple(out_specs or [VMEM] * len(outs)),
        scratch_shapes=list(scratch),
        name=body.__name__,
        cost_estimate=pl.CostEstimate(
            flops=int(us * 600e6), bytes_accessed=int(us * 1.5e6), transcendentals=0
        ),
        compiler_params=pltpu.CompilerParams(vmem_limit_bytes=vmem << 20),
    )(*args)


def dot(left, right):
    return jnp.dot(left, right, preferred_element_type=F32)


def dot_t(left, right):
    return lax.dot_general(left, right, (((1,), (1,)), ((), ())), preferred_element_type=F32)


def outer(left, right):
    return lax.dot_general(left, right, (((0,), (0,)), ((), ())), preferred_element_type=F32)


def places(s_ref):
    return s_ref[0], s_ref[1], s_ref[2], s_ref[3], s_ref[4]


def wrap(value):
    return lax.rem(value + 4, 4)


def seat(place, core, j):
    return place ^ (0, 1 + 2 * core, 3 - 2 * core, 2)[j]


def unit_table(transposed):
    dims = (1536, 384) if transposed else (384, 1536)
    unit = lax.broadcasted_iota(I32, dims, 0 if transposed else 1)
    group = (unit * 2731) >> 16
    rest = unit - group * 24
    spot = group * 6 + rest - 6 * ((rest * 43) >> 8)
    return jnp.where(
        spot == lax.broadcasted_iota(I32, dims, 1 if transposed else 0), 1.0, 0.0
    ).astype(BF)


def unit_quarter():
    unit = lax.broadcasted_iota(I32, (8, 1536), 1)
    rest = unit - 24 * ((unit * 2731) >> 16)
    return ((rest * 43) >> 8) == lax.broadcasted_iota(I32, (8, 1536), 0)


def flat(blocks):
    count, _, columns = blocks.shape
    return blocks.astype(F32).reshape(count * 24, columns).astype(BF)


def cut(rows):
    return rows.reshape(rows.shape[0] // 24, 24, rows.shape[1]).astype(BF)


def move_all(copies, sems):
    moves = [pltpu.make_async_copy(a, b, sems.at[i]) for i, (a, b) in enumerate(copies)]
    for move in moves:
        move.start()
    return moves


def unit_of(values):
    centered = values - jnp.mean(values, -1, keepdims=True)
    scale = lax.rsqrt(jnp.mean(centered * centered, -1, keepdims=True) + 1e-05)
    return centered * scale, scale


def norm_backward(grad_out, unit, scale, gain):
    scaled = grad_out * gain
    return scale * (
        scaled
        - jnp.mean(scaled, -1, keepdims=True)
        - unit * jnp.mean(scaled * unit, -1, keepdims=True)
    )


def halves_kernel(s_ref, in_ref, up_ref, small_ref, mine_ref, send_ref):
    core = s_ref[0]
    small = small_ref[...].T[0:6, :]

    def half(which):
        parts = [in_ref[:, j * 384 + which * 192 : j * 384 + which * 192 + 192] for j in range(6)]
        parts.append(small)
        parts += [up_ref[:, j * 1536 + which * 768 : j * 1536 + which * 768 + 768] for j in range(2)]
        return jnp.concatenate([p.astype(F32) for p in parts], 1)

    first, second = half(0), half(1)
    mine_ref[0:6, :] = jnp.where(core == 0, first, second).astype(BF)
    send_ref[0:6, :] = jnp.where(core == 0, second, first).astype(BF)
    mine_ref[6:8, :] = jnp.zeros((2, 2816), BF)
    send_ref[6:8, :] = jnp.zeros((2, 2816), BF)


def pack_kernel(mine_ref, other_ref, out_ref, pack_ref):
    pack_ref[:, 0:2816] = mine_ref[...]
    pack_ref[:, 2816:5632] = other_ref[...]
    pack_ref[0:6, 5632:] = out_ref[...]
    pack_ref[6:8, 5632:] = jnp.zeros((2, 768), BF)


def rows_kernel(s_ref, p0, p1, p2, p3, down_ref, a_ref, b_ref, up_ref):
    y = s_ref[3]
    pieces = [p[...].astype(F32) for p in (p0, p1, p2, p3)]
    parts = []
    for place in range(4):
        d = wrap(y - place)
        block = pieces[0]
        for k in (1, 2, 3):
            block = jnp.where(d == k, pieces[k], block)
        parts.append(block[0:6])
    rows = jnp.concatenate(parts, 0).astype(BF)
    a_ref[:, 0:1280] = rows[:, 0:1280]
    a_ref[:, 1280:] = rows[:, 5632:6016]
    b_ref[:, 0:1280] = rows[:, 2816:4096]
    b_ref[:, 1280:] = rows[:, 6016:]
    up_ref[:, 0:1536] = rows[:, 1280:2816]
    up_ref[:, 1536:3072] = rows[:, 4096:5632]
    up_ref[:, 3072:] = down_ref[...]


def half_row(row, core):
    first = jnp.concatenate([row[:, 0:192], row[:, 384:576]], 1)
    second = jnp.concatenate([row[:, 192:384], row[:, 576:768]], 1)
    return jnp.where(core == 0, first, second)


def attend_kernel(
    s_ref, m0, m1, m2, m3, m4, o_ref, w0, w1, w2, w3,
    low_ref, win_ref, wout_ref, vec_ref, q_ref, kv_ref, att_ref, lse_ref, mask_ref, pm_ref, po_ref, up_ref,
    win, wout, sems,
):
    core, x, z, _, chip = places(s_ref)
    mine = (m0, m1, m2, m3, m4)
    copies = []
    for j in range(4):
        for i in range(4):
            for k, c in enumerate((core, 1 - core)):
                outer_, inner_ = ((x, z), (z, x))[k]
                outer_, inner_ = seat(outer_, core, j), seat(inner_, core, i)
                xs, zs = ((outer_, inner_), (inner_, outer_))[k]
                base = xs * 2 + (zs >> 1)
                zl = zs & 1
                piece = ((w0, w1), (w2, w3))[k][j // 2]
                copies.append(
                    (piece.at[j % 2, i, :, pl.ds(0, 1280)], win.at[zl * 16 + c * 8 + base])
                )
                copies.append(
                    (
                        piece.at[j % 2, i, :, pl.ds(1280, 384)],
                        wout.at[zl * 8 + base, :, pl.ds(k * 384, 384)],
                    )
                )
    moves = move_all(copies, sems)
    seg_rows = []
    for i in range(5):
        seg_rows.append(mine[i][128:136, 0:128].astype(F32)[0:1])
        seg_rows.append(o_ref[i, 128:136, 0:128].astype(F32)[0:1])
    seg_query = jnp.concatenate(seg_rows[8:], 1)
    seg_cols = jnp.concatenate(seg_rows + [jnp.zeros((118, 128), F32)], 0).T
    lane = lax.broadcasted_iota(I32, (1, 256), 1)
    start = chip * 256
    pos_query = jnp.where(lane < 128, start + core * 128 + lane, start + (1 - core) * 128 + lane - 128)
    for b in range(10):
        i, k = b // 2, b % 2
        first = start - (4 - i) * 256 + (core if k == 0 else 1 - core) * 128
        pos = first + lax.broadcasted_iota(I32, (128, 256), 0)
        allowed = (seg_cols[:, b : b + 1] == seg_query) & (pos <= pos_query) & (pos >= 0)
        mask_ref[b * 128 : (b + 1) * 128, :] = jnp.where(allowed, 0.0, -1e30).astype(BF)
    for move in moves:
        move.wait()
    win_ref[...] = flat(win[...])
    wout_ref[...] = flat(wout[...])
    vec_ref[...] = win_ref[:, 1152:1280].astype(F32).T[0:16]
    gain, shift = vec_ref[0:1, :], vec_ref[1:2, :]
    bias_q = half_row(vec_ref[2:3, :], core)
    bias_v = half_row(vec_ref[3:4, :], core)
    bias_kv = jnp.concatenate([jnp.zeros((1, 384), F32), bias_v], 1)
    for i in range(5):
        values = jnp.concatenate([mine[i][0:128, :], o_ref[i, 0:128, :]], 0).astype(F32)
        unit, _ = unit_of(values)
        low = (unit * gain + shift).astype(BF)
        low_ref[i * 256 : (i + 1) * 256, :] = low
        kv_ref[i * 256 : (i + 1) * 256, :] = (dot(low, win_ref[:, 384:1152]) + bias_kv).astype(BF)
        if i == 4:
            q_ref[...] = (dot(low, win_ref[:, 0:384]) + bias_q).astype(BF)
    head_lane = lax.broadcasted_iota(I32, (1, 128), 1)
    for p in range(3):
        keys = kv_ref[:, p * 128 : (p + 1) * 128]
        vals_t = kv_ref[:, 384 + p * 128 : 512 + p * 128].T
        query = q_ref[:, p * 128 : (p + 1) * 128]
        parts = []
        for h in range(2):
            picked = jnp.where((head_lane < 64) == (h == 0), query, jnp.zeros_like(query))
            scores = dot_t(keys, picked) * 0.125 + mask_ref[...].astype(F32)
            top = jnp.max(scores, 0, keepdims=True)
            expo = jnp.exp(scores - top)
            total = jnp.sum(expo, 0, keepdims=True)
            probs = (expo * (1.0 / total)).astype(BF)
            lse_ref[2 * p + h : 2 * p + h + 1, :] = top + jnp.log(total)
            parts.append(dot(vals_t[h * 64 : (h + 1) * 64], probs))
        att_ref[:, p * 128 : (p + 1) * 128] = jnp.concatenate(parts, 0).T.astype(BF)
    part = dot(att_ref[...], wout_ref[...])
    pm_ref[...] = part[0:128]
    po_ref[...] = part[128:256]
    quarters = jnp.concatenate(
        [half_row(vec_ref[8 + k : 9 + k, :], core) for k in range(4)] + [jnp.zeros((4, 384), F32)], 0
    )
    biases = dot(quarters.astype(BF), unit_table(False))
    up_ref[...] = jnp.sum(jnp.where(unit_quarter(), biases, 0.0), 0, keepdims=True)


def attend(s, mine, other, pieces):
    return run(
        attend_kernel,
        [
            shape((1280, 768), BF),
            shape((768, 1280), BF),
            shape((384, 768), BF),
            shape((16, 768), F32),
            shape((256, 384), BF),
            shape((1280, 768), BF),
            shape((256, 384), BF),
            shape((8, 256), F32),
            shape((1280, 256), BF),
            shape((128, 768), F32),
            shape((128, 768), F32),
            shape((1, 1536), F32),
        ],
        [SMEM] + [VMEM] * 6 + [ANY] * 4,
        [s, *mine, other, *pieces],
        [
            pltpu.VMEM((32, 24, 1280), BF),
            pltpu.VMEM((16, 24, 768), BF),
            pltpu.SemaphoreType.DMA((64,)),
        ],
        us=40.0,
        vmem=24,
    )


def attend_back_kernel(
    s_ref, gm_ref, go_ref, att_ref, win_ref, wout_ref, low_ref, q_ref, kv_ref, lse_ref, mask_ref,
    m0, m1, m2, m3, m4, o_ref, sums_ref, ups_ref,
    s0, s1, s2, s3, dm_ref, do_ref,
    dwin, dwout, dq, dkv, sems,
):
    core, x, z, _, _ = places(s_ref)
    mine = (m0, m1, m2, m3, m4)
    grad = jnp.concatenate([gm_ref[...], go_ref[...]], 0)
    dwout[...] = cut(outer(att_ref[...], grad))
    back = dot_t(grad, wout_ref[...]).astype(BF)
    head_lane = lax.broadcasted_iota(I32, (1, 128), 1)
    for p in range(3):
        keys = kv_ref[:, p * 128 : (p + 1) * 128]
        vals = kv_ref[:, 384 + p * 128 : 512 + p * 128]
        keys_t = keys.T
        query = q_ref[:, p * 128 : (p + 1) * 128]
        grad_p = back[:, p * 128 : (p + 1) * 128]
        parts = []
        dk = jnp.zeros((1280, 128), F32)
        dv = jnp.zeros((1280, 128), F32)
        for h in range(2):
            here = (head_lane < 64) == (h == 0)
            picked = jnp.where(here, query, jnp.zeros_like(query))
            grad_h = jnp.where(here, grad_p, jnp.zeros_like(grad_p))
            scores = dot_t(keys, picked) * 0.125 + mask_ref[...].astype(F32)
            probs = jnp.exp(scores - lse_ref[2 * p + h : 2 * p + h + 1, :])
            dp = dot_t(vals, grad_h)
            inner = jnp.sum(probs * dp, 0, keepdims=True)
            ds = (probs * (dp - inner)).astype(BF)
            dv = dv + dot(probs.astype(BF), grad_h)
            dk = dk + dot(ds, picked)
            parts.append(dot(keys_t[h * 64 : (h + 1) * 64], ds))
        dq[:, p * 128 : (p + 1) * 128] = (jnp.concatenate(parts, 0).T * 0.125).astype(BF)
        dkv[:, p * 128 : (p + 1) * 128] = (dk * 0.125).astype(BF)
        dkv[:, 384 + p * 128 : 512 + p * 128] = dv.astype(BF)
    dwin[:, :, 0:384] = cut(outer(low_ref[1024:1280, :], dq[...]))
    dwin[:, :, 384:1152] = cut(outer(low_ref[...], dkv[...]))
    gain_sum = jnp.zeros((1, 768), F32)
    shift_sum = jnp.zeros((1, 768), F32)
    value_sum = jnp.zeros((1, 384), F32)
    for i in range(5):
        rows = slice(i * 256, (i + 1) * 256)
        da = dot_t(dkv[rows, :], win_ref[:, 384:1152])
        if i == 4:
            da = da + dot_t(dq[...], win_ref[:, 0:384])
        values = jnp.concatenate([mine[i][0:128, :], o_ref[i, 0:128, :]], 0).astype(F32)
        unit, _ = unit_of(values)
        gain_sum = gain_sum + jnp.sum(da * unit, 0, keepdims=True)
        shift_sum = shift_sum + jnp.sum(da, 0, keepdims=True)
        value_sum = value_sum + jnp.sum(dkv[rows, 384:768].astype(F32), 0, keepdims=True)
        dm_ref[i] = da[0:128]
        do_ref[i] = da[128:256].astype(BF)
    query_sum = jnp.sum(dq[...].astype(F32), 0, keepdims=True)

    def widened(row):
        zero = jnp.zeros((1, 192), F32)
        a, b = row[:, 0:192], row[:, 192:384]
        return jnp.where(
            core == 0,
            jnp.concatenate([a, zero, b, zero], 1),
            jnp.concatenate([zero, a, zero, b], 1),
        )

    quarters = dot(jnp.where(unit_quarter(), ups_ref[...], 0.0).astype(BF), unit_table(True))
    table = jnp.concatenate(
        [
            gain_sum,
            shift_sum,
            widened(query_sum),
            widened(value_sum),
            sums_ref[0:4, :],
            *[widened(quarters[k : k + 1, :]) for k in range(4)],
            jnp.zeros((116, 768), F32),
        ],
        0,
    )
    dwin[:, :, 1152:1280] = cut(table.T)
    copies = []
    for j in range(4):
        for i in range(4):
            for k, c in enumerate((core, 1 - core)):
                first = seat((x, z)[k], core, j)
                xs, zs = ((first, i), (i, first))[k]
                base = xs * 2 + (zs >> 1)
                zl = zs & 1
                piece = ((s0, s1), (s2, s3))[k][j // 2]
                copies.append(
                    (dwin.at[zl * 16 + c * 8 + base], piece.at[j % 2, i, :, pl.ds(0, 1280)])
                )
                copies.append(
                    (
                        dwout.at[zl * 8 + base, :, pl.ds(k * 384, 384)],
                        piece.at[j % 2, i, :, pl.ds(1280, 384)],
                    )
                )
    for move in move_all(copies, sems):
        move.wait()


def attend_back(args):
    return run(
        attend_back_kernel,
        [shape((2, 4, 24, 1664), BF)] * 4 + [shape((5, 128, 768), F32), shape((5, 128, 768), BF)],
        [SMEM] + [VMEM] * 18,
        args,
        [
            pltpu.VMEM((32, 24, 1280), BF),
            pltpu.VMEM((16, 24, 768), BF),
            pltpu.VMEM((256, 384), BF),
            pltpu.VMEM((1280, 768), BF),
            pltpu.SemaphoreType.DMA((64,)),
        ],
        [ANY] * 4 + [VMEM] * 2,
        us=40.0,
        vmem=28,
    )


def middle_kernel(x_ref, a_ref, b_ref, vec_ref, mid_ref, low_ref):
    middle = x_ref[...].astype(F32) + (a_ref[...] + b_ref[...]) + vec_ref[4:5, :]
    unit, _ = unit_of(middle)
    mid_ref[...] = middle
    low_ref[...] = (unit * vec_ref[5:6, :] + vec_ref[6:7, :]).astype(BF)


def forward_kernel(
    s_ref, am_ref, ao_ref, gm_ref, go_ref, bias_ref, e0, e1, r0, r1,
    om_ref, oo_ref, dm_ref, do_ref, ups_ref, p0, p1, t0, t1,
    wup3, wdown3, wup, wdown, dup, ddown, sems,
):
    core, x, z, y, _ = places(s_ref)
    copies = []
    for j in range(4):
        zs = seat(z, core, j)
        for i in range(4):
            base = (zs & 1) * 16 + seat(x, core, i) * 2 + (zs >> 1)
            for k, c in enumerate((core, 1 - core)):
                copies.append(
                    (
                        (e0, e1)[j // 2].at[j % 2, i, :, pl.ds(k * 1536, 1536)],
                        wup3.at[base + c * 8],
                    )
                )
    for j in range(4):
        for iz in range(4):
            zs = seat(z, core, iz)
            for ix in range(4):
                base = (zs & 1) * 32 + (zs >> 1) * 4 + seat(x, core, ix) * 8 + seat(y, core, j)
                copies.append(((r0, r1)[j // 2].at[j % 2, iz, ix], wdown3.at[base]))
    for move in move_all(copies, sems):
        move.wait()
    low = jnp.concatenate([am_ref[...], ao_ref[...]], 0)
    grad = jnp.concatenate([gm_ref[...], go_ref[...]], 0)
    low_t = low.T
    out = jnp.zeros((256, 768), F32)
    da = jnp.zeros((256, 768), F32)
    for b in range(2):
        cols = slice(b * 768, (b + 1) * 768)
        blocks = slice(b * 32, (b + 1) * 32)
        wup[:, cols] = flat(wup3[:, :, cols])
        wdown[cols, :] = flat(wdown3[blocks])
        hidden = dot(low, wup[:, cols]) + bias_ref[:, cols]
        square = hidden * hidden
        bent = jnp.tanh(0.7978845608 * hidden * (1.0 + 0.044715 * square))
        rest = 0.5 * (1.0 + bent)
        active = (hidden * rest).astype(BF)
        slope = rest + 0.5 * hidden * (1.0 - bent * bent) * (
            0.7978845608 * (1.0 + 3.0 * 0.044715 * square)
        )
        back = (dot_t(grad, wdown[cols, :]) * slope).astype(BF)
        out = out + dot(active, wdown[cols, :])
        da = da + dot_t(back, wup[:, cols])
        ddown[blocks] = cut(outer(active, grad))
        dup[:, :, cols] = cut(dot(low_t, back))
        ups_ref[:, cols] = jnp.sum(back.astype(F32), 0, keepdims=True)
    om_ref[...] = out[0:128]
    oo_ref[...] = out[128:256]
    dm_ref[...] = da[0:128]
    do_ref[...] = da[128:256]
    copies = []
    for j in range(4):
        zs = seat(z, core, j)
        for i in range(4):
            base = (zs & 1) * 16 + i * 2 + (zs >> 1)
            for k, c in enumerate((core, 1 - core)):
                copies.append(
                    (
                        dup.at[base + c * 8],
                        (p0, p1)[j // 2].at[j % 2, i, :, pl.ds(k * 1536, 1536)],
                    )
                )
    for j in range(4):
        ys = seat(y, core, j)
        for iz in range(4):
            for ix in range(4):
                base = (iz % 2) * 32 + ix * 8 + (iz // 2) * 4 + ys
                copies.append((ddown.at[base], (t0, t1)[j // 2].at[j % 2, ix, iz]))
    for move in move_all(copies, sems):
        move.wait()


def forward(args):
    return run(
        forward_kernel,
        [shape((128, 768), F32)] * 4
        + [shape((1, 1536), F32)]
        + [shape((2, 4, 24, 3072), BF)] * 2
        + [shape((2, 4, 4, 24, 768), BF)] * 2,
        [SMEM] + [VMEM] * 5 + [ANY] * 4,
        args,
        [
            pltpu.VMEM((32, 24, 1536), BF),
            pltpu.VMEM((64, 24, 768), BF),
            pltpu.VMEM((768, 1536), BF),
            pltpu.VMEM((1536, 768), BF),
            pltpu.VMEM((32, 24, 1536), BF),
            pltpu.VMEM((64, 24, 768), BF),
            pltpu.SemaphoreType.DMA((96,)),
        ],
        [VMEM] * 5 + [ANY] * 4,
        us=30.0,
        vmem=24,
    )


def middle_back_kernel(
    mid_ref, om_ref, ox_ref, dm_ref, dx_ref, g_ref, vec_ref, out_ref, gmid_ref, low_ref, sums_ref
):
    middle = mid_ref[...]
    out_ref[...] = (middle + (om_ref[...] + ox_ref[...]) + vec_ref[7:8, :]).astype(BF)
    unit, scale = unit_of(middle)
    da = dm_ref[...] + dx_ref[...]
    grad = g_ref[...].astype(F32)
    total = grad + norm_backward(da, unit, scale, vec_ref[5:6, :])
    low = total.astype(BF)
    gmid_ref[...] = total
    low_ref[...] = low
    sums_ref[0:1, :] = jnp.sum(low.astype(F32), 0, keepdims=True)
    sums_ref[1:2, :] = jnp.sum(da * unit, 0, keepdims=True)
    sums_ref[2:3, :] = jnp.sum(da, 0, keepdims=True)
    sums_ref[3:4, :] = jnp.sum(grad, 0, keepdims=True)
    sums_ref[4:8, :] = jnp.zeros((4, 768), F32)


def added(refs, index=None):
    total = None
    for ref in refs:
        value = (ref[...] if index is None else ref[index]).astype(F32)
        total = value if total is None else total + value
    return total


def total_of(keep, got, *index):
    if not index:
        return keep[...].astype(F32) + got[...].astype(F32)
    return keep[index].astype(F32) + got[index].astype(F32)


def pair_kernel(keep, got, mine, send):
    mine[...] = total_of(keep, got, 0).astype(BF)
    send[...] = total_of(keep, got, 1).astype(BF)


def two_pairs_kernel(ka, ga, kb, gb, ma, sa, mb, sb):
    pair_kernel(ka, ga, ma, sa)
    pair_kernel(kb, gb, mb, sb)


def up_down_kernel(s_ref, ka, ga, kb, gb, mine, send):
    core, x = s_ref[0], s_ref[1]
    for j in range(4):
        xs = seat(x, core, j)
        out = (mine, send)[j // 2]
        out[j % 2, :, 0:3072] = total_of(ka, ga, xs).astype(BF)
        for zs in range(4):
            out[j % 2, :, 3072 + zs * 768 : 3840 + zs * 768] = total_of(kb, gb, xs, zs).astype(BF)


def up_down_again_kernel(s_ref, keep, got, up_ref, o0, o1, o2, o3):
    z = s_ref[2]
    total = total_of(keep, got)
    up_ref[...] = total[:, 0:3072].astype(BF)
    parts = [total[:, 3072 + i * 768 : 3840 + i * 768] for i in range(4)]
    for k, out in enumerate((o0, o1, o2, o3)):
        zs = wrap(z + k)
        block = parts[0]
        for i in (1, 2, 3):
            block = jnp.where(zs == i, parts[i], block)
        out[...] = block.astype(BF)


def down_kernel(a0, a1, a2, a3, out_ref):
    out_ref[...] = added((a0, a1, a2, a3))


def in_kernel(s_ref, ka, ga, kb, gb, ma, sa, mb, sb):
    core, x, z, _, _ = places(s_ref)
    for j in range(4):
        (ma, sa)[j // 2][j % 2] = total_of(ka, ga, seat(z, core, j)).astype(BF)
        (mb, sb)[j // 2][j % 2] = total_of(kb, gb, seat(x, core, j)).astype(BF)


def in_again_kernel(s_ref, ka, ga, kb, gb, up_ref, o0, o1, o2, o3):
    y = s_ref[3]
    a, b = total_of(ka, ga), total_of(kb, gb)
    up = up_ref[...].astype(F32)
    rows = jnp.concatenate(
        [a[:, 0:1280], up[:, 0:1536], b[:, 0:1280], up[:, 1536:], a[:, 1280:], b[:, 1280:]], 1
    )
    parts = [rows[i * 6 : i * 6 + 6] for i in range(4)]
    for k, out in enumerate((o0, o1, o2, o3)):
        ys = wrap(y + k)
        block = parts[0]
        for i in (1, 2, 3):
            block = jnp.where(ys == i, parts[i], block)
        out[0:6, :] = block.astype(BF)
        out[6:8, :] = jnp.zeros((2, 6400), BF)


def last_kernel(a0, a1, a2, a3, keep_ref, send_ref):
    total = added((a0, a1, a2, a3))
    keep_ref[:, 0:2816] = total[:, 0:2816]
    keep_ref[:, 2816:] = total[:, 5632:]
    send_ref[...] = total[:, 2816:5632].astype(BF)


def owned_kernel(s_ref, keep_ref, got_ref, in_ref, up_ref, out_ref, sums_ref):
    core = s_ref[0]
    mine = keep_ref[:, 0:2816]
    other = got_ref[...].astype(F32)
    first = jnp.where(core == 0, mine, other)
    second = jnp.where(core == 0, other, mine)
    for j in range(6):
        part = slice(j * 192, j * 192 + 192)
        in_ref[:, j * 384 : j * 384 + 192] = first[0:6, part]
        in_ref[:, j * 384 + 192 : j * 384 + 384] = second[0:6, part]
    for j in range(2):
        part = slice(1280 + j * 768, 2048 + j * 768)
        up_ref[:, j * 1536 : j * 1536 + 768] = first[0:6, part]
        up_ref[:, j * 1536 + 768 : j * 1536 + 1536] = second[0:6, part]
    out_ref[...] = keep_ref[0:6, 2816:]
    sums_ref[...] = (mine[:, 1152:1280] + other[:, 1152:1280]).T[0:16, :]


def halo_kernel(dm_ref, dx_ref, own_ref, h0, h1, h2, h3):
    for i, out in enumerate((h0, h1, h2, h3)):
        out[...] = (dm_ref[i] + dx_ref[i].astype(F32)).astype(BF)
    own_ref[...] = dm_ref[4] + dx_ref[4].astype(F32)


def input_kernel(own_ref, h0, h1, h2, h3, x_ref, gmid_ref, vec_ref, out_ref):
    total = own_ref[...] + added((h0, h1, h2, h3))
    unit, scale = unit_of(x_ref[...].astype(F32))
    out_ref[...] = gmid_ref[...] + norm_backward(total, unit, scale, vec_ref[0:1, :])


def local(
    tokens,
    cotangent,
    segments,
    first_gain,
    first_shift,
    input_weight,
    query_bias,
    value_bias,
    output_weight,
    output_bias,
    second_gain,
    second_shift,
    expand_weight,
    expand_bias,
    reduce_weight,
    reduce_bias,
):
    core = lax.axis_index("c")
    zl, zh = lax.axis_index("zl"), lax.axis_index("zh")
    x, y = lax.axis_index("x"), lax.axis_index("y")
    chip = ((x * 2 + zh) * 4 + y) * 2 + zl
    s = jnp.stack([core, x, zh * 2 + zl, y, chip]).astype(I32)
    vectors = [
        first_gain,
        first_shift,
        query_bias,
        value_bias,
        output_bias,
        second_gain,
        second_shift,
        reduce_bias,
        *[expand_bias[k * 6 : k * 6 + 6] for k in range(4)],
    ]
    small = jnp.concatenate(
        [part for v in vectors for part in (v.astype(F32), jnp.zeros((122,), F32))]
        + [jnp.zeros((116 * 128,), F32)]
    ).reshape(128, 128)
    mine, send = run(
        halves_kernel,
        [shape((8, 2816), BF)] * 2,
        [SMEM] + [VMEM] * 3,
        [s, input_weight, expand_weight, small],
    )
    other = swap(send)
    (pack,) = run(
        pack_kernel, [shape((8, 6400), BF)], [VMEM] * 3, [mine, other, output_weight], us=0.7
    )
    part_a, part_b, up_part = run(
        rows_kernel,
        [shape((24, 1664), BF), shape((24, 1664), BF), shape((24, 3840), BF)],
        [SMEM] + [VMEM] * 5,
        [s, *around_once(pack, "y"), reduce_weight],
        us=1.5,
    )
    in_a = around(jnp.concatenate(around(part_a, "z"), 0), "x")
    in_b = around(jnp.concatenate(around(part_b, "x"), 0), "z")
    seg_own = lax.dynamic_slice_in_dim(segments, (zl * 2 + core) * 128, 128).astype(BF)
    ext = jnp.concatenate([tokens, jnp.pad(seg_own[None], ((0, 7), (0, 640)))], 0)
    chunks = [chip_shift(ext, d) for d in (4, 3, 2, 1)] + [ext]
    chunks_other = swap(jnp.stack(chunks))
    grad_other = swap(cotangent)
    up_x = jnp.concatenate(around(up_part, "x"), 0)
    up_pieces = around(up_x[:, :, :3072], "z")
    down_pieces = around(jnp.concatenate(around(up_x[:, :, 3072:], "z"), 0), "y")

    low, win, wout, vec, query, pair, att, lse, mask, part_m, part_o, bias_up = attend(
        s, chunks, chunks_other, in_a + in_b
    )
    middle, low_two = run(
        middle_kernel,
        [shape((128, 768), F32), shape((128, 768), BF)],
        [VMEM] * 4,
        [tokens, part_m, swap(part_o), vec],
    )
    (out_m, out_o, da_m, da_o, ups, up_keep, up_send, down_keep, down_send) = forward(
        [s, low_two, swap(low_two), cotangent, grad_other, bias_up, *up_pieces, *down_pieces]
    )
    layer_out, grad_middle, grad_branch, sums = run(
        middle_back_kernel,
        [shape((128, 768), BF), shape((128, 768), F32), shape((128, 768), BF), shape((8, 768), F32)],
        [VMEM] * 7,
        [middle, out_m, swap(out_o), da_m, swap(da_o), cotangent, vec],
        us=2.0,
    )
    up_got = trade(up_send, "z", 1)
    down_got = trade(down_send, "y", 1)
    (a_keep, a_send, b_keep, b_send, da_mine, da_other) = attend_back(
        [
            s, grad_branch, swap(grad_branch), att, win, wout, low, query, pair, lse, mask,
            *chunks, chunks_other, sums, ups,
        ]
    )
    a_got, b_got = trade(a_send, "x", 1), trade(b_send, "z", 1)
    own, *halo = run(
        halo_kernel,
        [shape((128, 768), F32)] + [shape((128, 768), BF)] * 4,
        [VMEM] * 2,
        [da_mine, swap(da_other)],
    )
    halo = [chip_shift(h, -d) for h, d in zip(halo, (4, 3, 2, 1))]
    up_keep, up_send, down_keep, down_send = run(
        two_pairs_kernel,
        [shape((4, 24, 3072), BF)] * 2 + [shape((4, 4, 24, 768), BF)] * 2,
        [VMEM] * 4,
        [up_keep, up_got, down_keep, down_got],
        us=2.0,
    )
    mixed_keep, mixed_send = run(
        up_down_kernel,
        [shape((2, 24, 6144), BF)] * 2,
        [SMEM] + [VMEM] * 4,
        [s, up_keep, trade(up_send, "z", 0), down_keep, trade(down_send, "y", 0)],
        us=1.5,
    )
    mixed_keep, mixed_send = run(
        pair_kernel,
        [shape((24, 6144), BF)] * 2,
        [VMEM] * 2,
        [mixed_keep, trade(mixed_send, "x", 1)],
    )
    up_sum, *down_sends = run(
        up_down_again_kernel,
        [shape((24, 3072), BF)] + [shape((24, 768), BF)] * 4,
        [SMEM] + [VMEM] * 2,
        [s, mixed_keep, trade(mixed_send, "x", 0)],
    )
    (reduce_weight_grad,) = run(
        down_kernel, [shape((24, 768), F32)], [VMEM] * 4, spread_once(down_sends, "z"), us=0.7
    )
    a_keep, a_send, b_keep, b_send = run(
        two_pairs_kernel,
        [shape((4, 24, 1664), BF)] * 4,
        [VMEM] * 4,
        [a_keep, a_got, b_keep, b_got],
        us=1.5,
    )
    a_keep, a_send, b_keep, b_send = run(
        in_kernel,
        [shape((2, 24, 1664), BF)] * 4,
        [SMEM] + [VMEM] * 4,
        [s, a_keep, trade(a_send, "x", 0), b_keep, trade(b_send, "z", 0)],
    )
    a_keep, a_send, b_keep, b_send = run(
        two_pairs_kernel,
        [shape((24, 1664), BF)] * 4,
        [VMEM] * 4,
        [a_keep, trade(a_send, "z", 1), b_keep, trade(b_send, "x", 1)],
    )
    pack_sends = run(
        in_again_kernel,
        [shape((8, 6400), BF)] * 4,
        [SMEM] + [VMEM] * 5,
        [s, a_keep, trade(a_send, "z", 0), b_keep, trade(b_send, "x", 0), up_sum],
        us=1.5,
    )
    keep, send = run(
        last_kernel,
        [shape((8, 3584), F32), shape((8, 2816), BF)],
        [VMEM] * 4,
        spread_once(pack_sends, "y"),
    )
    input_weight_grad, expand_weight_grad, output_weight_grad, table = run(
        owned_kernel,
        [shape((6, 2304), F32), shape((6, 3072), F32), shape((6, 768), F32), shape((16, 8), F32)],
        [SMEM] + [VMEM] * 2,
        [s, keep, swap(send)],
    )
    (grad_input,) = run(
        input_kernel,
        [shape((128, 768), F32)],
        [VMEM] * 8,
        [own, *halo, tokens, grad_middle, vec],
    )
    vectors = [table[k, 0:6] for k in range(12)]
    return (
        layer_out,
        grad_input,
        vectors[0],
        vectors[1],
        input_weight_grad,
        vectors[2],
        vectors[3],
        output_weight_grad,
        vectors[4],
        vectors[5],
        vectors[6],
        expand_weight_grad,
        table[8:12, 0:6].reshape(24),
        reduce_weight_grad,
        vectors[7],
    )


def solution(mesh):
    fine = Mesh(mesh.devices.reshape(2, 2, 4, 2, 4), ("zl", "c", "x", "zh", "y"))
    token = P(("x", "zh", "y", "zl", "c"))
    param = P(("zl", "c", "x", "zh", "y"))
    return jax.shard_map(
        local,
        mesh=fine,
        in_specs=(token, token, P(("x", "zh", "y"))) + (param,) * 13,
        out_specs=(token, token) + (param,) * 13,
        check_vma=False,
    )
```

```python
import jax
import jax.numpy as jnp
from jax import lax
from jax.experimental import pallas as pl
from jax.experimental.pallas import tpu as pltpu
from jax.sharding import Mesh
from jax.sharding import PartitionSpec as P

CHIPS = ("zl", "x", "zh", "y")
BF = jnp.bfloat16
F32 = jnp.float32
I32 = jnp.int32
SMEM = pl.BlockSpec(memory_space=pltpu.SMEM)
VMEM = pl.BlockSpec(memory_space=pltpu.VMEM)
HBM = pl.BlockSpec(memory_space=pltpu.HBM)


def chip_shift(value, distance):
    def at(place):
        place = place % 64
        zl, rest = place % 2, place // 2
        y, rest = rest % 4, rest // 4
        zh, x = rest % 2, rest // 2
        return ((zl * 4 + x) * 2 + zh) * 4 + y

    return lax.ppermute(value, CHIPS, [(at(t), at(t + distance)) for t in range(64)])


def swap(value):
    return lax.ppermute(value, "c", [(0, 1), (1, 0)])


def ring_shift(value, axis, distance):
    if axis == "z":
        place = [0, 2, 1, 3]
        return lax.ppermute(
            value, ("zl", "zh"), [(place[i], place[(i + distance) % 4]) for i in range(4)]
        )
    return lax.ppermute(value, axis, [(i, (i + distance) % 4) for i in range(4)])


def trade(value, axis, step):
    def at(core, place):
        if axis == "z":
            return ((place % 2) * 2 + core) * 2 + place // 2
        return core * 4 + place

    pairs = []
    for core in range(2):
        flip = 1 if core == step else 3
        pairs += [(at(core, m), at(core, m ^ flip)) for m in range(4)]
    return lax.ppermute(value, ("zl", "c", "zh") if axis == "z" else ("c", axis), pairs)


def around(value, axis):
    pair = jnp.stack([value, trade(value, axis, 0)])
    return pair, trade(pair, axis, 1)


def around_once(value, axis):
    after = ring_shift(value, axis, 1), ring_shift(value, axis, 3), ring_shift(value, axis, 2)
    return (value, after[0], after[2], after[1])


def spread_once(blocks, axis):
    got = (
        ring_shift(blocks[1], axis, 1),
        ring_shift(blocks[3], axis, 3),
        ring_shift(blocks[2], axis, 2),
    )
    return (blocks[0], got[0], got[2], got[1])


def after(value, *others):
    return lax.optimization_barrier((value, others))[0]


def shape(dims, kind):
    return jax.ShapeDtypeStruct(dims, kind)


def run(body, outs, specs, args, scratch=(), out_specs=None, us=1.0, vmem=24):
    return pl.pallas_call(
        body,
        out_shape=tuple(outs),
        in_specs=list(specs),
        out_specs=tuple(out_specs or [VMEM] * len(outs)),
        scratch_shapes=list(scratch),
        name=body.__name__,
        cost_estimate=pl.CostEstimate(
            flops=int(us * 600e6), bytes_accessed=int(us * 1.5e6), transcendentals=0
        ),
        compiler_params=pltpu.CompilerParams(vmem_limit_bytes=vmem << 20),
    )(*args)


def dot(left, right):
    return jnp.dot(left, right, preferred_element_type=F32)


def dot_t(left, right):
    return lax.dot_general(left, right, (((1,), (1,)), ((), ())), preferred_element_type=F32)


def outer(left, right):
    return lax.dot_general(left, right, (((0,), (0,)), ((), ())), preferred_element_type=F32)


def places(s_ref):
    return s_ref[0], s_ref[1], s_ref[2], s_ref[3], s_ref[4]


def wrap(value):
    return lax.rem(value + 4, 4)


def seat(place, core, j):
    return place ^ (0, 1 + 2 * core, 3 - 2 * core, 2)[j]


def unit_table(transposed):
    dims = (1536, 384) if transposed else (384, 1536)
    unit = lax.broadcasted_iota(I32, dims, 0 if transposed else 1)
    group = (unit * 2731) >> 16
    rest = unit - group * 24
    spot = group * 6 + rest - 6 * ((rest * 43) >> 8)
    return jnp.where(
        spot == lax.broadcasted_iota(I32, dims, 1 if transposed else 0), 1.0, 0.0
    ).astype(BF)


def unit_quarter():
    unit = lax.broadcasted_iota(I32, (8, 1536), 1)
    rest = unit - 24 * ((unit * 2731) >> 16)
    return ((rest * 43) >> 8) == lax.broadcasted_iota(I32, (8, 1536), 0)


def flat(blocks):
    count, _, columns = blocks.shape
    return blocks.astype(F32).reshape(count * 24, columns).astype(BF)


def cut(rows):
    return rows.reshape(rows.shape[0] // 24, 24, rows.shape[1]).astype(BF)


def move_all(copies):
    for source, target in copies:
        target[...] = source[...]


def unit_of(values):
    centered = values - jnp.mean(values, -1, keepdims=True)
    scale = lax.rsqrt(jnp.mean(centered * centered, -1, keepdims=True) + 1e-05)
    return centered * scale, scale


def norm_backward(grad_out, unit, scale, gain):
    scaled = grad_out * gain
    return scale * (
        scaled
        - jnp.mean(scaled, -1, keepdims=True)
        - unit * jnp.mean(scaled * unit, -1, keepdims=True)
    )


def halves_kernel(s_ref, in_hbm, up_hbm, *refs):
    vectors, (mine_ref, send_ref, in_ref, up_ref), held, sems = (
        refs[0:9], refs[9:13], refs[13:22], refs[22]
    )
    moves = [
        pltpu.make_async_copy(a, b, sems.at[i])
        for i, (a, b) in enumerate(zip((in_hbm, up_hbm, *vectors), (in_ref, up_ref, *held)))
    ]
    for move in moves:
        move.start()
    for move in moves:
        move.wait()
    core = s_ref[0]
    v0, v1, v2, v3, v4, v5, v6, v7, v8 = held
    rows = [v[...].astype(F32) for v in (v0, v1, v2, v3, v4, v5, v6, v7)]
    rows += [v8[...].astype(F32)[:, k * 6 : k * 6 + 6] for k in range(4)]
    rows = jnp.concatenate(rows + [jnp.zeros((4, 6), F32)], 0)
    small = jnp.concatenate(
        [jnp.concatenate([rows, jnp.zeros((16, 122), F32)], 1), jnp.zeros((112, 128), F32)], 0
    ).T[0:6, :]

    def half(which):
        parts = [in_ref[:, j * 384 + which * 192 : j * 384 + which * 192 + 192] for j in range(6)]
        parts.append(small)
        parts += [up_ref[:, j * 1536 + which * 768 : j * 1536 + which * 768 + 768] for j in range(2)]
        return jnp.concatenate([p.astype(F32) for p in parts], 1)

    first, second = half(0), half(1)
    mine_ref[0:6, :] = jnp.where(core == 0, first, second).astype(BF)
    send_ref[0:6, :] = jnp.where(core == 0, second, first).astype(BF)
    mine_ref[6:8, :] = jnp.zeros((2, 2816), BF)
    send_ref[6:8, :] = jnp.zeros((2, 2816), BF)


def pack_kernel(mine_ref, other_ref, out_ref, pack_ref):
    pack_ref[:, 0:2816] = mine_ref[...]
    pack_ref[:, 2816:5632] = other_ref[...]
    pack_ref[0:6, 5632:] = out_ref[...]
    pack_ref[6:8, 5632:] = jnp.zeros((2, 768), BF)


def rows_kernel(s_ref, p0, p1, p2, p3, down_ref, a_ref, b_ref, up_ref):
    y = s_ref[3]
    pieces = [p[...].astype(F32) for p in (p0, p1, p2, p3)]
    parts = []
    for place in range(4):
        d = wrap(y - place)
        block = pieces[0]
        for k in (1, 2, 3):
            block = jnp.where(d == k, pieces[k], block)
        parts.append(block[0:6])
    rows = jnp.concatenate(parts, 0).astype(BF)
    a_ref[:, 0:1280] = rows[:, 0:1280]
    a_ref[:, 1280:] = rows[:, 5632:6016]
    b_ref[:, 0:1280] = rows[:, 2816:4096]
    b_ref[:, 1280:] = rows[:, 6016:]
    up_ref[:, 0:1536] = rows[:, 1280:2816]
    up_ref[:, 1536:3072] = rows[:, 4096:5632]
    up_ref[:, 3072:] = down_ref[...]


def half_row(row, core):
    first = jnp.concatenate([row[:, 0:192], row[:, 384:576]], 1)
    second = jnp.concatenate([row[:, 192:384], row[:, 576:768]], 1)
    return jnp.where(core == 0, first, second)


def project_kernel(
    s_ref, m0, m1, m2, m3, m4, o_ref, w0, w1, w2, w3,
    low_ref, win_ref, wout_ref, vec_ref, q_ref, kv_ref, mask_ref, up_ref,
    win, wout,
):
    core, x, z, _, chip = places(s_ref)
    mine = (m0, m1, m2, m3, m4)
    copies = []
    for j in range(4):
        for i in range(4):
            for k, c in enumerate((core, 1 - core)):
                outer_, inner_ = ((x, z), (z, x))[k]
                outer_, inner_ = seat(outer_, core, j), seat(inner_, core, i)
                xs, zs = ((outer_, inner_), (inner_, outer_))[k]
                base = xs * 2 + (zs >> 1)
                zl = zs & 1
                piece = ((w0, w1), (w2, w3))[k][j // 2]
                copies.append(
                    (piece.at[j % 2, i, :, pl.ds(0, 1280)], win.at[zl * 16 + c * 8 + base])
                )
                copies.append(
                    (
                        piece.at[j % 2, i, :, pl.ds(1280, 384)],
                        wout.at[zl * 8 + base, :, pl.ds(k * 384, 384)],
                    )
                )
    move_all(copies)
    seg_rows = []
    for i in range(5):
        seg_rows.append(mine[i][128:136, 0:128].astype(F32)[0:1])
        seg_rows.append(o_ref[i, 128:136, 0:128].astype(F32)[0:1])
    seg_query = jnp.concatenate(seg_rows[8:], 1)
    seg_cols = jnp.concatenate(seg_rows + [jnp.zeros((118, 128), F32)], 0).T
    lane = lax.broadcasted_iota(I32, (1, 256), 1)
    start = chip * 256
    pos_query = jnp.where(lane < 128, start + core * 128 + lane, start + (1 - core) * 128 + lane - 128)
    for b in range(10):
        i, k = b // 2, b % 2
        first = start - (4 - i) * 256 + (core if k == 0 else 1 - core) * 128
        pos = first + lax.broadcasted_iota(I32, (128, 256), 0)
        allowed = (seg_cols[:, b : b + 1] == seg_query) & (pos <= pos_query) & (pos >= 0)
        mask_ref[b * 128 : (b + 1) * 128, :] = jnp.where(allowed, 0.0, -1e30).astype(BF)
    win_ref[...] = flat(win[...])
    wout_ref[...] = flat(wout[...])
    vec_ref[...] = win_ref[:, 1152:1280].astype(F32).T[0:16]
    gain, shift = vec_ref[0:1, :], vec_ref[1:2, :]
    bias_q = half_row(vec_ref[2:3, :], core)
    bias_v = half_row(vec_ref[3:4, :], core)
    bias_kv = jnp.concatenate([jnp.zeros((1, 384), F32), bias_v], 1)
    for i in range(5):
        values = jnp.concatenate([mine[i][0:128, :], o_ref[i, 0:128, :]], 0).astype(F32)
        unit, _ = unit_of(values)
        low = (unit * gain + shift).astype(BF)
        low_ref[i * 256 : (i + 1) * 256, :] = low
        kv_ref[i * 256 : (i + 1) * 256, :] = (dot(low, win_ref[:, 384:1152]) + bias_kv).astype(BF)
        if i == 4:
            q_ref[...] = (dot(low, win_ref[:, 0:384]) + bias_q).astype(BF)
    quarters = jnp.concatenate(
        [half_row(vec_ref[8 + k : 9 + k, :], core) for k in range(4)] + [jnp.zeros((4, 384), F32)], 0
    )
    biases = dot(quarters.astype(BF), unit_table(False))
    up_ref[...] = jnp.sum(jnp.where(unit_quarter(), biases, 0.0), 0, keepdims=True)


def attend_kernel(q_ref, kv_ref, mask_ref, wout_ref, att_ref, lse_ref, pm_ref, po_ref):
    head_lane = lax.broadcasted_iota(I32, (1, 128), 1)
    for p in range(3):
        keys = kv_ref[:, p * 128 : (p + 1) * 128]
        vals_t = kv_ref[:, 384 + p * 128 : 512 + p * 128].T
        query = q_ref[:, p * 128 : (p + 1) * 128]
        parts = []
        for h in range(2):
            picked = jnp.where((head_lane < 64) == (h == 0), query, jnp.zeros_like(query))
            scores = dot_t(keys, picked) * 0.125 + mask_ref[...].astype(F32)
            top = jnp.max(scores, 0, keepdims=True)
            expo = jnp.exp(scores - top)
            total = jnp.sum(expo, 0, keepdims=True)
            probs = (expo * (1.0 / total)).astype(BF)
            lse_ref[2 * p + h : 2 * p + h + 1, :] = top + jnp.log(total)
            parts.append(dot(vals_t[h * 64 : (h + 1) * 64], probs))
        att_ref[:, p * 128 : (p + 1) * 128] = jnp.concatenate(parts, 0).T.astype(BF)
    part = dot(att_ref[...], wout_ref[...])
    pm_ref[...] = part[0:128]
    po_ref[...] = part[128:256]


def project(s, mine, other, pieces):
    return run(
        project_kernel,
        [
            shape((1280, 768), BF),
            shape((768, 1280), BF),
            shape((384, 768), BF),
            shape((16, 768), F32),
            shape((256, 384), BF),
            shape((1280, 768), BF),
            shape((1280, 256), BF),
            shape((1, 1536), F32),
        ],
        [SMEM] + [VMEM] * 10,
        [s, *mine, other, *pieces],
        [pltpu.VMEM((32, 24, 1280), BF), pltpu.VMEM((16, 24, 768), BF)],
        us=60.0,
        vmem=20,
    )


def attend(args):
    return run(
        attend_kernel,
        [
            shape((256, 384), BF),
            shape((8, 256), F32),
            shape((128, 768), F32),
            shape((128, 768), F32),
        ],
        [VMEM] * 4,
        args,
        us=60.0,
        vmem=16,
    )


def attend_back_kernel(
    gm_ref, go_ref, att_ref, wout_ref, q_ref, kv_ref, lse_ref, mask_ref, dq, dkv, dwout
):
    grad = jnp.concatenate([gm_ref[...], go_ref[...]], 0)
    back = dot_t(grad, wout_ref[...]).astype(BF)
    head_lane = lax.broadcasted_iota(I32, (1, 128), 1)
    for p in range(3):
        keys = kv_ref[:, p * 128 : (p + 1) * 128]
        vals = kv_ref[:, 384 + p * 128 : 512 + p * 128]
        keys_t = keys.T
        query = q_ref[:, p * 128 : (p + 1) * 128]
        grad_p = back[:, p * 128 : (p + 1) * 128]
        parts = []
        dk = jnp.zeros((1280, 128), F32)
        dv = jnp.zeros((1280, 128), F32)
        for h in range(2):
            here = (head_lane < 64) == (h == 0)
            picked = jnp.where(here, query, jnp.zeros_like(query))
            grad_h = jnp.where(here, grad_p, jnp.zeros_like(grad_p))
            scores = dot_t(keys, picked) * 0.125 + mask_ref[...].astype(F32)
            probs = jnp.exp(scores - lse_ref[2 * p + h : 2 * p + h + 1, :])
            dp = dot_t(vals, grad_h)
            inner = jnp.sum(probs * dp, 0, keepdims=True)
            ds = (probs * (dp - inner)).astype(BF)
            dv = dv + dot(probs.astype(BF), grad_h)
            dk = dk + dot(ds, picked)
            parts.append(dot(keys_t[h * 64 : (h + 1) * 64], ds))
        dq[:, p * 128 : (p + 1) * 128] = (jnp.concatenate(parts, 0).T * 0.125).astype(BF)
        dkv[:, p * 128 : (p + 1) * 128] = (dk * 0.125).astype(BF)
        dkv[:, 384 + p * 128 : 512 + p * 128] = dv.astype(BF)
    dwout[...] = outer(att_ref[...], grad).astype(BF)


def attend_back(args):
    return run(
        attend_back_kernel,
        [shape((256, 384), BF), shape((1280, 768), BF), shape((384, 768), BF)],
        [VMEM] * 8,
        args,
        us=2.0,
        vmem=20,
    )


def early_back_kernel(
    s_ref, dq, dkv, win_ref, m0, m1, m2, m3, m4, o_ref, dm_ref, do_ref, sums_ref
):
    core = s_ref[0]
    mine = (m0, m1, m2, m3, m4)
    gain_sum = jnp.zeros((1, 768), F32)
    shift_sum = jnp.zeros((1, 768), F32)
    value_sum = jnp.zeros((1, 384), F32)
    for i in range(5):
        rows = slice(i * 256, (i + 1) * 256)
        da = dot_t(dkv[rows, :], win_ref[:, 384:1152])
        if i == 4:
            da = da + dot_t(dq[...], win_ref[:, 0:384])
        values = jnp.concatenate([mine[i][0:128, :], o_ref[i, 0:128, :]], 0).astype(F32)
        unit, _ = unit_of(values)
        gain_sum = gain_sum + jnp.sum(da * unit, 0, keepdims=True)
        shift_sum = shift_sum + jnp.sum(da, 0, keepdims=True)
        value_sum = value_sum + jnp.sum(dkv[rows, 384:768].astype(F32), 0, keepdims=True)
        dm_ref[i] = da[0:128]
        do_ref[i] = da[128:256].astype(BF)
    query_sum = jnp.sum(dq[...].astype(F32), 0, keepdims=True)
    sums_ref[0:1, :] = gain_sum
    sums_ref[1:2, :] = shift_sum
    sums_ref[2:3, :] = widened(query_sum, core)
    sums_ref[3:4, :] = widened(value_sum, core)
    sums_ref[4:8, :] = jnp.zeros((4, 768), F32)


def early_back(args):
    return run(
        early_back_kernel,
        [shape((5, 128, 768), F32), shape((5, 128, 768), BF), shape((8, 768), F32)],
        [SMEM] + [VMEM] * 9,
        args,
        us=2.0,
        vmem=20,
    )


def widened(row, core):
    zero = jnp.zeros((1, 192), F32)
    a, b = row[:, 0:192], row[:, 192:384]
    return jnp.where(
        core == 0,
        jnp.concatenate([a, zero, b, zero], 1),
        jnp.concatenate([zero, a, zero, b], 1),
    )


def weight_back_kernel(
    s_ref, dq, dkv, dwo_ref, low_ref, sums_ref, more_ref, ups_ref, s0, s1, s2, s3, dwin, dwout
):
    core, x, z, _, _ = places(s_ref)
    dwin[:, :, 0:384] = cut(outer(low_ref[1024:1280, :], dq[...]))
    dwin[:, :, 384:1152] = cut(outer(low_ref[...], dkv[...]))
    dwout[...] = cut(dwo_ref[...].astype(F32))
    quarters = dot(jnp.where(unit_quarter(), ups_ref[...], 0.0).astype(BF), unit_table(True))
    table = jnp.concatenate(
        [
            more_ref[0:4, :],
            sums_ref[0:4, :],
            *[widened(quarters[k : k + 1, :], core) for k in range(4)],
            jnp.zeros((116, 768), F32),
        ],
        0,
    )
    dwin[:, :, 1152:1280] = cut(table.T)
    copies = []
    for j in range(4):
        for i in range(4):
            for k, c in enumerate((core, 1 - core)):
                first = seat((x, z)[k], core, j)
                xs, zs = ((first, i), (i, first))[k]
                base = xs * 2 + (zs >> 1)
                zl = zs & 1
                piece = ((s0, s1), (s2, s3))[k][j // 2]
                copies.append(
                    (dwin.at[zl * 16 + c * 8 + base], piece.at[j % 2, i, :, pl.ds(0, 1280)])
                )
                copies.append(
                    (
                        dwout.at[zl * 8 + base, :, pl.ds(k * 384, 384)],
                        piece.at[j % 2, i, :, pl.ds(1280, 384)],
                    )
                )
    move_all(copies)


def weight_back(args):
    return run(
        weight_back_kernel,
        [shape((2, 4, 24, 1664), BF)] * 4,
        [SMEM] + [VMEM] * 7,
        args,
        [pltpu.VMEM((32, 24, 1280), BF), pltpu.VMEM((16, 24, 768), BF)],
        us=2.0,
        vmem=20,
    )


def middle_kernel(x_ref, a_ref, b_ref, vec_ref, mid_ref, low_ref):
    middle = x_ref[...].astype(F32) + (a_ref[...] + b_ref[...]) + vec_ref[4:5, :]
    unit, _ = unit_of(middle)
    mid_ref[...] = middle
    low_ref[...] = (unit * vec_ref[5:6, :] + vec_ref[6:7, :]).astype(BF)


def forward_kernel(
    s_ref, am_ref, ao_ref, gm_ref, go_ref, bias_ref, e0, e1, r0, r1,
    om_ref, oo_ref, dm_ref, do_ref, ups_ref, p0, p1, t0, t1,
    wup3, wdown3, wup, wdown, dup, ddown,
):
    core, x, z, y, _ = places(s_ref)
    copies = []
    for j in range(4):
        xs = seat(x, core, j)
        for i in range(4):
            zs = seat(z, core, i)
            base = (zs & 1) * 16 + xs * 2 + (zs >> 1)
            for k, c in enumerate((core, 1 - core)):
                copies.append(
                    (
                        (e0, e1)[j // 2].at[j % 2, i, :, pl.ds(k * 1536, 1536)],
                        wup3.at[base + c * 8],
                    )
                )
    for j in range(4):
        for iz in range(4):
            zs = seat(z, core, iz)
            for ix in range(4):
                base = (zs & 1) * 32 + (zs >> 1) * 4 + seat(x, core, ix) * 8 + seat(y, core, j)
                copies.append(((r0, r1)[j // 2].at[j % 2, ix, iz], wdown3.at[base]))
    move_all(copies)
    low = jnp.concatenate([am_ref[...], ao_ref[...]], 0)
    grad = jnp.concatenate([gm_ref[...], go_ref[...]], 0)
    low_t = low.T
    out = jnp.zeros((256, 768), F32)
    da = jnp.zeros((256, 768), F32)
    for b in range(2):
        cols = slice(b * 768, (b + 1) * 768)
        blocks = slice(b * 32, (b + 1) * 32)
        wup[:, cols] = flat(wup3[:, :, cols])
        hidden = dot(low, wup[:, cols]) + bias_ref[:, cols]
        square = hidden * hidden
        bent = jnp.tanh(0.7978845608 * hidden * (1.0 + 0.044715 * square))
        rest = 0.5 * (1.0 + bent)
        active = (hidden * rest).astype(BF)
        slope = rest + 0.5 * hidden * (1.0 - bent * bent) * (
            0.7978845608 * (1.0 + 3.0 * 0.044715 * square)
        )
        wdown[cols, :] = flat(wdown3[blocks])
        back = (dot_t(grad, wdown[cols, :]) * slope).astype(BF)
        out = out + dot(active, wdown[cols, :])
        da = da + dot_t(back, wup[:, cols])
        ddown[blocks] = cut(outer(active, grad))
        dup[:, :, cols] = cut(dot(low_t, back))
        ups_ref[:, cols] = jnp.sum(back.astype(F32), 0, keepdims=True)
        copies = []
        for j in range(4):
            xs = seat(x, core, j)
            for i in range(4):
                base = (i % 2) * 16 + xs * 2 + i // 2
                for k, c in enumerate((core, 1 - core)):
                    copies.append(
                        (
                            dup.at[base + c * 8, :, pl.ds(b * 768, 768)],
                            (p0, p1)[j // 2].at[j % 2, i, :, pl.ds(k * 1536 + b * 768, 768)],
                        )
                    )
        for j in range(4):
            ys = seat(y, core, j)
            for zh in range(2):
                for ix in range(4):
                    copies.append(
                        (
                            ddown.at[b * 32 + ix * 8 + zh * 4 + ys],
                            (t0, t1)[j // 2].at[j % 2, zh * 2 + b, ix],
                        )
                    )
        move_all(copies)
    om_ref[...] = out[0:128]
    oo_ref[...] = out[128:256]
    dm_ref[...] = da[0:128]
    do_ref[...] = da[128:256]


def forward(args):
    return run(
        forward_kernel,
        [shape((128, 768), F32)] * 4
        + [shape((1, 1536), F32)]
        + [shape((2, 4, 24, 3072), BF)] * 2
        + [shape((2, 4, 4, 24, 768), BF)] * 2,
        [SMEM] + [VMEM] * 9,
        args,
        [
            pltpu.VMEM((32, 24, 1536), BF),
            pltpu.VMEM((64, 24, 768), BF),
            pltpu.VMEM((768, 1536), BF),
            pltpu.VMEM((1536, 768), BF),
            pltpu.VMEM((32, 24, 1536), BF),
            pltpu.VMEM((64, 24, 768), BF),
        ],
        us=6.0,
        vmem=24,
    )


def middle_back_kernel(
    mid_ref, om_ref, ox_ref, dm_ref, dx_ref, g_ref, vec_ref, out_ref, gmid_ref, low_ref, sums_ref
):
    middle = mid_ref[...]
    out_ref[...] = (middle + (om_ref[...] + ox_ref[...]) + vec_ref[7:8, :]).astype(BF)
    unit, scale = unit_of(middle)
    da = dm_ref[...] + dx_ref[...]
    grad = g_ref[...].astype(F32)
    total = grad + norm_backward(da, unit, scale, vec_ref[5:6, :])
    low = total.astype(BF)
    gmid_ref[...] = total
    low_ref[...] = low
    sums_ref[0:1, :] = jnp.sum(low.astype(F32), 0, keepdims=True)
    sums_ref[1:2, :] = jnp.sum(da * unit, 0, keepdims=True)
    sums_ref[2:3, :] = jnp.sum(da, 0, keepdims=True)
    sums_ref[3:4, :] = jnp.sum(grad, 0, keepdims=True)
    sums_ref[4:8, :] = jnp.zeros((4, 768), F32)


def added(refs, index=None):
    total = None
    for ref in refs:
        value = (ref[...] if index is None else ref[index]).astype(F32)
        total = value if total is None else total + value
    return total


def total_of(keep, got, *index):
    if not index:
        return keep[...].astype(F32) + got[...].astype(F32)
    return keep[index].astype(F32) + got[index].astype(F32)


def pair_kernel(keep, got, mine, send):
    mine[...] = total_of(keep, got, 0).astype(BF)
    send[...] = total_of(keep, got, 1).astype(BF)


def two_pairs_kernel(ka, ga, kb, gb, ma, sa, mb, sb):
    pair_kernel(ka, ga, ma, sa)
    pair_kernel(kb, gb, mb, sb)


def up_down_kernel(s_ref, ka, ga, kb, gb, mine, send):
    core, z = s_ref[0], s_ref[2]
    for j in range(4):
        zs = seat(z, core, j)
        out = (mine, send)[j // 2]
        out[j % 2, :, 0:3072] = total_of(ka, ga, zs).astype(BF)
        for xs in range(4):
            out[j % 2, :, 3072 + xs * 768 : 3840 + xs * 768] = total_of(kb, gb, zs, xs).astype(BF)


def up_down_again_kernel(s_ref, keep, got, up_ref, o0, o1, o2, o3):
    x = s_ref[1]
    total = total_of(keep, got)
    up_ref[...] = total[:, 0:3072].astype(BF)
    parts = [total[:, 3072 + i * 768 : 3840 + i * 768] for i in range(4)]
    for k, out in enumerate((o0, o1, o2, o3)):
        xs = wrap(x + k)
        block = parts[0]
        for i in (1, 2, 3):
            block = jnp.where(xs == i, parts[i], block)
        out[...] = block.astype(BF)


def down_kernel(a0, a1, a2, a3, out_ref):
    out_ref[...] = added((a0, a1, a2, a3))


def in_kernel(s_ref, ka, ga, kb, gb, ma, sa, mb, sb):
    core, x, z, _, _ = places(s_ref)
    for j in range(4):
        (ma, sa)[j // 2][j % 2] = total_of(ka, ga, seat(z, core, j)).astype(BF)
        (mb, sb)[j // 2][j % 2] = total_of(kb, gb, seat(x, core, j)).astype(BF)


def in_again_kernel(s_ref, ka, ga, kb, gb, up_ref, o0, o1, o2, o3):
    y = s_ref[3]
    a, b = total_of(ka, ga), total_of(kb, gb)
    up = up_ref[...].astype(F32)
    rows = jnp.concatenate(
        [a[:, 0:1280], up[:, 0:1536], b[:, 0:1280], up[:, 1536:], a[:, 1280:], b[:, 1280:]], 1
    )
    parts = [rows[i * 6 : i * 6 + 6] for i in range(4)]
    for k, out in enumerate((o0, o1, o2, o3)):
        ys = wrap(y + k)
        block = parts[0]
        for i in (1, 2, 3):
            block = jnp.where(ys == i, parts[i], block)
        out[0:6, :] = block.astype(BF)
        out[6:8, :] = jnp.zeros((2, 6400), BF)


def last_kernel(a0, a1, a2, a3, keep_ref, send_ref):
    total = added((a0, a1, a2, a3))
    keep_ref[:, 0:2816] = total[:, 0:2816]
    keep_ref[:, 2816:] = total[:, 5632:]
    send_ref[...] = total[:, 2816:5632].astype(BF)


def owned_kernel(s_ref, keep_ref, got_ref, in_ref, up_ref, out_ref, sums_ref):
    core = s_ref[0]
    mine = keep_ref[:, 0:2816]
    other = got_ref[...].astype(F32)
    first = jnp.where(core == 0, mine, other)
    second = jnp.where(core == 0, other, mine)
    for j in range(6):
        part = slice(j * 192, j * 192 + 192)
        in_ref[:, j * 384 : j * 384 + 192] = first[0:6, part]
        in_ref[:, j * 384 + 192 : j * 384 + 384] = second[0:6, part]
    for j in range(2):
        part = slice(1280 + j * 768, 2048 + j * 768)
        up_ref[:, j * 1536 : j * 1536 + 768] = first[0:6, part]
        up_ref[:, j * 1536 + 768 : j * 1536 + 1536] = second[0:6, part]
    out_ref[...] = keep_ref[0:6, 2816:]
    sums_ref[...] = (mine[:, 1152:1280] + other[:, 1152:1280]).T[0:16, :]


def halo_kernel(dm_ref, dx_ref, own_ref, h0, h1, h2, h3):
    for i, out in enumerate((h0, h1, h2, h3)):
        out[...] = (dm_ref[i] + dx_ref[i].astype(F32)).astype(BF)
    own_ref[...] = dm_ref[4] + dx_ref[4].astype(F32)


def input_kernel(own_ref, h0, h1, h2, h3, x_ref, gmid_ref, vec_ref, out_ref):
    total = own_ref[...] + added((h0, h1, h2, h3))
    unit, scale = unit_of(x_ref[...].astype(F32))
    out_ref[...] = gmid_ref[...] + norm_backward(total, unit, scale, vec_ref[0:1, :])


def local(
    tokens,
    cotangent,
    segments,
    first_gain,
    first_shift,
    input_weight,
    query_bias,
    value_bias,
    output_weight,
    output_bias,
    second_gain,
    second_shift,
    expand_weight,
    expand_bias,
    reduce_weight,
    reduce_bias,
):
    core = lax.axis_index("c")
    zl, zh = lax.axis_index("zl"), lax.axis_index("zh")
    x, y = lax.axis_index("x"), lax.axis_index("y")
    chip = ((x * 2 + zh) * 4 + y) * 2 + zl
    s = jnp.stack([core, x, zh * 2 + zl, y, chip]).astype(I32)
    seg_own = lax.dynamic_slice_in_dim(segments, (zl * 2 + core) * 128, 128).astype(BF)
    ext = jnp.concatenate([tokens, jnp.pad(seg_own[None], ((0, 7), (0, 640)))], 0)
    grad_other = swap(cotangent)
    chunks = [chip_shift(ext, d) for d in (4, 3)]
    small = [
        first_gain,
        first_shift,
        query_bias,
        value_bias,
        output_bias,
        second_gain,
        second_shift,
        reduce_bias,
        expand_bias,
    ]
    mine, send = run(
        halves_kernel,
        [shape((8, 2816), BF)] * 2,
        [SMEM] + [HBM] * 11,
        [s, *[pltpu.with_memory_space_constraint(v, pltpu.HBM) for v in (input_weight, expand_weight, *[v[None] for v in small])]],
        [pltpu.VMEM((6, 2304), BF), pltpu.VMEM((6, 3072), BF)]
        + [pltpu.VMEM((1, 6), BF)] * 8
        + [pltpu.VMEM((1, 24), BF), pltpu.SemaphoreType.DMA((11,))],
    )
    other = swap(send)
    (pack,) = run(
        pack_kernel, [shape((8, 6400), BF)], [VMEM] * 3, [mine, other, output_weight], us=0.7
    )
    part_a, part_b, up_part = run(
        rows_kernel,
        [shape((24, 1664), BF), shape((24, 1664), BF), shape((24, 3840), BF)],
        [SMEM] + [VMEM] * 5,
        [s, *around_once(pack, "y"), reduce_weight],
        us=1.5,
    )
    pair_a = jnp.stack([part_a, trade(part_a, "z", 0)])
    pair_b = jnp.stack([part_b, trade(part_b, "x", 0)])
    up_part = after(up_part, pair_a, pair_b)
    all_a = jnp.concatenate([pair_a, trade(pair_a, "z", 1)], 0)
    all_b = jnp.concatenate([pair_b, trade(pair_b, "x", 1)], 0)
    up_pair = jnp.stack([up_part, trade(up_part, "z", 0)])
    chunks += [chip_shift(after(ext, pair_a, pair_b), d) for d in (2, 1)] + [ext]
    up_pair = after(up_pair, all_a, all_b)
    pair_a = jnp.stack([all_a, trade(all_a, "x", 0)])
    pair_b = jnp.stack([all_b, trade(all_b, "z", 0)])
    up_z = jnp.concatenate([up_pair, trade(up_pair, "z", 1)], 0)
    up_z = after(up_z, pair_a, pair_b)
    in_a = (pair_a, trade(pair_a, "x", 1))
    in_b = (pair_b, trade(pair_b, "z", 1))
    chunks_other = swap(jnp.stack(chunks))
    up_pieces = around(up_z[:, :, :3072], "x")
    down_pieces = around(jnp.concatenate(around(up_z[:, :, 3072:], "x"), 0), "y")

    low, win, wout, vec, query, pair, mask, bias_up = project(
        s, chunks, chunks_other, in_a + in_b
    )
    att, lse, part_m, part_o = attend([query, pair, mask, wout])
    middle, low_two = run(
        middle_kernel,
        [shape((128, 768), F32), shape((128, 768), BF)],
        [VMEM] * 4,
        [tokens, part_m, swap(part_o), vec],
    )
    (out_m, out_o, da_m, da_o, ups, up_keep, up_send, down_keep, down_send) = forward(
        [s, low_two, swap(low_two), cotangent, grad_other, bias_up, *up_pieces, *down_pieces]
    )
    layer_out, grad_middle, grad_branch, sums = run(
        middle_back_kernel,
        [shape((128, 768), BF), shape((128, 768), F32), shape((128, 768), BF), shape((8, 768), F32)],
        [VMEM] * 7,
        [middle, out_m, swap(out_o), da_m, swap(da_o), cotangent, vec],
        us=2.0,
    )
    up_got = trade(up_send, "x", 1)
    down_got = trade(down_send, "y", 1)
    dq, dkv, dwout = attend_back(
        [grad_branch, swap(grad_branch), att, wout, query, pair, lse, mask]
    )
    up_got = after(up_got, dq)
    up_keep, up_send, down_keep, down_send = run(
        two_pairs_kernel,
        [shape((4, 24, 3072), BF)] * 2 + [shape((4, 4, 24, 768), BF)] * 2,
        [VMEM] * 4,
        [up_keep, up_got, down_keep, down_got],
        us=2.0,
    )
    up_got, down_got = trade(up_send, "x", 0), trade(down_send, "y", 0)
    da_mine, da_other, more = early_back(
        [s, after(dq, up_keep), dkv, win, *chunks, chunks_other]
    )
    a_keep, a_send, b_keep, b_send = weight_back([s, dq, dkv, dwout, low, sums, more, ups])
    up_got = after(up_got, a_keep)
    a_got, b_got = trade(a_send, "x", 1), trade(b_send, "z", 1)
    own, *halo = run(
        halo_kernel,
        [shape((128, 768), F32)] + [shape((128, 768), BF)] * 4,
        [VMEM] * 2,
        [da_mine, swap(da_other)],
    )
    halo = [chip_shift(h, -d) for h, d in zip(halo, (4, 3, 2, 1))]
    a_keep = after(a_keep, own)
    mixed_keep, mixed_send = run(
        up_down_kernel,
        [shape((2, 24, 6144), BF)] * 2,
        [SMEM] + [VMEM] * 4,
        [s, up_keep, up_got, down_keep, down_got],
        us=1.5,
    )
    mixed_keep, mixed_send = run(
        pair_kernel,
        [shape((24, 6144), BF)] * 2,
        [VMEM] * 2,
        [mixed_keep, trade(mixed_send, "z", 1)],
    )
    up_sum, *down_sends = run(
        up_down_again_kernel,
        [shape((24, 3072), BF)] + [shape((24, 768), BF)] * 4,
        [SMEM] + [VMEM] * 2,
        [s, mixed_keep, trade(mixed_send, "z", 0)],
    )
    (reduce_weight_grad,) = run(
        down_kernel, [shape((24, 768), F32)], [VMEM] * 4, spread_once(down_sends, "x"), us=0.7
    )
    a_keep, a_send, b_keep, b_send = run(
        two_pairs_kernel,
        [shape((4, 24, 1664), BF)] * 4,
        [VMEM] * 4,
        [a_keep, a_got, b_keep, b_got],
        us=1.5,
    )
    a_keep, a_send, b_keep, b_send = run(
        in_kernel,
        [shape((2, 24, 1664), BF)] * 4,
        [SMEM] + [VMEM] * 4,
        [s, a_keep, trade(a_send, "x", 0), b_keep, trade(b_send, "z", 0)],
    )
    a_keep = after(a_keep, *halo[0:2])
    a_keep, a_send, b_keep, b_send = run(
        two_pairs_kernel,
        [shape((24, 1664), BF)] * 4,
        [VMEM] * 4,
        [a_keep, trade(a_send, "z", 1), b_keep, trade(b_send, "x", 1)],
    )
    pack_sends = run(
        in_again_kernel,
        [shape((8, 6400), BF)] * 4,
        [SMEM] + [VMEM] * 5,
        [s, a_keep, trade(a_send, "z", 0), b_keep, trade(b_send, "x", 0), up_sum],
        us=1.5,
    )
    pack_sends = (after(pack_sends[0], *halo), *pack_sends[1:])
    keep, send = run(
        last_kernel,
        [shape((8, 3584), F32), shape((8, 2816), BF)],
        [VMEM] * 4,
        spread_once(pack_sends, "y"),
    )
    input_weight_grad, expand_weight_grad, output_weight_grad, table = run(
        owned_kernel,
        [shape((6, 2304), F32), shape((6, 3072), F32), shape((6, 768), F32), shape((16, 8), F32)],
        [SMEM] + [VMEM] * 2,
        [s, keep, swap(send)],
    )
    (grad_input,) = run(
        input_kernel,
        [shape((128, 768), F32)],
        [VMEM] * 8,
        [own, *halo, tokens, grad_middle, vec],
    )
    vectors = [table[k, 0:6] for k in range(12)]
    return (
        layer_out,
        grad_input,
        vectors[0],
        vectors[1],
        input_weight_grad,
        vectors[2],
        vectors[3],
        output_weight_grad,
        vectors[4],
        vectors[5],
        vectors[6],
        expand_weight_grad,
        table[8:12, 0:6].reshape(24),
        reduce_weight_grad,
        vectors[7],
    )


def solution(mesh):
    fine = Mesh(mesh.devices.reshape(2, 2, 4, 2, 4), ("zl", "c", "x", "zh", "y"))
    token = P(("x", "zh", "y", "zl", "c"))
    param = P(("zl", "c", "x", "zh", "y"))
    return jax.shard_map(
        local,
        mesh=fine,
        in_specs=(token, token, P(("x", "zh", "y"))) + (param,) * 13,
        out_specs=(token, token) + (param,) * 13,
        check_vma=False,
    )
```

```python
import jax
import jax.numpy as jnp
from jax import lax
from jax.experimental import pallas as pl
from jax.experimental.pallas import tpu as pltpu
from jax.sharding import Mesh
from jax.sharding import PartitionSpec as P

CHIPS = ("zl", "x", "zh", "y")
BF = jnp.bfloat16
F32 = jnp.float32
I32 = jnp.int32
SMEM = pl.BlockSpec(memory_space=pltpu.SMEM)
VMEM = pl.BlockSpec(memory_space=pltpu.VMEM)
HBM = pl.BlockSpec(memory_space=pltpu.HBM)


def chip_shift(value, distance):
    def at(place):
        place = place % 64
        zl, rest = place % 2, place // 2
        y, rest = rest % 4, rest // 4
        zh, x = rest % 2, rest // 2
        return ((zl * 4 + x) * 2 + zh) * 4 + y

    return lax.ppermute(value, CHIPS, [(at(t), at(t + distance)) for t in range(64)])


def swap(value):
    return lax.ppermute(value, "c", [(0, 1), (1, 0)])


def ring_shift(value, axis, distance):
    if axis == "z":
        place = [0, 2, 1, 3]
        return lax.ppermute(
            value, ("zl", "zh"), [(place[i], place[(i + distance) % 4]) for i in range(4)]
        )
    return lax.ppermute(value, axis, [(i, (i + distance) % 4) for i in range(4)])


def trade(value, axis, step):
    def at(core, place):
        if axis == "z":
            return ((place % 2) * 2 + core) * 2 + place // 2
        return core * 4 + place

    pairs = []
    for core in range(2):
        flip = 1 if core == step else 3
        pairs += [(at(core, m), at(core, m ^ flip)) for m in range(4)]
    return lax.ppermute(value, ("zl", "c", "zh") if axis == "z" else ("c", axis), pairs)


def around(value, axis):
    pair = jnp.stack([value, trade(value, axis, 0)])
    return pair, trade(pair, axis, 1)


def around_once(value, axis):
    after = ring_shift(value, axis, 1), ring_shift(value, axis, 3), ring_shift(value, axis, 2)
    return (value, after[0], after[2], after[1])


def spread_once(blocks, axis):
    got = (
        ring_shift(blocks[1], axis, 1),
        ring_shift(blocks[3], axis, 3),
        ring_shift(blocks[2], axis, 2),
    )
    return (blocks[0], got[0], got[2], got[1])


def after(value, *others):
    return lax.optimization_barrier((value, others))[0]


def shape(dims, kind):
    return jax.ShapeDtypeStruct(dims, kind)


def run(body, outs, specs, args, scratch=(), out_specs=None, us=1.0, vmem=24):
    return pl.pallas_call(
        body,
        out_shape=tuple(outs),
        in_specs=list(specs),
        out_specs=tuple(out_specs or [VMEM] * len(outs)),
        scratch_shapes=list(scratch),
        name=body.__name__,
        cost_estimate=pl.CostEstimate(
            flops=int(us * 600e6), bytes_accessed=int(us * 1.5e6), transcendentals=0
        ),
        compiler_params=pltpu.CompilerParams(vmem_limit_bytes=vmem << 20),
    )(*args)


def dot(left, right):
    return jnp.dot(left, right, preferred_element_type=F32)


def dot_t(left, right):
    return lax.dot_general(left, right, (((1,), (1,)), ((), ())), preferred_element_type=F32)


def outer(left, right):
    return lax.dot_general(left, right, (((0,), (0,)), ((), ())), preferred_element_type=F32)


def places(s_ref):
    return s_ref[0], s_ref[1], s_ref[2], s_ref[3], s_ref[4]


def wrap(value):
    return lax.rem(value + 4, 4)


def seat(place, core, j):
    return place ^ (0, 1 + 2 * core, 3 - 2 * core, 2)[j]


def unit_table(transposed):
    dims = (1536, 384) if transposed else (384, 1536)
    unit = lax.broadcasted_iota(I32, dims, 0 if transposed else 1)
    group = (unit * 2731) >> 16
    rest = unit - group * 24
    spot = group * 6 + rest - 6 * ((rest * 43) >> 8)
    return jnp.where(
        spot == lax.broadcasted_iota(I32, dims, 1 if transposed else 0), 1.0, 0.0
    ).astype(BF)


def unit_quarter():
    unit = lax.broadcasted_iota(I32, (8, 1536), 1)
    rest = unit - 24 * ((unit * 2731) >> 16)
    return ((rest * 43) >> 8) == lax.broadcasted_iota(I32, (8, 1536), 0)


def flat(blocks):
    count, _, columns = blocks.shape
    return blocks.astype(F32).reshape(count * 24, columns).astype(BF)


def cut(rows):
    return rows.reshape(rows.shape[0] // 24, 24, rows.shape[1]).astype(BF)


def move_all(copies):
    for source, target in copies:
        target[...] = source[...]


def unit_of(values):
    centered = values - jnp.mean(values, -1, keepdims=True)
    scale = lax.rsqrt(jnp.mean(centered * centered, -1, keepdims=True) + 1e-05)
    return centered * scale, scale


def norm_backward(grad_out, unit, scale, gain):
    scaled = grad_out * gain
    return scale * (
        scaled
        - jnp.mean(scaled, -1, keepdims=True)
        - unit * jnp.mean(scaled * unit, -1, keepdims=True)
    )


def halves_kernel(s_ref, in_hbm, up_hbm, *refs):
    vectors, (mine_ref, send_ref, in_ref, up_ref), held, sems = (
        refs[0:9], refs[9:13], refs[13:22], refs[22]
    )
    moves = [
        pltpu.make_async_copy(a, b, sems.at[i])
        for i, (a, b) in enumerate(zip((in_hbm, up_hbm, *vectors), (in_ref, up_ref, *held)))
    ]
    for move in moves:
        move.start()
    for move in moves:
        move.wait()
    core = s_ref[0]
    v0, v1, v2, v3, v4, v5, v6, v7, v8 = held
    rows = [v[...].astype(F32) for v in (v0, v1, v2, v3, v4, v5, v6, v7)]
    rows += [v8[...].astype(F32)[:, k * 6 : k * 6 + 6] for k in range(4)]
    rows = jnp.concatenate(rows + [jnp.zeros((4, 6), F32)], 0)
    small = jnp.concatenate(
        [jnp.concatenate([rows, jnp.zeros((16, 122), F32)], 1), jnp.zeros((112, 128), F32)], 0
    ).T[0:6, :]

    def half(which):
        parts = [in_ref[:, j * 384 + which * 192 : j * 384 + which * 192 + 192] for j in range(6)]
        parts.append(small)
        parts += [up_ref[:, j * 1536 + which * 768 : j * 1536 + which * 768 + 768] for j in range(2)]
        return jnp.concatenate([p.astype(F32) for p in parts], 1)

    first, second = half(0), half(1)
    mine_ref[0:6, :] = jnp.where(core == 0, first, second).astype(BF)
    send_ref[0:6, :] = jnp.where(core == 0, second, first).astype(BF)
    mine_ref[6:8, :] = jnp.zeros((2, 2816), BF)
    send_ref[6:8, :] = jnp.zeros((2, 2816), BF)


def pack_kernel(mine_ref, other_ref, out_ref, pack_ref):
    pack_ref[:, 0:2816] = mine_ref[...]
    pack_ref[:, 2816:5632] = other_ref[...]
    pack_ref[0:6, 5632:] = out_ref[...]
    pack_ref[6:8, 5632:] = jnp.zeros((2, 768), BF)


def rows_kernel(s_ref, p0, p1, p2, p3, a_ref, b_ref, up_ref):
    y = s_ref[3]
    pieces = [p[...].astype(F32) for p in (p0, p1, p2, p3)]
    parts = []
    for place in range(4):
        d = wrap(y - place)
        block = pieces[0]
        for k in (1, 2, 3):
            block = jnp.where(d == k, pieces[k], block)
        parts.append(block[0:6])
    rows = jnp.concatenate(parts, 0).astype(BF)
    a_ref[:, 0:1280] = rows[:, 0:1280]
    a_ref[:, 1280:] = rows[:, 5632:6016]
    b_ref[:, 0:1280] = rows[:, 2816:4096]
    b_ref[:, 1280:] = rows[:, 6016:]
    up_ref[:, 0:1536] = rows[:, 1280:2816]
    up_ref[:, 1536:3072] = rows[:, 4096:5632]


def half_row(row, core):
    first = jnp.concatenate([row[:, 0:192], row[:, 384:576]], 1)
    second = jnp.concatenate([row[:, 192:384], row[:, 576:768]], 1)
    return jnp.where(core == 0, first, second)


def project_kernel(
    s_ref, m0, m12, m3, m4, o_ref, w0, w1, w2, w3,
    low_ref, win_ref, wout_ref, vec_ref, q_ref, kv_ref, mask_ref, up_ref,
    win, wout,
):
    core, x, z, _, chip = places(s_ref)
    mine = (m0, m12.at[0], m12.at[1], m3, m4)
    copies = []
    for j in range(4):
        for i in range(4):
            for k, c in enumerate((core, 1 - core)):
                outer_, inner_ = ((x, z), (z, x))[k]
                outer_, inner_ = seat(outer_, core, j), seat(inner_, core, i)
                xs, zs = ((outer_, inner_), (inner_, outer_))[k]
                base = xs * 2 + (zs >> 1)
                zl = zs & 1
                piece = ((w0, w1), (w2, w3))[k][j // 2]
                copies.append(
                    (piece.at[j % 2, i, :, pl.ds(0, 1280)], win.at[zl * 16 + c * 8 + base])
                )
                copies.append(
                    (
                        piece.at[j % 2, i, :, pl.ds(1280, 384)],
                        wout.at[zl * 8 + base, :, pl.ds(k * 384, 384)],
                    )
                )
    move_all(copies)
    seg_rows = []
    for i in range(5):
        seg_rows.append(mine[i][128:136, 0:128].astype(F32)[0:1])
        seg_rows.append(o_ref[i, 128:136, 0:128].astype(F32)[0:1])
    seg_query = jnp.concatenate(seg_rows[8:], 1)
    seg_cols = jnp.concatenate(seg_rows + [jnp.zeros((118, 128), F32)], 0).T
    lane = lax.broadcasted_iota(I32, (1, 256), 1)
    start = chip * 256
    pos_query = jnp.where(lane < 128, start + core * 128 + lane, start + (1 - core) * 128 + lane - 128)
    for b in range(10):
        i, k = b // 2, b % 2
        first = start - (4 - i) * 256 + (core if k == 0 else 1 - core) * 128
        pos = first + lax.broadcasted_iota(I32, (128, 256), 0)
        allowed = (seg_cols[:, b : b + 1] == seg_query) & (pos <= pos_query) & (pos >= 0)
        mask_ref[b * 128 : (b + 1) * 128, :] = jnp.where(allowed, 0.0, -1e30).astype(BF)
    win_ref[...] = flat(win[...])
    wout_ref[...] = flat(wout[...])
    vec_ref[...] = win_ref[:, 1152:1280].astype(F32).T[0:16]
    gain, shift = vec_ref[0:1, :], vec_ref[1:2, :]
    bias_q = half_row(vec_ref[2:3, :], core)
    bias_v = half_row(vec_ref[3:4, :], core)
    bias_kv = jnp.concatenate([jnp.zeros((1, 384), F32), bias_v], 1)
    for i in range(5):
        values = jnp.concatenate([mine[i][0:128, :], o_ref[i, 0:128, :]], 0).astype(F32)
        unit, _ = unit_of(values)
        low = (unit * gain + shift).astype(BF)
        low_ref[i * 256 : (i + 1) * 256, :] = low
        kv_ref[i * 256 : (i + 1) * 256, :] = (dot(low, win_ref[:, 384:1152]) + bias_kv).astype(BF)
        if i == 4:
            q_ref[...] = (dot(low, win_ref[:, 0:384]) + bias_q).astype(BF)
    quarters = jnp.concatenate(
        [half_row(vec_ref[8 + k : 9 + k, :], core) for k in range(4)] + [jnp.zeros((4, 384), F32)], 0
    )
    biases = dot(quarters.astype(BF), unit_table(False))
    up_ref[...] = jnp.sum(jnp.where(unit_quarter(), biases, 0.0), 0, keepdims=True)


def attend_kernel(q_ref, kv_ref, mask_ref, wout_ref, att_ref, lse_ref, pm_ref, po_ref):
    head_lane = lax.broadcasted_iota(I32, (1, 128), 1)
    for p in range(3):
        keys = kv_ref[:, p * 128 : (p + 1) * 128]
        vals_t = kv_ref[:, 384 + p * 128 : 512 + p * 128].T
        query = q_ref[:, p * 128 : (p + 1) * 128]
        parts = []
        for h in range(2):
            picked = jnp.where((head_lane < 64) == (h == 0), query, jnp.zeros_like(query))
            scores = dot_t(keys, picked) * 0.125 + mask_ref[...].astype(F32)
            top = jnp.max(scores, 0, keepdims=True)
            expo = jnp.exp(scores - top)
            total = jnp.sum(expo, 0, keepdims=True)
            probs = (expo * (1.0 / total)).astype(BF)
            lse_ref[2 * p + h : 2 * p + h + 1, :] = top + jnp.log(total)
            parts.append(dot(vals_t[h * 64 : (h + 1) * 64], probs))
        att_ref[:, p * 128 : (p + 1) * 128] = jnp.concatenate(parts, 0).T.astype(BF)
    part = dot(att_ref[...], wout_ref[...])
    pm_ref[...] = part[0:128]
    po_ref[...] = part[128:256]


def project(s, mine, other, pieces):
    return run(
        project_kernel,
        [
            shape((1280, 768), BF),
            shape((768, 1280), BF),
            shape((384, 768), BF),
            shape((16, 768), F32),
            shape((256, 384), BF),
            shape((1280, 768), BF),
            shape((1280, 256), BF),
            shape((1, 1536), F32),
        ],
        [SMEM] + [VMEM] * 9,
        [s, *mine, other, *pieces],
        [pltpu.VMEM((32, 24, 1280), BF), pltpu.VMEM((16, 24, 768), BF)],
        us=60.0,
        vmem=20,
    )


def attend(args):
    return run(
        attend_kernel,
        [
            shape((256, 384), BF),
            shape((8, 256), F32),
            shape((128, 768), F32),
            shape((128, 768), F32),
        ],
        [VMEM] * 4,
        args,
        us=60.0,
        vmem=16,
    )


def attend_back_kernel(
    gm_ref, go_ref, att_ref, wout_ref, q_ref, kv_ref, lse_ref, mask_ref, dq, dkv, dwout
):
    grad = jnp.concatenate([gm_ref[...], go_ref[...]], 0)
    back = dot_t(grad, wout_ref[...]).astype(BF)
    head_lane = lax.broadcasted_iota(I32, (1, 128), 1)
    for p in range(3):
        keys = kv_ref[:, p * 128 : (p + 1) * 128]
        vals = kv_ref[:, 384 + p * 128 : 512 + p * 128]
        keys_t = keys.T
        query = q_ref[:, p * 128 : (p + 1) * 128]
        grad_p = back[:, p * 128 : (p + 1) * 128]
        parts = []
        dk = jnp.zeros((1280, 128), F32)
        dv = jnp.zeros((1280, 128), F32)
        for h in range(2):
            here = (head_lane < 64) == (h == 0)
            picked = jnp.where(here, query, jnp.zeros_like(query))
            grad_h = jnp.where(here, grad_p, jnp.zeros_like(grad_p))
            scores = dot_t(keys, picked) * 0.125 + mask_ref[...].astype(F32)
            probs = jnp.exp(scores - lse_ref[2 * p + h : 2 * p + h + 1, :])
            dp = dot_t(vals, grad_h)
            inner = jnp.sum(probs * dp, 0, keepdims=True)
            ds = (probs * (dp - inner)).astype(BF)
            dv = dv + dot(probs.astype(BF), grad_h)
            dk = dk + dot(ds, picked)
            parts.append(dot(keys_t[h * 64 : (h + 1) * 64], ds))
        dq[:, p * 128 : (p + 1) * 128] = (jnp.concatenate(parts, 0).T * 0.125).astype(BF)
        dkv[:, p * 128 : (p + 1) * 128] = (dk * 0.125).astype(BF)
        dkv[:, 384 + p * 128 : 512 + p * 128] = dv.astype(BF)
    dwout[...] = outer(att_ref[...], grad).astype(BF)


def attend_back(args):
    return run(
        attend_back_kernel,
        [shape((256, 384), BF), shape((1280, 768), BF), shape((384, 768), BF)],
        [VMEM] * 8,
        args,
        us=2.0,
        vmem=20,
    )


def early_back_kernel(
    s_ref, dq, dkv, win_ref, m0, m12, m3, m4, o_ref, dm_ref, do_ref, sums_ref
):
    core = s_ref[0]
    mine = (m0, m12.at[0], m12.at[1], m3, m4)
    gain_sum = jnp.zeros((1, 768), F32)
    shift_sum = jnp.zeros((1, 768), F32)
    value_sum = jnp.zeros((1, 384), F32)
    for i in range(5):
        rows = slice(i * 256, (i + 1) * 256)
        da = dot_t(dkv[rows, :], win_ref[:, 384:1152])
        if i == 4:
            da = da + dot_t(dq[...], win_ref[:, 0:384])
        values = jnp.concatenate([mine[i][0:128, :], o_ref[i, 0:128, :]], 0).astype(F32)
        unit, _ = unit_of(values)
        gain_sum = gain_sum + jnp.sum(da * unit, 0, keepdims=True)
        shift_sum = shift_sum + jnp.sum(da, 0, keepdims=True)
        value_sum = value_sum + jnp.sum(dkv[rows, 384:768].astype(F32), 0, keepdims=True)
        dm_ref[i] = da[0:128]
        do_ref[i] = da[128:256].astype(BF)
    query_sum = jnp.sum(dq[...].astype(F32), 0, keepdims=True)
    sums_ref[0:1, :] = gain_sum
    sums_ref[1:2, :] = shift_sum
    sums_ref[2:3, :] = widened(query_sum, core)
    sums_ref[3:4, :] = widened(value_sum, core)
    sums_ref[4:8, :] = jnp.zeros((4, 768), F32)


def early_back(args):
    return run(
        early_back_kernel,
        [shape((5, 128, 768), F32), shape((5, 128, 768), BF), shape((8, 768), F32)],
        [SMEM] + [VMEM] * 8,
        args,
        us=2.0,
        vmem=20,
    )


def widened(row, core):
    zero = jnp.zeros((1, 192), F32)
    a, b = row[:, 0:192], row[:, 192:384]
    return jnp.where(
        core == 0,
        jnp.concatenate([a, zero, b, zero], 1),
        jnp.concatenate([zero, a, zero, b], 1),
    )


def weight_back_kernel(
    s_ref, dq, dkv, dwo_ref, low_ref, sums_ref, more_ref, ups_ref, s0, s1, s2, s3, dwin, dwout
):
    core, x, z, _, _ = places(s_ref)
    dwin[:, :, 0:384] = cut(outer(low_ref[1024:1280, :], dq[...]))
    dwin[:, :, 384:1152] = cut(outer(low_ref[...], dkv[...]))
    dwout[...] = cut(dwo_ref[...].astype(F32))
    quarters = dot(jnp.where(unit_quarter(), ups_ref[...], 0.0).astype(BF), unit_table(True))
    table = jnp.concatenate(
        [
            more_ref[0:4, :],
            sums_ref[0:4, :],
            *[widened(quarters[k : k + 1, :], core) for k in range(4)],
            jnp.zeros((116, 768), F32),
        ],
        0,
    )
    dwin[:, :, 1152:1280] = cut(table.T)
    copies = []
    for j in range(4):
        for i in range(4):
            for k, c in enumerate((core, 1 - core)):
                first = seat((x, z)[k], core, j)
                xs, zs = ((first, i), (i, first))[k]
                base = xs * 2 + (zs >> 1)
                zl = zs & 1
                piece = ((s0, s1), (s2, s3))[k][j // 2]
                copies.append(
                    (dwin.at[zl * 16 + c * 8 + base], piece.at[j % 2, i, :, pl.ds(0, 1280)])
                )
                copies.append(
                    (
                        dwout.at[zl * 8 + base, :, pl.ds(k * 384, 384)],
                        piece.at[j % 2, i, :, pl.ds(1280, 384)],
                    )
                )
    move_all(copies)


def weight_back(args):
    return run(
        weight_back_kernel,
        [shape((2, 4, 24, 1664), BF)] * 4,
        [SMEM] + [VMEM] * 7,
        args,
        [pltpu.VMEM((32, 24, 1280), BF), pltpu.VMEM((16, 24, 768), BF)],
        us=2.0,
        vmem=20,
    )


def middle_kernel(x_ref, a_ref, b_ref, vec_ref, mid_ref, low_ref):
    middle = x_ref[...].astype(F32) + (a_ref[...] + b_ref[...]) + vec_ref[4:5, :]
    unit, _ = unit_of(middle)
    mid_ref[...] = middle
    low_ref[...] = (unit * vec_ref[5:6, :] + vec_ref[6:7, :]).astype(BF)


def forward_kernel(
    s_ref, am_ref, ao_ref, gm_ref, go_ref, bias_ref, e0, e1, r0, r1,
    om_ref, oo_ref, dm_ref, do_ref, ups_ref, p0, p1, t0, t1,
    wup3, wdown3, wup, wdown, dup, ddown,
):
    core, x, z, y, _ = places(s_ref)
    copies = []
    for j in range(4):
        xs = seat(x, core, j)
        for i in range(4):
            zs = seat(z, core, i)
            base = (zs & 1) * 16 + xs * 2 + (zs >> 1)
            for k, c in enumerate((core, 1 - core)):
                copies.append(
                    (
                        (e0, e1)[j // 2].at[j % 2, i, :, pl.ds(k * 1536, 1536)],
                        wup3.at[base + c * 8],
                    )
                )
    for j in range(4):
        for iz in range(4):
            zs = seat(z, core, iz)
            for ix in range(4):
                base = (zs & 1) * 32 + (zs >> 1) * 4 + seat(x, core, ix) * 8 + seat(y, core, j)
                copies.append(((r0, r1)[j // 2].at[j % 2, ix, iz], wdown3.at[base]))
    move_all(copies)
    low = jnp.concatenate([am_ref[...], ao_ref[...]], 0)
    grad = jnp.concatenate([gm_ref[...], go_ref[...]], 0)
    low_t = low.T
    out = jnp.zeros((256, 768), F32)
    da = jnp.zeros((256, 768), F32)
    for b in range(2):
        cols = slice(b * 768, (b + 1) * 768)
        blocks = slice(b * 32, (b + 1) * 32)
        wup[:, cols] = flat(wup3[:, :, cols])
        hidden = dot(low, wup[:, cols]) + bias_ref[:, cols]
        square = hidden * hidden
        bent = jnp.tanh(0.7978845608 * hidden * (1.0 + 0.044715 * square))
        rest = 0.5 * (1.0 + bent)
        active = (hidden * rest).astype(BF)
        slope = rest + 0.5 * hidden * (1.0 - bent * bent) * (
            0.7978845608 * (1.0 + 3.0 * 0.044715 * square)
        )
        wdown[cols, :] = flat(wdown3[blocks])
        back = (dot_t(grad, wdown[cols, :]) * slope).astype(BF)
        out = out + dot(active, wdown[cols, :])
        da = da + dot_t(back, wup[:, cols])
        ddown[blocks] = cut(outer(active, grad))
        dup[:, :, cols] = cut(dot(low_t, back))
        ups_ref[:, cols] = jnp.sum(back.astype(F32), 0, keepdims=True)
        copies = []
        for j in range(4):
            xs = seat(x, core, j)
            for i in range(4):
                base = (i % 2) * 16 + xs * 2 + i // 2
                for k, c in enumerate((core, 1 - core)):
                    copies.append(
                        (
                            dup.at[base + c * 8, :, pl.ds(b * 768, 768)],
                            (p0, p1)[j // 2].at[j % 2, i, :, pl.ds(k * 1536 + b * 768, 768)],
                        )
                    )
        for j in range(4):
            ys = seat(y, core, j)
            for zh in range(2):
                for ix in range(4):
                    copies.append(
                        (
                            ddown.at[b * 32 + ix * 8 + zh * 4 + ys],
                            (t0, t1)[j // 2].at[j % 2, zh * 2 + b, ix],
                        )
                    )
        move_all(copies)
    om_ref[...] = out[0:128]
    oo_ref[...] = out[128:256]
    dm_ref[...] = da[0:128]
    do_ref[...] = da[128:256]


def forward(args):
    return run(
        forward_kernel,
        [shape((128, 768), F32)] * 4
        + [shape((1, 1536), F32)]
        + [shape((2, 4, 24, 3072), BF)] * 2
        + [shape((2, 4, 4, 24, 768), BF)] * 2,
        [SMEM] + [VMEM] * 9,
        args,
        [
            pltpu.VMEM((32, 24, 1536), BF),
            pltpu.VMEM((64, 24, 768), BF),
            pltpu.VMEM((768, 1536), BF),
            pltpu.VMEM((1536, 768), BF),
            pltpu.VMEM((32, 24, 1536), BF),
            pltpu.VMEM((64, 24, 768), BF),
        ],
        us=6.0,
        vmem=24,
    )


def middle_back_kernel(
    mid_ref, om_ref, ox_ref, dm_ref, dx_ref, g_ref, vec_ref, out_ref, gmid_ref, low_ref, sums_ref
):
    middle = mid_ref[...]
    out_ref[...] = (middle + (om_ref[...] + ox_ref[...]) + vec_ref[7:8, :]).astype(BF)
    unit, scale = unit_of(middle)
    da = dm_ref[...] + dx_ref[...]
    grad = g_ref[...].astype(F32)
    total = grad + norm_backward(da, unit, scale, vec_ref[5:6, :])
    low = total.astype(BF)
    gmid_ref[...] = total
    low_ref[...] = low
    sums_ref[0:1, :] = jnp.sum(low.astype(F32), 0, keepdims=True)
    sums_ref[1:2, :] = jnp.sum(da * unit, 0, keepdims=True)
    sums_ref[2:3, :] = jnp.sum(da, 0, keepdims=True)
    sums_ref[3:4, :] = jnp.sum(grad, 0, keepdims=True)
    sums_ref[4:8, :] = jnp.zeros((4, 768), F32)


def added(refs, index=None):
    total = None
    for ref in refs:
        value = (ref[...] if index is None else ref[index]).astype(F32)
        total = value if total is None else total + value
    return total


def total_of(keep, got, *index):
    if not index:
        return keep[...].astype(F32) + got[...].astype(F32)
    return keep[index].astype(F32) + got[index].astype(F32)


def pair_kernel(keep, got, mine, send):
    mine[...] = total_of(keep, got, 0).astype(BF)
    send[...] = total_of(keep, got, 1).astype(BF)


def two_pairs_kernel(ka, ga, kb, gb, ma, sa, mb, sb):
    pair_kernel(ka, ga, ma, sa)
    pair_kernel(kb, gb, mb, sb)


def up_down_kernel(s_ref, ka, ga, kb, gb, mine, send):
    core, z = s_ref[0], s_ref[2]
    for j in range(4):
        zs = seat(z, core, j)
        out = (mine, send)[j // 2]
        out[j % 2, :, 0:3072] = total_of(ka, ga, zs).astype(BF)
        for xs in range(4):
            out[j % 2, :, 3072 + xs * 768 : 3840 + xs * 768] = total_of(kb, gb, zs, xs).astype(BF)


def up_down_again_kernel(s_ref, keep, got, up_ref, o0, o1, o2, o3):
    x = s_ref[1]
    total = total_of(keep, got)
    up_ref[...] = total[:, 0:3072].astype(BF)
    parts = [total[:, 3072 + i * 768 : 3840 + i * 768] for i in range(4)]
    for k, out in enumerate((o0, o1, o2, o3)):
        xs = wrap(x + k)
        block = parts[0]
        for i in (1, 2, 3):
            block = jnp.where(xs == i, parts[i], block)
        out[...] = block.astype(BF)


def down_kernel(a0, a1, a2, a3, out_ref):
    out_ref[...] = added((a0, a1, a2, a3))


def in_kernel(s_ref, ka, ga, kb, gb, ma, sa, mb, sb):
    core, x, z, _, _ = places(s_ref)
    for j in range(4):
        (ma, sa)[j // 2][j % 2] = total_of(ka, ga, seat(z, core, j)).astype(BF)
        (mb, sb)[j // 2][j % 2] = total_of(kb, gb, seat(x, core, j)).astype(BF)


def in_again_kernel(s_ref, ka, ga, kb, gb, up_ref, o0, o1, o2, o3):
    y = s_ref[3]
    a, b = total_of(ka, ga), total_of(kb, gb)
    up = up_ref[...].astype(F32)
    rows = jnp.concatenate(
        [a[:, 0:1280], up[:, 0:1536], b[:, 0:1280], up[:, 1536:], a[:, 1280:], b[:, 1280:]], 1
    )
    parts = [rows[i * 6 : i * 6 + 6] for i in range(4)]
    for k, out in enumerate((o0, o1, o2, o3)):
        ys = wrap(y + k)
        block = parts[0]
        for i in (1, 2, 3):
            block = jnp.where(ys == i, parts[i], block)
        out[0:6, :] = block.astype(BF)
        out[6:8, :] = jnp.zeros((2, 6400), BF)


def last_kernel(a0, a1, a2, a3, keep_ref, send_ref):
    total = added((a0, a1, a2, a3))
    keep_ref[:, 0:2816] = total[:, 0:2816]
    keep_ref[:, 2816:] = total[:, 5632:]
    send_ref[...] = total[:, 2816:5632].astype(BF)


def owned_kernel(s_ref, keep_ref, got_ref, in_ref, up_ref, out_ref, sums_ref):
    core = s_ref[0]
    mine = keep_ref[:, 0:2816]
    other = got_ref[...].astype(F32)
    first = jnp.where(core == 0, mine, other)
    second = jnp.where(core == 0, other, mine)
    for j in range(6):
        part = slice(j * 192, j * 192 + 192)
        in_ref[:, j * 384 : j * 384 + 192] = first[0:6, part]
        in_ref[:, j * 384 + 192 : j * 384 + 384] = second[0:6, part]
    for j in range(2):
        part = slice(1280 + j * 768, 2048 + j * 768)
        up_ref[:, j * 1536 : j * 1536 + 768] = first[0:6, part]
        up_ref[:, j * 1536 + 768 : j * 1536 + 1536] = second[0:6, part]
    out_ref[...] = keep_ref[0:6, 2816:]
    sums_ref[...] = (mine[:, 1152:1280] + other[:, 1152:1280]).T[0:16, :]


def halo_kernel(dm_ref, dx_ref, own_ref, near_ref, two_ref, far_ref):
    far_ref[...] = total_of(dm_ref, dx_ref, 0).astype(BF)
    near_ref[0] = total_of(dm_ref, dx_ref, 1).astype(BF)
    near_ref[1] = total_of(dm_ref, dx_ref, 3).astype(BF)
    two_ref[...] = total_of(dm_ref, dx_ref, 2)
    own_ref[...] = total_of(dm_ref, dx_ref, 4)


def relay_kernel(two_ref, got_ref, out_ref):
    out_ref[...] = (two_ref[...] + got_ref[0].astype(F32)).astype(BF)


def input_kernel(own_ref, near_ref, two_ref, far_ref, x_ref, gmid_ref, vec_ref, out_ref):
    total = own_ref[...] + near_ref[1].astype(F32) + two_ref[...].astype(F32)
    total = total + far_ref[...].astype(F32)
    unit, scale = unit_of(x_ref[...].astype(F32))
    out_ref[...] = gmid_ref[...] + norm_backward(total, unit, scale, vec_ref[0:1, :])


def local(
    tokens,
    cotangent,
    segments,
    first_gain,
    first_shift,
    input_weight,
    query_bias,
    value_bias,
    output_weight,
    output_bias,
    second_gain,
    second_shift,
    expand_weight,
    expand_bias,
    reduce_weight,
    reduce_bias,
):
    core = lax.axis_index("c")
    zl, zh = lax.axis_index("zl"), lax.axis_index("zh")
    x, y = lax.axis_index("x"), lax.axis_index("y")
    chip = ((x * 2 + zh) * 4 + y) * 2 + zl
    s = jnp.stack([core, x, zh * 2 + zl, y, chip]).astype(I32)
    seg_own = lax.dynamic_slice_in_dim(segments, (zl * 2 + core) * 128, 128).astype(BF)
    ext = jnp.concatenate([tokens, jnp.pad(seg_own[None], ((0, 7), (0, 640)))], 0)
    grad_other = swap(cotangent)
    far = chip_shift(ext, 4)
    down_z = around(reduce_weight, "z")
    small = [
        first_gain,
        first_shift,
        query_bias,
        value_bias,
        output_bias,
        second_gain,
        second_shift,
        reduce_bias,
        expand_bias,
    ]
    mine, send = run(
        halves_kernel,
        [shape((8, 2816), BF)] * 2,
        [SMEM] + [HBM] * 11,
        [s, *[pltpu.with_memory_space_constraint(v, pltpu.HBM) for v in (input_weight, expand_weight, *[v[None] for v in small])]],
        [pltpu.VMEM((6, 2304), BF), pltpu.VMEM((6, 3072), BF)]
        + [pltpu.VMEM((1, 6), BF)] * 8
        + [pltpu.VMEM((1, 24), BF), pltpu.SemaphoreType.DMA((11,))],
    )
    other = swap(send)
    (pack,) = run(
        pack_kernel, [shape((8, 6400), BF)], [VMEM] * 3, [mine, other, output_weight], us=0.7
    )
    part_a, part_b, up_part = run(
        rows_kernel,
        [shape((24, 1664), BF), shape((24, 1664), BF), shape((24, 3072), BF)],
        [SMEM] + [VMEM] * 4,
        [s, *around_once(pack, "y")],
        us=1.5,
    )
    down_x = around(jnp.concatenate(down_z, 0), "x")
    near = chip_shift(after(ext, part_a), 1)
    pair_a = jnp.stack([part_a, trade(part_a, "z", 0)])
    pair_b = jnp.stack([part_b, trade(part_b, "x", 0)])
    up_pair = jnp.stack([up_part, trade(up_part, "z", 0)])
    all_a = jnp.concatenate([pair_a, trade(pair_a, "z", 1)], 0)
    all_b = jnp.concatenate([pair_b, trade(pair_b, "x", 1)], 0)
    up_z = jnp.concatenate([up_pair, trade(up_pair, "z", 1)], 0)
    down_pieces = around(jnp.concatenate(down_x, 0), "y")
    middle_two = chip_shift(jnp.stack([after(near, all_a), ext]), 2)
    chunks = [far, middle_two, near, ext]
    pair_a = jnp.stack([all_a, trade(all_a, "x", 0)])
    pair_b = jnp.stack([all_b, trade(all_b, "z", 0)])
    up_z = after(up_z, pair_a, pair_b)
    in_a = (pair_a, trade(pair_a, "x", 1))
    in_b = (pair_b, trade(pair_b, "z", 1))
    chunks_other = swap(jnp.concatenate([far[None], middle_two, near[None], ext[None]], 0))
    up_pieces = around(up_z, "x")

    low, win, wout, vec, query, pair, mask, bias_up = project(
        s, chunks, chunks_other, in_a + in_b
    )
    att, lse, part_m, part_o = attend([query, pair, mask, wout])
    middle, low_two = run(
        middle_kernel,
        [shape((128, 768), F32), shape((128, 768), BF)],
        [VMEM] * 4,
        [tokens, part_m, swap(part_o), vec],
    )
    (out_m, out_o, da_m, da_o, ups, up_keep, up_send, down_keep, down_send) = forward(
        [s, low_two, swap(low_two), cotangent, grad_other, bias_up, *up_pieces, *down_pieces]
    )
    layer_out, grad_middle, grad_branch, sums = run(
        middle_back_kernel,
        [shape((128, 768), BF), shape((128, 768), F32), shape((128, 768), BF), shape((8, 768), F32)],
        [VMEM] * 7,
        [middle, out_m, swap(out_o), da_m, swap(da_o), cotangent, vec],
        us=2.0,
    )
    up_got = trade(up_send, "x", 1)
    down_got = trade(down_send, "y", 1)
    dq, dkv, dwout = attend_back(
        [grad_branch, swap(grad_branch), att, wout, query, pair, lse, mask]
    )
    up_got = after(up_got, dq)
    up_keep, up_send, down_keep, down_send = run(
        two_pairs_kernel,
        [shape((4, 24, 3072), BF)] * 2 + [shape((4, 4, 24, 768), BF)] * 2,
        [VMEM] * 4,
        [up_keep, up_got, down_keep, down_got],
        us=2.0,
    )
    up_got, down_got = trade(up_send, "x", 0), trade(down_send, "y", 0)
    da_mine, da_other, more = early_back(
        [s, after(dq, up_keep), dkv, win, *chunks, chunks_other]
    )
    a_keep, a_send, b_keep, b_send = weight_back([s, dq, dkv, dwout, low, sums, more, ups])
    up_got = after(up_got, a_keep)
    a_got, b_got = trade(a_send, "x", 1), trade(b_send, "z", 1)
    own, near, two, far = run(
        halo_kernel,
        [
            shape((128, 768), F32),
            shape((2, 128, 768), BF),
            shape((128, 768), F32),
            shape((128, 768), BF),
        ],
        [VMEM] * 2,
        [da_mine, swap(da_other)],
    )
    near, far = chip_shift(near, -1), chip_shift(far, -4)
    (two,) = run(relay_kernel, [shape((128, 768), BF)], [VMEM] * 2, [two, near], us=0.5)
    relayed = two
    two = chip_shift(two, -2)
    a_keep = after(a_keep, own)
    mixed_keep, mixed_send = run(
        up_down_kernel,
        [shape((2, 24, 6144), BF)] * 2,
        [SMEM] + [VMEM] * 4,
        [s, up_keep, up_got, down_keep, down_got],
        us=1.5,
    )
    mixed_got = trade(mixed_send, "z", 1)
    a_keep, a_send, b_keep, b_send = run(
        two_pairs_kernel,
        [shape((4, 24, 1664), BF)] * 4,
        [VMEM] * 4,
        [a_keep, a_got, b_keep, b_got],
        us=1.5,
    )
    a_keep, a_send, b_keep, b_send = run(
        in_kernel,
        [shape((2, 24, 1664), BF)] * 4,
        [SMEM] + [VMEM] * 4,
        [s, a_keep, trade(a_send, "x", 0), b_keep, trade(b_send, "z", 0)],
    )
    mixed_keep, mixed_send = run(
        pair_kernel,
        [shape((24, 6144), BF)] * 2,
        [VMEM] * 2,
        [mixed_keep, after(mixed_got, a_keep)],
    )
    mixed_got = trade(mixed_send, "z", 0)
    a_keep = after(a_keep, relayed)
    a_keep, a_send, b_keep, b_send = run(
        two_pairs_kernel,
        [shape((24, 1664), BF)] * 4,
        [VMEM] * 4,
        [a_keep, trade(a_send, "z", 1), b_keep, trade(b_send, "x", 1)],
    )
    up_sum, *down_sends = run(
        up_down_again_kernel,
        [shape((24, 3072), BF)] + [shape((24, 768), BF)] * 4,
        [SMEM] + [VMEM] * 2,
        [s, mixed_keep, after(mixed_got, a_keep)],
    )
    pack_sends = run(
        in_again_kernel,
        [shape((8, 6400), BF)] * 4,
        [SMEM] + [VMEM] * 5,
        [s, a_keep, trade(a_send, "z", 0), b_keep, trade(b_send, "x", 0), up_sum],
        us=1.5,
    )
    pack_sends = (after(pack_sends[0], two, far), *pack_sends[1:])
    down_sends = after(down_sends, pack_sends)
    (reduce_weight_grad,) = run(
        down_kernel, [shape((24, 768), F32)], [VMEM] * 4, spread_once(down_sends, "x"), us=0.7
    )
    keep, send = run(
        last_kernel,
        [shape((8, 3584), F32), shape((8, 2816), BF)],
        [VMEM] * 4,
        spread_once(pack_sends, "y"),
    )
    input_weight_grad, expand_weight_grad, output_weight_grad, table = run(
        owned_kernel,
        [shape((6, 2304), F32), shape((6, 3072), F32), shape((6, 768), F32), shape((16, 8), F32)],
        [SMEM] + [VMEM] * 2,
        [s, keep, swap(send)],
    )
    (grad_input,) = run(
        input_kernel,
        [shape((128, 768), F32)],
        [VMEM] * 7,
        [own, near, two, far, tokens, grad_middle, vec],
    )
    vectors = [table[k, 0:6] for k in range(12)]
    return (
        layer_out,
        grad_input,
        vectors[0],
        vectors[1],
        input_weight_grad,
        vectors[2],
        vectors[3],
        output_weight_grad,
        vectors[4],
        vectors[5],
        vectors[6],
        expand_weight_grad,
        table[8:12, 0:6].reshape(24),
        reduce_weight_grad,
        vectors[7],
    )


def solution(mesh):
    fine = Mesh(mesh.devices.reshape(2, 2, 4, 2, 4), ("zl", "c", "x", "zh", "y"))
    token = P(("x", "zh", "y", "zl", "c"))
    param = P(("zl", "c", "x", "zh", "y"))
    return jax.shard_map(
        local,
        mesh=fine,
        in_specs=(token, token, P(("x", "zh", "y"))) + (param,) * 13,
        out_specs=(token, token) + (param,) * 13,
        check_vma=False,
    )
```

```python
import jax
import jax.numpy as jnp
from jax import lax
from jax.experimental import pallas as pl
from jax.experimental.pallas import tpu as pltpu
from jax.sharding import Mesh
from jax.sharding import PartitionSpec as P

CHIPS = ("zl", "x", "zh", "y")
BF = jnp.bfloat16
F32 = jnp.float32
I32 = jnp.int32
SMEM = pl.BlockSpec(memory_space=pltpu.SMEM)
VMEM = pl.BlockSpec(memory_space=pltpu.VMEM)
HBM = pl.BlockSpec(memory_space=pltpu.HBM)


def chip_shift(value, distance):
    def at(place):
        place = place % 64
        zl, rest = place % 2, place // 2
        y, rest = rest % 4, rest // 4
        zh, x = rest % 2, rest // 2
        return ((zl * 4 + x) * 2 + zh) * 4 + y

    return lax.ppermute(value, CHIPS, [(at(t), at(t + distance)) for t in range(64)])


def swap(value):
    return lax.ppermute(value, "c", [(0, 1), (1, 0)])


def ring_shift(value, axis, distance):
    if axis == "z":
        place = [0, 2, 1, 3]
        return lax.ppermute(
            value, ("zl", "zh"), [(place[i], place[(i + distance) % 4]) for i in range(4)]
        )
    return lax.ppermute(value, axis, [(i, (i + distance) % 4) for i in range(4)])


def trade(value, axis, step):
    def at(core, place):
        if axis == "z":
            return ((place % 2) * 2 + core) * 2 + place // 2
        return core * 4 + place

    pairs = []
    for core in range(2):
        flip = 1 if core == step else 3
        pairs += [(at(core, m), at(core, m ^ flip)) for m in range(4)]
    return lax.ppermute(value, ("zl", "c", "zh") if axis == "z" else ("c", axis), pairs)


def around(value, axis):
    pair = jnp.stack([value, trade(value, axis, 0)])
    return pair, trade(pair, axis, 1)


def around_once(value, axis):
    after = ring_shift(value, axis, 1), ring_shift(value, axis, 3), ring_shift(value, axis, 2)
    return (value, after[0], after[2], after[1])


def spread_once(blocks, axis):
    got = (
        ring_shift(blocks[1], axis, 1),
        ring_shift(blocks[3], axis, 3),
        ring_shift(blocks[2], axis, 2),
    )
    return (blocks[0], got[0], got[2], got[1])


def after(value, *others):
    return lax.optimization_barrier((value, others))[0]


def shape(dims, kind):
    return jax.ShapeDtypeStruct(dims, kind)


def run(body, outs, specs, args, scratch=(), out_specs=None, us=1.0, vmem=24):
    return pl.pallas_call(
        body,
        out_shape=tuple(outs),
        in_specs=list(specs),
        out_specs=tuple(out_specs or [VMEM] * len(outs)),
        scratch_shapes=list(scratch),
        name=body.__name__,
        cost_estimate=pl.CostEstimate(
            flops=int(us * 600e6), bytes_accessed=int(us * 1.5e6), transcendentals=0
        ),
        compiler_params=pltpu.CompilerParams(vmem_limit_bytes=vmem << 20),
    )(*args)


def dot(left, right):
    return jnp.dot(left, right, preferred_element_type=F32)


def dot_t(left, right):
    return lax.dot_general(left, right, (((1,), (1,)), ((), ())), preferred_element_type=F32)


def outer(left, right):
    return lax.dot_general(left, right, (((0,), (0,)), ((), ())), preferred_element_type=F32)


def places(s_ref):
    return s_ref[0], s_ref[1], s_ref[2], s_ref[3], s_ref[4]


def wrap(value):
    return lax.rem(value + 4, 4)


def seat(place, core, j):
    return place ^ (0, 1 + 2 * core, 3 - 2 * core, 2)[j]


def unit_table(transposed):
    dims = (1536, 384) if transposed else (384, 1536)
    unit = lax.broadcasted_iota(I32, dims, 0 if transposed else 1)
    group = (unit * 2731) >> 16
    rest = unit - group * 24
    spot = group * 6 + rest - 6 * ((rest * 43) >> 8)
    return jnp.where(
        spot == lax.broadcasted_iota(I32, dims, 1 if transposed else 0), 1.0, 0.0
    ).astype(BF)


def unit_quarter():
    unit = lax.broadcasted_iota(I32, (8, 1536), 1)
    rest = unit - 24 * ((unit * 2731) >> 16)
    return ((rest * 43) >> 8) == lax.broadcasted_iota(I32, (8, 1536), 0)


def flat(blocks):
    count, _, columns = blocks.shape
    return blocks.astype(F32).reshape(count * 24, columns).astype(BF)


def cut(rows):
    return rows.reshape(rows.shape[0] // 24, 24, rows.shape[1]).astype(BF)


def move_all(copies):
    for source, target in copies:
        target[...] = source[...]


def unit_of(values):
    centered = values - jnp.mean(values, -1, keepdims=True)
    scale = lax.rsqrt(jnp.mean(centered * centered, -1, keepdims=True) + 1e-05)
    return centered * scale, scale


def norm_backward(grad_out, unit, scale, gain):
    scaled = grad_out * gain
    return scale * (
        scaled
        - jnp.mean(scaled, -1, keepdims=True)
        - unit * jnp.mean(scaled * unit, -1, keepdims=True)
    )


def halves_kernel(s_ref, in_hbm, up_hbm, *refs):
    vectors, (mine_ref, send_ref, in_ref, up_ref), held, sems = (
        refs[0:9], refs[9:13], refs[13:22], refs[22]
    )
    moves = [
        pltpu.make_async_copy(a, b, sems.at[i])
        for i, (a, b) in enumerate(zip((in_hbm, up_hbm, *vectors), (in_ref, up_ref, *held)))
    ]
    for move in moves:
        move.start()
    for move in moves:
        move.wait()
    core = s_ref[0]
    v0, v1, v2, v3, v4, v5, v6, v7, v8 = held
    rows = [v[...].astype(F32) for v in (v0, v1, v2, v3, v4, v5, v6, v7)]
    rows += [v8[...].astype(F32)[:, k * 6 : k * 6 + 6] for k in range(4)]
    rows = jnp.concatenate(rows + [jnp.zeros((4, 6), F32)], 0)
    small = jnp.concatenate(
        [jnp.concatenate([rows, jnp.zeros((16, 122), F32)], 1), jnp.zeros((112, 128), F32)], 0
    ).T[0:6, :]

    def half(which):
        parts = [in_ref[:, j * 384 + which * 192 : j * 384 + which * 192 + 192] for j in range(6)]
        parts.append(small)
        parts += [up_ref[:, j * 1536 + which * 768 : j * 1536 + which * 768 + 768] for j in range(2)]
        return jnp.concatenate([p.astype(F32) for p in parts], 1)

    first, second = half(0), half(1)
    mine_ref[0:6, :] = jnp.where(core == 0, first, second).astype(BF)
    send_ref[0:6, :] = jnp.where(core == 0, second, first).astype(BF)
    mine_ref[6:8, :] = jnp.zeros((2, 2816), BF)
    send_ref[6:8, :] = jnp.zeros((2, 2816), BF)


def pack_kernel(mine_ref, other_ref, out_ref, pack_ref):
    pack_ref[:, 0:2816] = mine_ref[...]
    pack_ref[:, 2816:5632] = other_ref[...]
    pack_ref[0:6, 5632:] = out_ref[...]
    pack_ref[6:8, 5632:] = jnp.zeros((2, 768), BF)


def rows_kernel(s_ref, p0, p1, p2, p3, a_ref, b_ref, up_ref):
    y = s_ref[3]
    pieces = [p[...].astype(F32) for p in (p0, p1, p2, p3)]
    parts = []
    for place in range(4):
        d = wrap(y - place)
        block = pieces[0]
        for k in (1, 2, 3):
            block = jnp.where(d == k, pieces[k], block)
        parts.append(block[0:6])
    rows = jnp.concatenate(parts, 0).astype(BF)
    a_ref[:, 0:1280] = rows[:, 0:1280]
    a_ref[:, 1280:] = rows[:, 5632:6016]
    b_ref[:, 0:1280] = rows[:, 2816:4096]
    b_ref[:, 1280:] = rows[:, 6016:]
    up_ref[:, 0:1536] = rows[:, 1280:2816]
    up_ref[:, 1536:3072] = rows[:, 4096:5632]


def half_row(row, core):
    first = jnp.concatenate([row[:, 0:192], row[:, 384:576]], 1)
    second = jnp.concatenate([row[:, 192:384], row[:, 576:768]], 1)
    return jnp.where(core == 0, first, second)


def project_kernel(
    s_ref, m0, m12, m3, m4, o_ref, w0, w1, w2, w3,
    low_ref, win_ref, wout_ref, vec_ref, q_ref, kv_ref, mask_ref, up_ref,
    win, wout,
):
    core, x, z, _, chip = places(s_ref)
    mine = (m0, m12.at[0], m12.at[1], m3, m4)
    copies = []
    for j in range(4):
        for i in range(4):
            for k, c in enumerate((core, 1 - core)):
                outer_, inner_ = ((x, z), (z, x))[k]
                outer_, inner_ = seat(outer_, core, j), seat(inner_, core, i)
                xs, zs = ((outer_, inner_), (inner_, outer_))[k]
                base = xs * 2 + (zs >> 1)
                zl = zs & 1
                piece = ((w0, w1), (w2, w3))[k][j // 2]
                copies.append(
                    (piece.at[j % 2, i, :, pl.ds(0, 1280)], win.at[zl * 16 + c * 8 + base])
                )
                copies.append(
                    (
                        piece.at[j % 2, i, :, pl.ds(1280, 384)],
                        wout.at[zl * 8 + base, :, pl.ds(k * 384, 384)],
                    )
                )
    move_all(copies)
    seg_rows = []
    for i in range(5):
        seg_rows.append(mine[i][128:136, 0:128].astype(F32)[0:1])
        seg_rows.append(o_ref[i, 128:136, 0:128].astype(F32)[0:1])
    seg_query = jnp.concatenate(seg_rows[8:], 1)
    seg_cols = jnp.concatenate(seg_rows + [jnp.zeros((118, 128), F32)], 0).T
    lane = lax.broadcasted_iota(I32, (1, 256), 1)
    start = chip * 256
    pos_query = jnp.where(lane < 128, start + core * 128 + lane, start + (1 - core) * 128 + lane - 128)
    for b in range(10):
        i, k = b // 2, b % 2
        first = start - (4 - i) * 256 + (core if k == 0 else 1 - core) * 128
        pos = first + lax.broadcasted_iota(I32, (128, 256), 0)
        allowed = (seg_cols[:, b : b + 1] == seg_query) & (pos <= pos_query) & (pos >= 0)
        mask_ref[b * 128 : (b + 1) * 128, :] = jnp.where(allowed, 0.0, -1e30)
    win_ref[...] = flat(win[...])
    wout_ref[...] = flat(wout[...])
    vec_ref[...] = win_ref[:, 1152:1280].astype(F32).T[0:16]
    gain, shift = vec_ref[0:1, :], vec_ref[1:2, :]
    bias_q = half_row(vec_ref[2:3, :], core)
    bias_v = half_row(vec_ref[3:4, :], core)
    bias_kv = jnp.concatenate([jnp.zeros((1, 384), F32), bias_v], 1)
    for i in range(5):
        values = jnp.concatenate([mine[i][0:128, :], o_ref[i, 0:128, :]], 0).astype(F32)
        unit, _ = unit_of(values)
        low = (unit * gain + shift).astype(BF)
        low_ref[i * 256 : (i + 1) * 256, :] = low
        kv_ref[i * 256 : (i + 1) * 256, :] = (dot(low, win_ref[:, 384:1152]) + bias_kv).astype(BF)
        if i == 4:
            q_ref[...] = (dot(low, win_ref[:, 0:384]) + bias_q).astype(BF) * BF(0.125)
    quarters = jnp.concatenate(
        [half_row(vec_ref[8 + k : 9 + k, :], core) for k in range(4)] + [jnp.zeros((4, 384), F32)], 0
    )
    biases = dot(quarters.astype(BF), unit_table(False))
    up_ref[...] = jnp.sum(jnp.where(unit_quarter(), biases, 0.0), 0, keepdims=True)


def attend_kernel(q_ref, kv_ref, mask_ref, wout_ref, att_ref, lse_ref, pm_ref, po_ref):
    head_lane = lax.broadcasted_iota(I32, (1, 128), 1)
    for p in range(3):
        keys = kv_ref[:, p * 128 : (p + 1) * 128]
        vals_t = kv_ref[:, 384 + p * 128 : 512 + p * 128].T
        query = q_ref[:, p * 128 : (p + 1) * 128]
        parts = []
        for h in range(2):
            picked = jnp.where((head_lane < 64) == (h == 0), query, jnp.zeros_like(query))
            scores = dot_t(keys, picked) + mask_ref[...]
            top = jnp.max(scores, 0, keepdims=True)
            expo = jnp.exp(scores - top)
            total = jnp.sum(expo, 0, keepdims=True)
            probs = (expo * (1.0 / total)).astype(BF)
            lse_ref[2 * p + h : 2 * p + h + 1, :] = top + jnp.log(total)
            parts.append(dot(vals_t[h * 64 : (h + 1) * 64], probs))
        att_ref[:, p * 128 : (p + 1) * 128] = jnp.concatenate(parts, 0).T.astype(BF)
    part = dot(att_ref[...], wout_ref[...])
    pm_ref[...] = part[0:128]
    po_ref[...] = part[128:256]


def project(s, mine, other, pieces):
    return run(
        project_kernel,
        [
            shape((1280, 768), BF),
            shape((768, 1280), BF),
            shape((384, 768), BF),
            shape((16, 768), F32),
            shape((256, 384), BF),
            shape((1280, 768), BF),
            shape((1280, 256), F32),
            shape((1, 1536), F32),
        ],
        [SMEM] + [VMEM] * 9,
        [s, *mine, other, *pieces],
        [pltpu.VMEM((32, 24, 1280), BF), pltpu.VMEM((16, 24, 768), BF)],
        us=60.0,
        vmem=20,
    )


def attend(args):
    return run(
        attend_kernel,
        [
            shape((256, 384), BF),
            shape((8, 256), F32),
            shape((128, 768), F32),
            shape((128, 768), F32),
        ],
        [VMEM] * 4,
        args,
        us=60.0,
        vmem=16,
    )


def attend_back_kernel(
    gm_ref, go_ref, att_ref, wout_ref, q_ref, kv_ref, lse_ref, mask_ref, dq, dkv, dwout
):
    grad = jnp.concatenate([gm_ref[...], go_ref[...]], 0)
    back = dot_t(grad, wout_ref[...]).astype(BF)
    head_lane = lax.broadcasted_iota(I32, (1, 128), 1)
    for p in range(3):
        keys = kv_ref[:, p * 128 : (p + 1) * 128]
        vals = kv_ref[:, 384 + p * 128 : 512 + p * 128]
        keys_t = keys.T
        query = q_ref[:, p * 128 : (p + 1) * 128]
        grad_p = back[:, p * 128 : (p + 1) * 128]
        parts = []
        dk = jnp.zeros((1280, 128), F32)
        dv = jnp.zeros((1280, 128), F32)
        for h in range(2):
            here = (head_lane < 64) == (h == 0)
            picked = jnp.where(here, query, jnp.zeros_like(query))
            grad_h = jnp.where(here, grad_p, jnp.zeros_like(grad_p))
            scores = dot_t(keys, picked) + mask_ref[...]
            probs = jnp.exp(scores - lse_ref[2 * p + h : 2 * p + h + 1, :])
            dp = dot_t(vals, grad_h)
            inner = jnp.sum(probs * dp, 0, keepdims=True)
            ds = (probs * (dp - inner)).astype(BF)
            dv = dv + dot(probs.astype(BF), grad_h)
            dk = dk + dot(ds, picked)
            parts.append(dot(keys_t[h * 64 : (h + 1) * 64], ds))
        dq[:, p * 128 : (p + 1) * 128] = (jnp.concatenate(parts, 0).T * 0.125).astype(BF)
        dkv[:, p * 128 : (p + 1) * 128] = dk.astype(BF)
        dkv[:, 384 + p * 128 : 512 + p * 128] = dv.astype(BF)
    dwout[...] = outer(att_ref[...], grad).astype(BF)


def attend_back(args):
    return run(
        attend_back_kernel,
        [shape((256, 384), BF), shape((1280, 768), BF), shape((384, 768), BF)],
        [VMEM] * 8,
        args,
        us=2.0,
        vmem=20,
    )


def early_back_kernel(
    s_ref, dq, dkv, win_ref, m0, m12, m3, m4, o_ref, dm_ref, do_ref, sums_ref
):
    core = s_ref[0]
    mine = (m0, m12.at[0], m12.at[1], m3, m4)
    gain_sum = jnp.zeros((1, 768), F32)
    shift_sum = jnp.zeros((1, 768), F32)
    value_sum = jnp.zeros((1, 384), F32)
    for i in range(5):
        rows = slice(i * 256, (i + 1) * 256)
        da = dot_t(dkv[rows, :], win_ref[:, 384:1152])
        if i == 4:
            da = da + dot_t(dq[...], win_ref[:, 0:384])
        values = jnp.concatenate([mine[i][0:128, :], o_ref[i, 0:128, :]], 0).astype(F32)
        unit, _ = unit_of(values)
        gain_sum = gain_sum + jnp.sum(da * unit, 0, keepdims=True)
        shift_sum = shift_sum + jnp.sum(da, 0, keepdims=True)
        value_sum = value_sum + jnp.sum(dkv[rows, 384:768].astype(F32), 0, keepdims=True)
        dm_ref[i] = da[0:128]
        do_ref[i] = da[128:256].astype(BF)
    query_sum = jnp.sum(dq[...].astype(F32), 0, keepdims=True)
    sums_ref[0:1, :] = gain_sum
    sums_ref[1:2, :] = shift_sum
    sums_ref[2:3, :] = widened(query_sum, core)
    sums_ref[3:4, :] = widened(value_sum, core)
    sums_ref[4:8, :] = jnp.zeros((4, 768), F32)


def early_back(args):
    return run(
        early_back_kernel,
        [shape((5, 128, 768), F32), shape((5, 128, 768), BF), shape((8, 768), F32)],
        [SMEM] + [VMEM] * 8,
        args,
        us=2.0,
        vmem=20,
    )


def widened(row, core):
    zero = jnp.zeros((1, 192), F32)
    a, b = row[:, 0:192], row[:, 192:384]
    return jnp.where(
        core == 0,
        jnp.concatenate([a, zero, b, zero], 1),
        jnp.concatenate([zero, a, zero, b], 1),
    )


def weight_back_kernel(
    s_ref, dq, dkv, dwo_ref, low_ref, sums_ref, more_ref, ups_ref, s0, s1, s2, s3, dwin, dwout
):
    core, x, z, _, _ = places(s_ref)
    dwin[:, :, 0:384] = cut(outer(low_ref[1024:1280, :], dq[...]))
    dwin[:, :, 384:1152] = cut(outer(low_ref[...], dkv[...]))
    dwout[...] = cut(dwo_ref[...].astype(F32))
    quarters = dot(jnp.where(unit_quarter(), ups_ref[...], 0.0).astype(BF), unit_table(True))
    table = jnp.concatenate(
        [
            more_ref[0:4, :],
            sums_ref[0:4, :],
            *[widened(quarters[k : k + 1, :], core) for k in range(4)],
            jnp.zeros((116, 768), F32),
        ],
        0,
    )
    dwin[:, :, 1152:1280] = cut(table.T)
    copies = []
    for j in range(4):
        for i in range(4):
            for k, c in enumerate((core, 1 - core)):
                first = seat((x, z)[k], core, j)
                xs, zs = ((first, i), (i, first))[k]
                base = xs * 2 + (zs >> 1)
                zl = zs & 1
                piece = ((s0, s1), (s2, s3))[k][j // 2]
                copies.append(
                    (dwin.at[zl * 16 + c * 8 + base], piece.at[j % 2, i, :, pl.ds(0, 1280)])
                )
                copies.append(
                    (
                        dwout.at[zl * 8 + base, :, pl.ds(k * 384, 384)],
                        piece.at[j % 2, i, :, pl.ds(1280, 384)],
                    )
                )
    move_all(copies)


def weight_back(args):
    return run(
        weight_back_kernel,
        [shape((2, 4, 24, 1664), BF)] * 4,
        [SMEM] + [VMEM] * 7,
        args,
        [pltpu.VMEM((32, 24, 1280), BF), pltpu.VMEM((16, 24, 768), BF)],
        us=2.0,
        vmem=20,
    )


def middle_kernel(x_ref, a_ref, b_ref, vec_ref, mid_ref, low_ref):
    middle = x_ref[...].astype(F32) + (a_ref[...] + b_ref[...]) + vec_ref[4:5, :]
    unit, _ = unit_of(middle)
    mid_ref[...] = middle
    low_ref[...] = (unit * vec_ref[5:6, :] + vec_ref[6:7, :]).astype(BF)


def forward_kernel(
    s_ref, am_ref, ao_ref, gm_ref, go_ref, bias_ref, e0, e1, r0, r1,
    om_ref, oo_ref, dm_ref, do_ref, ups_ref, p0, p1, t0, t1,
    wup3, wdown3, wup, wdown, dup, ddown,
):
    core, x, z, y, _ = places(s_ref)
    copies = []
    for j in range(4):
        xs = seat(x, core, j)
        for i in range(4):
            zs = seat(z, core, i)
            base = (zs & 1) * 16 + xs * 2 + (zs >> 1)
            for k, c in enumerate((core, 1 - core)):
                copies.append(
                    (
                        (e0, e1)[j // 2].at[j % 2, i, :, pl.ds(k * 1536, 1536)],
                        wup3.at[base + c * 8],
                    )
                )
    for j in range(4):
        for iz in range(4):
            zs = seat(z, core, iz)
            for ix in range(4):
                base = (zs & 1) * 32 + (zs >> 1) * 4 + seat(x, core, ix) * 8 + seat(y, core, j)
                copies.append(((r0, r1)[j // 2].at[j % 2, ix, iz], wdown3.at[base]))
    move_all(copies)
    low = jnp.concatenate([am_ref[...], ao_ref[...]], 0)
    grad = jnp.concatenate([gm_ref[...], go_ref[...]], 0)
    low_t = low.T
    out = jnp.zeros((256, 768), F32)
    da = jnp.zeros((256, 768), F32)
    for b in range(2):
        cols = slice(b * 768, (b + 1) * 768)
        blocks = slice(b * 32, (b + 1) * 32)
        wup[:, cols] = flat(wup3[:, :, cols])
        hidden = dot(low, wup[:, cols]) + bias_ref[:, cols]
        square = hidden * hidden
        bent = jnp.tanh(0.7978845608 * hidden * (1.0 + 0.044715 * square))
        rest = 0.5 * (1.0 + bent)
        active = (hidden * rest).astype(BF)
        slope = rest + 0.5 * hidden * (1.0 - bent * bent) * (
            0.7978845608 * (1.0 + 3.0 * 0.044715 * square)
        )
        wdown[cols, :] = flat(wdown3[blocks])
        back = (dot_t(grad, wdown[cols, :]) * slope).astype(BF)
        out = out + dot(active, wdown[cols, :])
        da = da + dot_t(back, wup[:, cols])
        ddown[blocks] = cut(outer(active, grad))
        dup[:, :, cols] = cut(dot(low_t, back))
        ups_ref[:, cols] = jnp.sum(back.astype(F32), 0, keepdims=True)
        copies = []
        for j in range(4):
            xs = seat(x, core, j)
            for i in range(4):
                base = (i % 2) * 16 + xs * 2 + i // 2
                for k, c in enumerate((core, 1 - core)):
                    copies.append(
                        (
                            dup.at[base + c * 8, :, pl.ds(b * 768, 768)],
                            (p0, p1)[j // 2].at[j % 2, i, :, pl.ds(k * 1536 + b * 768, 768)],
                        )
                    )
        move_all(copies)
    copies = []
    for j in range(4):
        zs = seat(z, core, j)
        for ix in range(4):
            for iy in range(4):
                copies.append(
                    (
                        ddown.at[(zs & 1) * 32 + ix * 8 + (zs >> 1) * 4 + iy],
                        (t0, t1)[j // 2].at[j % 2, ix, iy],
                    )
                )
    move_all(copies)
    om_ref[...] = out[0:128]
    oo_ref[...] = out[128:256]
    dm_ref[...] = da[0:128]
    do_ref[...] = da[128:256]


def forward(args):
    return run(
        forward_kernel,
        [shape((128, 768), F32)] * 4
        + [shape((1, 1536), F32)]
        + [shape((2, 4, 24, 3072), BF)] * 2
        + [shape((2, 4, 4, 24, 768), BF)] * 2,
        [SMEM] + [VMEM] * 9,
        args,
        [
            pltpu.VMEM((32, 24, 1536), BF),
            pltpu.VMEM((64, 24, 768), BF),
            pltpu.VMEM((768, 1536), BF),
            pltpu.VMEM((1536, 768), BF),
            pltpu.VMEM((32, 24, 1536), BF),
            pltpu.VMEM((64, 24, 768), BF),
        ],
        us=6.0,
        vmem=24,
    )


def middle_back_kernel(
    mid_ref, om_ref, ox_ref, dm_ref, dx_ref, g_ref, vec_ref, out_ref, gmid_ref, low_ref, sums_ref
):
    middle = mid_ref[...]
    out_ref[...] = (middle + (om_ref[...] + ox_ref[...]) + vec_ref[7:8, :]).astype(BF)
    unit, scale = unit_of(middle)
    da = dm_ref[...] + dx_ref[...]
    grad = g_ref[...].astype(F32)
    total = grad + norm_backward(da, unit, scale, vec_ref[5:6, :])
    low = total.astype(BF)
    gmid_ref[...] = total
    low_ref[...] = low
    sums_ref[0:1, :] = jnp.sum(low.astype(F32), 0, keepdims=True)
    sums_ref[1:2, :] = jnp.sum(da * unit, 0, keepdims=True)
    sums_ref[2:3, :] = jnp.sum(da, 0, keepdims=True)
    sums_ref[3:4, :] = jnp.sum(grad, 0, keepdims=True)
    sums_ref[4:8, :] = jnp.zeros((4, 768), F32)


def added(refs, index=None):
    total = None
    for ref in refs:
        value = (ref[...] if index is None else ref[index]).astype(F32)
        total = value if total is None else total + value
    return total


def total_of(keep, got, *index):
    if not index:
        return keep[...].astype(F32) + got[...].astype(F32)
    return keep[index].astype(F32) + got[index].astype(F32)


def pair_kernel(keep, got, mine, send):
    mine[...] = total_of(keep, got, 0).astype(BF)
    send[...] = total_of(keep, got, 1).astype(BF)


def two_pairs_kernel(ka, ga, kb, gb, ma, sa, mb, sb):
    pair_kernel(ka, ga, ma, sa)
    pair_kernel(kb, gb, mb, sb)


def up_down_kernel(s_ref, ka, ga, kb, gb, ma, sa, mb, sb):
    core, x, z, _, _ = places(s_ref)
    for j in range(4):
        (ma, sa)[j // 2][j % 2] = total_of(ka, ga, seat(z, core, j)).astype(BF)
        (mb, sb)[j // 2][j % 2] = total_of(kb, gb, seat(x, core, j)).astype(BF)


def in_kernel(s_ref, ka, ga, kb, gb, ma, sa, mb, sb):
    core, x, z, _, _ = places(s_ref)
    for j in range(4):
        (ma, sa)[j // 2][j % 2] = total_of(ka, ga, seat(z, core, j)).astype(BF)
        (mb, sb)[j // 2][j % 2] = total_of(kb, gb, seat(x, core, j)).astype(BF)


def in_again_kernel(s_ref, ka, ga, kb, gb, ku, gu, kd, gd, o0, o1, o2, o3):
    y = s_ref[3]
    a, b, up = total_of(ka, ga), total_of(kb, gb), total_of(ku, gu)
    rows = jnp.concatenate(
        [a[:, 0:1280], up[:, 0:1536], b[:, 0:1280], up[:, 1536:], a[:, 1280:], b[:, 1280:]], 1
    )
    parts = [rows[i * 6 : i * 6 + 6] for i in range(4)]
    for k, out in enumerate((o0, o1, o2, o3)):
        ys = wrap(y + k)
        block = parts[0]
        for i in (1, 2, 3):
            block = jnp.where(ys == i, parts[i], block)
        out[0:6, 0:6400] = block.astype(BF)
        out[6:8, 0:6400] = jnp.zeros((2, 6400), BF)
        down = total_of(kd, gd, ys)
        down = jnp.concatenate([down[0:8], down[8:16], down[16:24]], 1)
        out[:, 6400:] = down.astype(BF)


def last_kernel(a0, a1, a2, a3, keep_ref, send_ref, down_ref):
    total = added((a0, a1, a2, a3))
    keep_ref[:, 0:2816] = total[:, 0:2816]
    keep_ref[:, 2816:] = total[:, 5632:6400]
    send_ref[...] = total[:, 2816:5632].astype(BF)
    for i in range(3):
        down_ref[i * 8 : i * 8 + 8, :] = total[:, 6400 + i * 768 : 7168 + i * 768]


def owned_kernel(s_ref, keep_ref, got_ref, in_ref, up_ref, out_ref, sums_ref):
    core = s_ref[0]
    mine = keep_ref[:, 0:2816]
    other = got_ref[...].astype(F32)
    first = jnp.where(core == 0, mine, other)
    second = jnp.where(core == 0, other, mine)
    for j in range(6):
        part = slice(j * 192, j * 192 + 192)
        in_ref[:, j * 384 : j * 384 + 192] = first[0:6, part]
        in_ref[:, j * 384 + 192 : j * 384 + 384] = second[0:6, part]
    for j in range(2):
        part = slice(1280 + j * 768, 2048 + j * 768)
        up_ref[:, j * 1536 : j * 1536 + 768] = first[0:6, part]
        up_ref[:, j * 1536 + 768 : j * 1536 + 1536] = second[0:6, part]
    out_ref[...] = keep_ref[0:6, 2816:]
    sums_ref[...] = (mine[:, 1152:1280] + other[:, 1152:1280]).T[0:16, :]


def halo_kernel(dm_ref, dx_ref, own_ref, near_ref, two_ref, far_ref):
    far_ref[...] = total_of(dm_ref, dx_ref, 0).astype(BF)
    near_ref[0] = total_of(dm_ref, dx_ref, 1).astype(BF)
    near_ref[1] = total_of(dm_ref, dx_ref, 3).astype(BF)
    two_ref[...] = total_of(dm_ref, dx_ref, 2)
    own_ref[...] = total_of(dm_ref, dx_ref, 4)


def relay_kernel(two_ref, got_ref, out_ref):
    out_ref[...] = (two_ref[...] + got_ref[0].astype(F32)).astype(BF)


def input_kernel(own_ref, near_ref, two_ref, far_ref, x_ref, gmid_ref, vec_ref, out_ref):
    total = own_ref[...] + near_ref[1].astype(F32) + two_ref[...].astype(F32)
    total = total + far_ref[...].astype(F32)
    unit, scale = unit_of(x_ref[...].astype(F32))
    out_ref[...] = gmid_ref[...] + norm_backward(total, unit, scale, vec_ref[0:1, :])


def local(
    tokens,
    cotangent,
    segments,
    first_gain,
    first_shift,
    input_weight,
    query_bias,
    value_bias,
    output_weight,
    output_bias,
    second_gain,
    second_shift,
    expand_weight,
    expand_bias,
    reduce_weight,
    reduce_bias,
):
    core = lax.axis_index("c")
    zl, zh = lax.axis_index("zl"), lax.axis_index("zh")
    x, y = lax.axis_index("x"), lax.axis_index("y")
    chip = ((x * 2 + zh) * 4 + y) * 2 + zl
    s = jnp.stack([core, x, zh * 2 + zl, y, chip]).astype(I32)
    seg_own = lax.dynamic_slice_in_dim(segments, (zl * 2 + core) * 128, 128).astype(BF)
    ext = jnp.concatenate([tokens, jnp.pad(seg_own[None], ((0, 7), (0, 640)))], 0)
    grad_other = swap(cotangent)
    far = chip_shift(ext, 4)
    down_z = around(reduce_weight, "z")
    small = [
        first_gain,
        first_shift,
        query_bias,
        value_bias,
        output_bias,
        second_gain,
        second_shift,
        reduce_bias,
        expand_bias,
    ]
    mine, send = run(
        halves_kernel,
        [shape((8, 2816), BF)] * 2,
        [SMEM] + [HBM] * 11,
        [s, *[pltpu.with_memory_space_constraint(v, pltpu.HBM) for v in (input_weight, expand_weight, *[v[None] for v in small])]],
        [pltpu.VMEM((6, 2304), BF), pltpu.VMEM((6, 3072), BF)]
        + [pltpu.VMEM((1, 6), BF)] * 8
        + [pltpu.VMEM((1, 24), BF), pltpu.SemaphoreType.DMA((11,))],
    )
    other = swap(send)
    (pack,) = run(
        pack_kernel, [shape((8, 6400), BF)], [VMEM] * 3, [mine, other, output_weight], us=0.7
    )
    part_a, part_b, up_part = run(
        rows_kernel,
        [shape((24, 1664), BF), shape((24, 1664), BF), shape((24, 3072), BF)],
        [SMEM] + [VMEM] * 4,
        [s, *around_once(pack, "y")],
        us=1.5,
    )
    down_x = around(jnp.concatenate(down_z, 0), "x")
    near = chip_shift(after(ext, part_a), 1)
    pair_a = jnp.stack([part_a, trade(part_a, "z", 0)])
    pair_b = jnp.stack([part_b, trade(part_b, "x", 0)])
    up_pair = jnp.stack([up_part, trade(up_part, "z", 0)])
    all_a = jnp.concatenate([pair_a, trade(pair_a, "z", 1)], 0)
    all_b = jnp.concatenate([pair_b, trade(pair_b, "x", 1)], 0)
    up_z = jnp.concatenate([up_pair, trade(up_pair, "z", 1)], 0)
    down_pieces = around(jnp.concatenate(down_x, 0), "y")
    middle_two = chip_shift(jnp.stack([after(near, all_a), ext]), 2)
    chunks = [far, middle_two, near, ext]
    pair_a = jnp.stack([all_a, trade(all_a, "x", 0)])
    pair_b = jnp.stack([all_b, trade(all_b, "z", 0)])
    in_a = (pair_a, trade(pair_a, "x", 1))
    in_b = (pair_b, trade(pair_b, "z", 1))
    chunks_other = swap(jnp.concatenate([far[None], middle_two, near[None], ext[None]], 0))
    up_pair = jnp.stack([up_z, trade(up_z, "x", 0)])
    up_pair = after(up_pair, in_a[1], in_b[1])
    up_pieces = (up_pair, trade(up_pair, "x", 1))

    low, win, wout, vec, query, pair, mask, bias_up = project(
        s, chunks, chunks_other, in_a + in_b
    )
    att, lse, part_m, part_o = attend([query, pair, mask, wout])
    middle, low_two = run(
        middle_kernel,
        [shape((128, 768), F32), shape((128, 768), BF)],
        [VMEM] * 4,
        [tokens, part_m, swap(part_o), vec],
    )
    (out_m, out_o, da_m, da_o, ups, up_keep, up_send, down_keep, down_send) = forward(
        [s, low_two, swap(low_two), cotangent, grad_other, bias_up, *up_pieces, *down_pieces]
    )
    layer_out, grad_middle, grad_branch, sums = run(
        middle_back_kernel,
        [shape((128, 768), BF), shape((128, 768), F32), shape((128, 768), BF), shape((8, 768), F32)],
        [VMEM] * 7,
        [middle, out_m, swap(out_o), da_m, swap(da_o), cotangent, vec],
        us=2.0,
    )
    up_got = trade(up_send, "x", 1)
    down_got = trade(down_send, "z", 1)
    dq, dkv, dwout = attend_back(
        [grad_branch, swap(grad_branch), att, wout, query, pair, lse, mask]
    )
    up_got = after(up_got, dq)
    up_keep, up_send, down_keep, down_send = run(
        two_pairs_kernel,
        [shape((4, 24, 3072), BF)] * 2 + [shape((4, 4, 24, 768), BF)] * 2,
        [VMEM] * 4,
        [up_keep, up_got, down_keep, down_got],
        us=2.0,
    )
    up_got, down_got = trade(up_send, "x", 0), trade(down_send, "z", 0)
    da_mine, da_other, more = early_back(
        [s, after(dq, up_keep), dkv, win, *chunks, chunks_other]
    )
    a_keep, a_send, b_keep, b_send = weight_back([s, dq, dkv, dwout, low, sums, more, ups])
    up_got = after(up_got, a_keep)
    a_got, b_got = trade(a_send, "x", 1), trade(b_send, "z", 1)
    up_keep, up_send, down_keep, down_send = run(
        up_down_kernel,
        [shape((2, 24, 3072), BF)] * 2 + [shape((2, 4, 24, 768), BF)] * 2,
        [SMEM] + [VMEM] * 4,
        [s, up_keep, up_got, down_keep, down_got],
        us=1.5,
    )
    own, near, two, far = run(
        halo_kernel,
        [
            shape((128, 768), F32),
            shape((2, 128, 768), BF),
            shape((128, 768), F32),
            shape((128, 768), BF),
        ],
        [VMEM] * 2,
        [after(da_mine, up_keep), swap(da_other)],
    )
    near, far = chip_shift(near, -1), chip_shift(far, -4)
    (two,) = run(relay_kernel, [shape((128, 768), BF)], [VMEM] * 2, [two, near], us=0.5)
    relayed = two
    two = chip_shift(two, -2)
    a_keep = after(a_keep, own)
    up_got, down_got = trade(up_send, "z", 1), trade(down_send, "x", 1)
    a_keep, a_send, b_keep, b_send = run(
        two_pairs_kernel,
        [shape((4, 24, 1664), BF)] * 4,
        [VMEM] * 4,
        [a_keep, a_got, b_keep, b_got],
        us=1.5,
    )
    a_keep, a_send, b_keep, b_send = run(
        in_kernel,
        [shape((2, 24, 1664), BF)] * 4,
        [SMEM] + [VMEM] * 4,
        [s, a_keep, trade(a_send, "x", 0), b_keep, trade(b_send, "z", 0)],
    )
    up_keep, up_send, down_keep, down_send = run(
        two_pairs_kernel,
        [shape((24, 3072), BF)] * 2 + [shape((4, 24, 768), BF)] * 2,
        [VMEM] * 4,
        [up_keep, after(up_got, a_keep), down_keep, after(down_got, a_keep)],
    )
    up_got, down_got = trade(up_send, "z", 0), trade(down_send, "x", 0)
    a_keep = after(a_keep, relayed)
    a_keep, a_send, b_keep, b_send = run(
        two_pairs_kernel,
        [shape((24, 1664), BF)] * 4,
        [VMEM] * 4,
        [a_keep, trade(a_send, "z", 1), b_keep, trade(b_send, "x", 1)],
    )
    pack_sends = run(
        in_again_kernel,
        [shape((8, 8704), BF)] * 4,
        [SMEM] + [VMEM] * 8,
        [s, a_keep, trade(a_send, "z", 0), b_keep, trade(b_send, "x", 0), up_keep, up_got, down_keep, down_got],
        us=1.5,
    )
    pack_sends = (after(pack_sends[0], two, far), *pack_sends[1:])
    keep, send, reduce_weight_grad = run(
        last_kernel,
        [shape((8, 3584), F32), shape((8, 2816), BF), shape((24, 768), F32)],
        [VMEM] * 4,
        spread_once(pack_sends, "y"),
    )
    input_weight_grad, expand_weight_grad, output_weight_grad, table = run(
        owned_kernel,
        [shape((6, 2304), F32), shape((6, 3072), F32), shape((6, 768), F32), shape((16, 8), F32)],
        [SMEM] + [VMEM] * 2,
        [s, keep, swap(send)],
    )
    (grad_input,) = run(
        input_kernel,
        [shape((128, 768), F32)],
        [VMEM] * 7,
        [own, near, two, far, tokens, grad_middle, vec],
    )
    vectors = [table[k, 0:6] for k in range(12)]
    return (
        layer_out,
        grad_input,
        vectors[0],
        vectors[1],
        input_weight_grad,
        vectors[2],
        vectors[3],
        output_weight_grad,
        vectors[4],
        vectors[5],
        vectors[6],
        expand_weight_grad,
        table[8:12, 0:6].reshape(24),
        reduce_weight_grad,
        vectors[7],
    )


def solution(mesh):
    fine = Mesh(mesh.devices.reshape(2, 2, 4, 2, 4), ("zl", "c", "x", "zh", "y"))
    token = P(("x", "zh", "y", "zl", "c"))
    param = P(("zl", "c", "x", "zh", "y"))
    return jax.shard_map(
        local,
        mesh=fine,
        in_specs=(token, token, P(("x", "zh", "y"))) + (param,) * 13,
        out_specs=(token, token) + (param,) * 13,
        check_vma=False,
    )
```

```python
import jax
import jax.numpy as jnp
from jax import lax
from jax.experimental import pallas as pl
from jax.experimental.pallas import tpu as pltpu
from jax.sharding import Mesh
from jax.sharding import PartitionSpec as P

CHIPS = ("zl", "x", "zh", "y")
BF = jnp.bfloat16
F32 = jnp.float32
I32 = jnp.int32
SMEM = pl.BlockSpec(memory_space=pltpu.SMEM)
VMEM = pl.BlockSpec(memory_space=pltpu.VMEM)
HBM = pl.BlockSpec(memory_space=pltpu.HBM)


def chip_shift(value, distance):
    def at(place):
        place = place % 64
        zl, rest = place % 2, place // 2
        y, rest = rest % 4, rest // 4
        zh, x = rest % 2, rest // 2
        return ((zl * 4 + x) * 2 + zh) * 4 + y

    return lax.ppermute(value, CHIPS, [(at(t), at(t + distance)) for t in range(64)])


def swap(value):
    return lax.ppermute(value, "c", [(0, 1), (1, 0)])


def ring_shift(value, axis, distance):
    if axis == "z":
        place = [0, 2, 1, 3]
        return lax.ppermute(
            value, ("zl", "zh"), [(place[i], place[(i + distance) % 4]) for i in range(4)]
        )
    return lax.ppermute(value, axis, [(i, (i + distance) % 4) for i in range(4)])


def trade(value, axis, step):
    def at(core, place):
        if axis == "z":
            return ((place % 2) * 2 + core) * 2 + place // 2
        return core * 4 + place

    pairs = []
    for core in range(2):
        flip = 1 if core == step else 3
        pairs += [(at(core, m), at(core, m ^ flip)) for m in range(4)]
    return lax.ppermute(value, ("zl", "c", "zh") if axis == "z" else ("c", axis), pairs)


def around(value, axis):
    pair = jnp.stack([value, trade(value, axis, 0)])
    return pair, trade(pair, axis, 1)


def around_once(value, axis):
    after = ring_shift(value, axis, 1), ring_shift(value, axis, 3), ring_shift(value, axis, 2)
    return (value, after[0], after[2], after[1])


def spread_once(blocks, axis):
    got = (
        ring_shift(blocks[1], axis, 1),
        ring_shift(blocks[3], axis, 3),
        ring_shift(blocks[2], axis, 2),
    )
    return (blocks[0], got[0], got[2], got[1])


def after(value, *others):
    return lax.optimization_barrier((value, others))[0]


def shape(dims, kind):
    return jax.ShapeDtypeStruct(dims, kind)


def run(body, outs, specs, args, scratch=(), out_specs=None, us=1.0, vmem=24):
    return pl.pallas_call(
        body,
        out_shape=tuple(outs),
        in_specs=list(specs),
        out_specs=tuple(out_specs or [VMEM] * len(outs)),
        scratch_shapes=list(scratch),
        name=body.__name__,
        cost_estimate=pl.CostEstimate(
            flops=int(us * 600e6), bytes_accessed=int(us * 1.5e6), transcendentals=0
        ),
        compiler_params=pltpu.CompilerParams(vmem_limit_bytes=vmem << 20),
    )(*args)


def dot(left, right):
    return jnp.dot(left, right, preferred_element_type=F32)


def dot_t(left, right):
    return lax.dot_general(left, right, (((1,), (1,)), ((), ())), preferred_element_type=F32)


def outer(left, right):
    return lax.dot_general(left, right, (((0,), (0,)), ((), ())), preferred_element_type=F32)


def places(s_ref):
    return s_ref[0], s_ref[1], s_ref[2], s_ref[3], s_ref[4]


def wrap(value):
    return lax.rem(value + 4, 4)


def seat(place, core, j):
    return place ^ (0, 1 + 2 * core, 3 - 2 * core, 2)[j]


def unit_table(transposed):
    dims = (1536, 384) if transposed else (384, 1536)
    unit = lax.broadcasted_iota(I32, dims, 0 if transposed else 1)
    group = (unit * 2731) >> 16
    rest = unit - group * 24
    spot = group * 6 + rest - 6 * ((rest * 43) >> 8)
    return jnp.where(
        spot == lax.broadcasted_iota(I32, dims, 1 if transposed else 0), 1.0, 0.0
    ).astype(BF)


def unit_quarter():
    unit = lax.broadcasted_iota(I32, (8, 1536), 1)
    rest = unit - 24 * ((unit * 2731) >> 16)
    return ((rest * 43) >> 8) == lax.broadcasted_iota(I32, (8, 1536), 0)


def flat(blocks):
    count, _, columns = blocks.shape
    return blocks.astype(F32).reshape(count * 24, columns).astype(BF)


def cut(rows):
    return rows.reshape(rows.shape[0] // 24, 24, rows.shape[1]).astype(BF)


def move_all(copies):
    for source, target in copies:
        target[...] = source[...]


def unit_of(values):
    centered = values - jnp.mean(values, -1, keepdims=True)
    scale = lax.rsqrt(jnp.mean(centered * centered, -1, keepdims=True) + 1e-05)
    return centered * scale, scale


def norm_backward(grad_out, unit, scale, gain):
    scaled = grad_out * gain
    return scale * (
        scaled
        - jnp.mean(scaled, -1, keepdims=True)
        - unit * jnp.mean(scaled * unit, -1, keepdims=True)
    )


def halves_kernel(s_ref, in_hbm, up_hbm, *refs):
    vectors, (mine_ref, send_ref, in_ref, up_ref), held, sems = (
        refs[0:9], refs[9:13], refs[13:22], refs[22]
    )
    moves = [
        pltpu.make_async_copy(a, b, sems.at[i])
        for i, (a, b) in enumerate(zip((in_hbm, up_hbm, *vectors), (in_ref, up_ref, *held)))
    ]
    for move in moves:
        move.start()
    for move in moves:
        move.wait()
    core = s_ref[0]
    v0, v1, v2, v3, v4, v5, v6, v7, v8 = held
    rows = [v[...].astype(F32) for v in (v0, v1, v2, v3, v4, v5, v6, v7)]
    rows += [v8[...].astype(F32)[:, k * 6 : k * 6 + 6] for k in range(4)]
    rows = jnp.concatenate(rows + [jnp.zeros((4, 6), F32)], 0)
    small = jnp.concatenate(
        [jnp.concatenate([rows, jnp.zeros((16, 122), F32)], 1), jnp.zeros((112, 128), F32)], 0
    ).T[0:6, :]

    def half(which):
        parts = [in_ref[:, j * 384 + which * 192 : j * 384 + which * 192 + 192] for j in range(6)]
        parts.append(small)
        parts += [up_ref[:, j * 1536 + which * 768 : j * 1536 + which * 768 + 768] for j in range(2)]
        return jnp.concatenate([p.astype(F32) for p in parts], 1)

    first, second = half(0), half(1)
    mine_ref[0:6, :] = jnp.where(core == 0, first, second).astype(BF)
    send_ref[0:6, :] = jnp.where(core == 0, second, first).astype(BF)
    mine_ref[6:8, :] = jnp.zeros((2, 2816), BF)
    send_ref[6:8, :] = jnp.zeros((2, 2816), BF)


def pack_kernel(mine_ref, other_ref, out_ref, pack_ref):
    pack_ref[:, 0:2816] = mine_ref[...]
    pack_ref[:, 2816:5632] = other_ref[...]
    pack_ref[0:6, 5632:] = out_ref[...]
    pack_ref[6:8, 5632:] = jnp.zeros((2, 768), BF)


def rows_kernel(s_ref, p0, p1, p2, p3, a_ref, b_ref, up_ref):
    y = s_ref[3]
    pieces = [p[...].astype(F32) for p in (p0, p1, p2, p3)]
    parts = []
    for place in range(4):
        d = wrap(y - place)
        block = pieces[0]
        for k in (1, 2, 3):
            block = jnp.where(d == k, pieces[k], block)
        parts.append(block[0:6])
    rows = jnp.concatenate(parts, 0).astype(BF)
    a_ref[:, 0:1280] = rows[:, 0:1280]
    a_ref[:, 1280:] = rows[:, 5632:6016]
    b_ref[:, 0:1280] = rows[:, 2816:4096]
    b_ref[:, 1280:] = rows[:, 6016:]
    up_ref[:, 0:1536] = rows[:, 1280:2816]
    up_ref[:, 1536:3072] = rows[:, 4096:5632]


def half_row(row, core):
    first = jnp.concatenate([row[:, 0:192], row[:, 384:576]], 1)
    second = jnp.concatenate([row[:, 192:384], row[:, 576:768]], 1)
    return jnp.where(core == 0, first, second)


def project_kernel(
    s_ref, m0, m12, m3, m4, o_ref, w0, w1, w2, w3,
    low_ref, win_ref, wout_ref, vec_ref, q_ref, kv_ref, mask_ref, up_ref,
    win, wout,
):
    core, x, z, _, chip = places(s_ref)
    mine = (m0, m12.at[0], m12.at[1], m3, m4)
    copies = []
    for j in range(4):
        for i in range(4):
            for k, c in enumerate((core, 1 - core)):
                outer_, inner_ = ((x, z), (z, x))[k]
                outer_, inner_ = seat(outer_, core, j), seat(inner_, core, i)
                xs, zs = ((outer_, inner_), (inner_, outer_))[k]
                base = xs * 2 + (zs >> 1)
                zl = zs & 1
                piece = ((w0, w1), (w2, w3))[k][j // 2]
                copies.append(
                    (piece.at[j % 2, i, :, pl.ds(0, 1280)], win.at[zl * 16 + c * 8 + base])
                )
                copies.append(
                    (
                        piece.at[j % 2, i, :, pl.ds(1280, 384)],
                        wout.at[zl * 8 + base, :, pl.ds(k * 384, 384)],
                    )
                )
    move_all(copies)
    seg_rows = []
    for i in range(5):
        seg_rows.append(mine[i][128:136, 0:128].astype(F32)[0:1])
        seg_rows.append(o_ref[i, 128:136, 0:128].astype(F32)[0:1])
    seg_query = jnp.concatenate(seg_rows[8:], 1)
    seg_cols = jnp.concatenate(seg_rows + [jnp.zeros((118, 128), F32)], 0).T
    lane = lax.broadcasted_iota(I32, (1, 256), 1)
    start = chip * 256
    pos_query = jnp.where(lane < 128, start + core * 128 + lane, start + (1 - core) * 128 + lane - 128)
    for b in range(10):
        i, k = b // 2, b % 2
        first = start - (4 - i) * 256 + (core if k == 0 else 1 - core) * 128
        pos = first + lax.broadcasted_iota(I32, (128, 256), 0)
        allowed = (seg_cols[:, b : b + 1] == seg_query) & (pos <= pos_query) & (pos >= 0)
        mask_ref[b * 128 : (b + 1) * 128, :] = jnp.where(allowed, 0.0, -1e30)
    win_ref[...] = flat(win[...])
    wout_ref[...] = flat(wout[...])
    vec_ref[...] = win_ref[:, 1152:1280].astype(F32).T[0:16]
    gain, shift = vec_ref[0:1, :], vec_ref[1:2, :]
    bias_q = half_row(vec_ref[2:3, :], core)
    bias_v = half_row(vec_ref[3:4, :], core)
    bias_kv = jnp.concatenate([jnp.zeros((1, 384), F32), bias_v], 1)
    for i in range(5):
        values = jnp.concatenate([mine[i][0:128, :], o_ref[i, 0:128, :]], 0).astype(F32)
        unit, _ = unit_of(values)
        low = (unit * gain + shift).astype(BF)
        low_ref[i * 256 : (i + 1) * 256, :] = low
        kv_ref[i * 256 : (i + 1) * 256, :] = (dot(low, win_ref[:, 384:1152]) + bias_kv).astype(BF)
        if i == 4:
            q_ref[...] = (dot(low, win_ref[:, 0:384]) + bias_q).astype(BF) * BF(0.125)
    quarters = jnp.concatenate(
        [half_row(vec_ref[8 + k : 9 + k, :], core) for k in range(4)] + [jnp.zeros((4, 384), F32)], 0
    )
    biases = dot(quarters.astype(BF), unit_table(False))
    up_ref[...] = jnp.sum(jnp.where(unit_quarter(), biases, 0.0), 0, keepdims=True)


def attend_kernel(q_ref, kv_ref, mask_ref, wout_ref, att_ref, lse_ref, pm_ref, po_ref):
    head_lane = lax.broadcasted_iota(I32, (1, 128), 1)
    for p in range(3):
        keys = kv_ref[:, p * 128 : (p + 1) * 128]
        vals_t = kv_ref[:, 384 + p * 128 : 512 + p * 128].T
        query = q_ref[:, p * 128 : (p + 1) * 128]
        parts = []
        for h in range(2):
            picked = jnp.where((head_lane < 64) == (h == 0), query, jnp.zeros_like(query))
            scores = dot_t(keys, picked) + mask_ref[...]
            top = jnp.max(scores, 0, keepdims=True)
            expo = jnp.exp(scores - top)
            total = jnp.sum(expo, 0, keepdims=True)
            probs = (expo * (1.0 / total)).astype(BF)
            lse_ref[2 * p + h : 2 * p + h + 1, :] = top + jnp.log(total)
            parts.append(dot(vals_t[h * 64 : (h + 1) * 64], probs))
        att_ref[:, p * 128 : (p + 1) * 128] = jnp.concatenate(parts, 0).T.astype(BF)
    part = dot(att_ref[...], wout_ref[...])
    pm_ref[...] = part[0:128]
    po_ref[...] = part[128:256]


def project(s, mine, other, pieces):
    return run(
        project_kernel,
        [
            shape((1280, 768), BF),
            shape((768, 1280), BF),
            shape((384, 768), BF),
            shape((16, 768), F32),
            shape((256, 384), BF),
            shape((1280, 768), BF),
            shape((1280, 256), F32),
            shape((1, 1536), F32),
        ],
        [SMEM] + [VMEM] * 9,
        [s, *mine, other, *pieces],
        [pltpu.VMEM((32, 24, 1280), BF), pltpu.VMEM((16, 24, 768), BF)],
        us=60.0,
        vmem=20,
    )


def attend(args):
    return run(
        attend_kernel,
        [
            shape((256, 384), BF),
            shape((8, 256), F32),
            shape((128, 768), F32),
            shape((128, 768), F32),
        ],
        [VMEM] * 4,
        args,
        us=60.0,
        vmem=16,
    )


def attend_back_kernel(
    gm_ref, go_ref, att_ref, wout_ref, q_ref, kv_ref, lse_ref, mask_ref, dq, dkv, dwout
):
    grad = jnp.concatenate([gm_ref[...], go_ref[...]], 0)
    back = dot_t(grad, wout_ref[...]).astype(BF)
    head_lane = lax.broadcasted_iota(I32, (1, 128), 1)
    for p in range(3):
        keys = kv_ref[:, p * 128 : (p + 1) * 128]
        vals = kv_ref[:, 384 + p * 128 : 512 + p * 128]
        keys_t = keys.T
        query = q_ref[:, p * 128 : (p + 1) * 128]
        grad_p = back[:, p * 128 : (p + 1) * 128]
        parts = []
        dk = jnp.zeros((1280, 128), F32)
        dv = jnp.zeros((1280, 128), F32)
        for h in range(2):
            here = (head_lane < 64) == (h == 0)
            picked = jnp.where(here, query, jnp.zeros_like(query))
            grad_h = jnp.where(here, grad_p, jnp.zeros_like(grad_p))
            scores = dot_t(keys, picked) + mask_ref[...]
            probs = jnp.exp(scores - lse_ref[2 * p + h : 2 * p + h + 1, :])
            dp = dot_t(vals, grad_h)
            inner = jnp.sum(probs * dp, 0, keepdims=True)
            ds = (probs * (dp - inner)).astype(BF)
            dv = dv + dot(probs.astype(BF), grad_h)
            dk = dk + dot(ds, picked)
            parts.append(dot(keys_t[h * 64 : (h + 1) * 64], ds))
        dq[:, p * 128 : (p + 1) * 128] = (jnp.concatenate(parts, 0).T * 0.125).astype(BF)
        dkv[:, p * 128 : (p + 1) * 128] = dk.astype(BF)
        dkv[:, 384 + p * 128 : 512 + p * 128] = dv.astype(BF)
    dwout[...] = outer(att_ref[...], grad).astype(BF)


def attend_back(args):
    return run(
        attend_back_kernel,
        [shape((256, 384), BF), shape((1280, 768), BF), shape((384, 768), BF)],
        [VMEM] * 8,
        args,
        us=2.0,
        vmem=20,
    )


def early_back_kernel(
    s_ref, dq, dkv, win_ref, m0, m12, m3, m4, o_ref, dm_ref, do_ref, sums_ref
):
    core = s_ref[0]
    mine = (m0, m12.at[0], m12.at[1], m3, m4)
    gain_sum = jnp.zeros((1, 768), F32)
    shift_sum = jnp.zeros((1, 768), F32)
    value_sum = jnp.zeros((1, 384), F32)
    for i in range(5):
        rows = slice(i * 256, (i + 1) * 256)
        da = dot_t(dkv[rows, :], win_ref[:, 384:1152])
        if i == 4:
            da = da + dot_t(dq[...], win_ref[:, 0:384])
        values = jnp.concatenate([mine[i][0:128, :], o_ref[i, 0:128, :]], 0).astype(F32)
        unit, _ = unit_of(values)
        gain_sum = gain_sum + jnp.sum(da * unit, 0, keepdims=True)
        shift_sum = shift_sum + jnp.sum(da, 0, keepdims=True)
        value_sum = value_sum + jnp.sum(dkv[rows, 384:768].astype(F32), 0, keepdims=True)
        dm_ref[i] = da[0:128]
        do_ref[i] = da[128:256].astype(BF)
    query_sum = jnp.sum(dq[...].astype(F32), 0, keepdims=True)
    sums_ref[0:1, :] = gain_sum
    sums_ref[1:2, :] = shift_sum
    sums_ref[2:3, :] = widened(query_sum, core)
    sums_ref[3:4, :] = widened(value_sum, core)
    sums_ref[4:8, :] = jnp.zeros((4, 768), F32)


def early_back(args):
    return run(
        early_back_kernel,
        [shape((5, 128, 768), F32), shape((5, 128, 768), BF), shape((8, 768), F32)],
        [SMEM] + [VMEM] * 8,
        args,
        us=2.0,
        vmem=20,
    )


def widened(row, core):
    zero = jnp.zeros((1, 192), F32)
    a, b = row[:, 0:192], row[:, 192:384]
    return jnp.where(
        core == 0,
        jnp.concatenate([a, zero, b, zero], 1),
        jnp.concatenate([zero, a, zero, b], 1),
    )


def weight_back_kernel(
    s_ref, dq, dkv, dwo_ref, low_ref, sums_ref, more_ref, ups_ref, s0, s1, s2, s3, dwin, dwout
):
    core, x, z, _, _ = places(s_ref)
    dwin[:, :, 0:384] = cut(outer(low_ref[1024:1280, :], dq[...]))
    dwin[:, :, 384:1152] = cut(outer(low_ref[...], dkv[...]))
    dwout[...] = cut(dwo_ref[...].astype(F32))
    quarters = dot(jnp.where(unit_quarter(), ups_ref[...], 0.0).astype(BF), unit_table(True))
    table = jnp.concatenate(
        [
            more_ref[0:4, :],
            sums_ref[0:4, :],
            *[widened(quarters[k : k + 1, :], core) for k in range(4)],
            jnp.zeros((116, 768), F32),
        ],
        0,
    )
    dwin[:, :, 1152:1280] = cut(table.T)
    copies = []
    for j in range(4):
        for i in range(4):
            for k, c in enumerate((core, 1 - core)):
                first = seat((x, z)[k], core, j)
                xs, zs = ((first, i), (i, first))[k]
                base = xs * 2 + (zs >> 1)
                zl = zs & 1
                piece = ((s0, s1), (s2, s3))[k][j // 2]
                copies.append(
                    (dwin.at[zl * 16 + c * 8 + base], piece.at[j % 2, i, :, pl.ds(0, 1280)])
                )
                copies.append(
                    (
                        dwout.at[zl * 8 + base, :, pl.ds(k * 384, 384)],
                        piece.at[j % 2, i, :, pl.ds(1280, 384)],
                    )
                )
    move_all(copies)


def weight_back(args):
    return run(
        weight_back_kernel,
        [shape((2, 4, 24, 1664), BF)] * 4,
        [SMEM] + [VMEM] * 7,
        args,
        [pltpu.VMEM((32, 24, 1280), BF), pltpu.VMEM((16, 24, 768), BF)],
        us=2.0,
        vmem=20,
    )


def middle_kernel(x_ref, a_ref, b_ref, vec_ref, mid_ref, low_ref):
    middle = x_ref[...].astype(F32) + (a_ref[...] + b_ref[...]) + vec_ref[4:5, :]
    unit, _ = unit_of(middle)
    mid_ref[...] = middle
    low_ref[...] = (unit * vec_ref[5:6, :] + vec_ref[6:7, :]).astype(BF)


def forward_kernel(
    s_ref, am_ref, ao_ref, gm_ref, go_ref, bias_ref, e0, e1, r0, r1,
    om_ref, oo_ref, dm_ref, do_ref, ups_ref, p0, p1, t0, t1,
    wup3, wdown3, wup, wdown, dup, ddown,
):
    core, x, z, y, _ = places(s_ref)
    copies = []
    for j in range(4):
        xs = seat(x, core, j)
        for i in range(4):
            zs = seat(z, core, i)
            base = (zs & 1) * 16 + xs * 2 + (zs >> 1)
            for k, c in enumerate((core, 1 - core)):
                copies.append(
                    (
                        (e0, e1)[j // 2].at[j % 2, i, :, pl.ds(k * 1536, 1536)],
                        wup3.at[base + c * 8],
                    )
                )
    for j in range(4):
        for iz in range(4):
            zs = seat(z, core, iz)
            for ix in range(4):
                base = (zs & 1) * 32 + (zs >> 1) * 4 + seat(x, core, ix) * 8 + seat(y, core, j)
                copies.append(((r0, r1)[j // 2].at[j % 2, ix, iz], wdown3.at[base]))
    move_all(copies)
    low = jnp.concatenate([am_ref[...], ao_ref[...]], 0)
    grad = jnp.concatenate([gm_ref[...], go_ref[...]], 0)
    low_t = low.T
    out = jnp.zeros((256, 768), F32)
    da = jnp.zeros((256, 768), F32)
    for b in range(2):
        cols = slice(b * 768, (b + 1) * 768)
        blocks = slice(b * 32, (b + 1) * 32)
        wup[:, cols] = flat(wup3[:, :, cols])
        hidden = dot(low, wup[:, cols]) + bias_ref[:, cols]
        square = hidden * hidden
        bent = jnp.tanh(0.7978845608 * hidden * (1.0 + 0.044715 * square))
        rest = 0.5 * (1.0 + bent)
        active = (hidden * rest).astype(BF)
        slope = rest + 0.5 * hidden * (1.0 - bent * bent) * (
            0.7978845608 * (1.0 + 3.0 * 0.044715 * square)
        )
        wdown[cols, :] = flat(wdown3[blocks])
        back = (dot_t(grad, wdown[cols, :]) * slope).astype(BF)
        out = out + dot(active, wdown[cols, :])
        da = da + dot_t(back, wup[:, cols])
        ddown[blocks] = cut(outer(active, grad))
        dup[:, :, cols] = cut(dot(low_t, back))
        ups_ref[:, cols] = jnp.sum(back.astype(F32), 0, keepdims=True)
        copies = []
        for j in range(4):
            xs = seat(x, core, j)
            for i in range(4):
                base = (i % 2) * 16 + xs * 2 + i // 2
                for k, c in enumerate((core, 1 - core)):
                    copies.append(
                        (
                            dup.at[base + c * 8, :, pl.ds(b * 768, 768)],
                            (p0, p1)[j // 2].at[j % 2, i, :, pl.ds(k * 1536 + b * 768, 768)],
                        )
                    )
        move_all(copies)
    copies = []
    for j in range(4):
        zs = seat(z, core, j)
        for ix in range(4):
            for iy in range(4):
                copies.append(
                    (
                        ddown.at[(zs & 1) * 32 + ix * 8 + (zs >> 1) * 4 + iy],
                        (t0, t1)[j // 2].at[j % 2, ix, iy],
                    )
                )
    move_all(copies)
    om_ref[...] = out[0:128]
    oo_ref[...] = out[128:256]
    dm_ref[...] = da[0:128]
    do_ref[...] = da[128:256]


def forward(args):
    return run(
        forward_kernel,
        [shape((128, 768), F32)] * 4
        + [shape((1, 1536), F32)]
        + [shape((2, 4, 24, 3072), BF)] * 2
        + [shape((2, 4, 4, 24, 768), BF)] * 2,
        [SMEM] + [VMEM] * 9,
        args,
        [
            pltpu.VMEM((32, 24, 1536), BF),
            pltpu.VMEM((64, 24, 768), BF),
            pltpu.VMEM((768, 1536), BF),
            pltpu.VMEM((1536, 768), BF),
            pltpu.VMEM((32, 24, 1536), BF),
            pltpu.VMEM((64, 24, 768), BF),
        ],
        us=6.0,
        vmem=24,
    )


def middle_back_kernel(
    mid_ref, om_ref, ox_ref, dm_ref, dx_ref, g_ref, vec_ref, out_ref, gmid_ref, low_ref, sums_ref
):
    middle = mid_ref[...]
    out_ref[...] = (middle + (om_ref[...] + ox_ref[...]) + vec_ref[7:8, :]).astype(BF)
    unit, scale = unit_of(middle)
    da = dm_ref[...] + dx_ref[...]
    grad = g_ref[...].astype(F32)
    total = grad + norm_backward(da, unit, scale, vec_ref[5:6, :])
    low = total.astype(BF)
    gmid_ref[...] = total
    low_ref[...] = low
    sums_ref[0:1, :] = jnp.sum(low.astype(F32), 0, keepdims=True)
    sums_ref[1:2, :] = jnp.sum(da * unit, 0, keepdims=True)
    sums_ref[2:3, :] = jnp.sum(da, 0, keepdims=True)
    sums_ref[3:4, :] = jnp.sum(grad, 0, keepdims=True)
    sums_ref[4:8, :] = jnp.zeros((4, 768), F32)


def added(refs, index=None):
    total = None
    for ref in refs:
        value = (ref[...] if index is None else ref[index]).astype(F32)
        total = value if total is None else total + value
    return total


def total_of(keep, got, *index):
    if not index:
        return keep[...].astype(F32) + got[...].astype(F32)
    return keep[index].astype(F32) + got[index].astype(F32)


def pair_kernel(keep, got, mine, send):
    mine[...] = total_of(keep, got, 0).astype(BF)
    send[...] = total_of(keep, got, 1).astype(BF)


def two_pairs_kernel(ka, ga, kb, gb, ma, sa, mb, sb):
    pair_kernel(ka, ga, ma, sa)
    pair_kernel(kb, gb, mb, sb)


def up_down_kernel(s_ref, ka, ga, kb, gb, ma, sa, mb, sb):
    core, x, z, _, _ = places(s_ref)
    for j in range(4):
        (ma, sa)[j // 2][j % 2] = total_of(ka, ga, seat(z, core, j)).astype(BF)
        (mb, sb)[j // 2][j % 2] = total_of(kb, gb, seat(x, core, j)).astype(BF)


def in_kernel(s_ref, ka, ga, kb, gb, ma, sa, mb, sb):
    core, x, z, _, _ = places(s_ref)
    for j in range(4):
        (ma, sa)[j // 2][j % 2] = total_of(ka, ga, seat(z, core, j)).astype(BF)
        (mb, sb)[j // 2][j % 2] = total_of(kb, gb, seat(x, core, j)).astype(BF)


def in_again_kernel(s_ref, ka, ga, kb, gb, ku, gu, kd, gd, o0, o1, o2, o3):
    y = s_ref[3]
    a, b, up = total_of(ka, ga), total_of(kb, gb), total_of(ku, gu)
    rows = jnp.concatenate(
        [a[:, 0:1280], up[:, 0:1536], b[:, 0:1280], up[:, 1536:], a[:, 1280:], b[:, 1280:]], 1
    )
    parts = [rows[i * 6 : i * 6 + 6] for i in range(4)]
    for k, out in enumerate((o0, o1, o2, o3)):
        ys = wrap(y + k)
        block = parts[0]
        for i in (1, 2, 3):
            block = jnp.where(ys == i, parts[i], block)
        out[0:6, 0:6400] = block.astype(BF)
        out[6:8, 0:6400] = jnp.zeros((2, 6400), BF)
        down = total_of(kd, gd, ys)
        down = jnp.concatenate([down[0:8], down[8:16], down[16:24]], 1)
        out[:, 6400:] = down.astype(BF)


def last_kernel(a0, a1, a2, a3, keep_ref, send_ref, down_ref):
    total = added((a0, a1, a2, a3))
    keep_ref[:, 0:2816] = total[:, 0:2816]
    keep_ref[:, 2816:] = total[:, 5632:6400]
    send_ref[...] = total[:, 2816:5632].astype(BF)
    for i in range(3):
        down_ref[i * 8 : i * 8 + 8, :] = total[:, 6400 + i * 768 : 7168 + i * 768]


def owned_kernel(s_ref, keep_ref, got_ref, in_ref, up_ref, out_ref, sums_ref):
    core = s_ref[0]
    mine = keep_ref[:, 0:2816]
    other = got_ref[...].astype(F32)
    first = jnp.where(core == 0, mine, other)
    second = jnp.where(core == 0, other, mine)
    for j in range(6):
        part = slice(j * 192, j * 192 + 192)
        in_ref[:, j * 384 : j * 384 + 192] = first[0:6, part]
        in_ref[:, j * 384 + 192 : j * 384 + 384] = second[0:6, part]
    for j in range(2):
        part = slice(1280 + j * 768, 2048 + j * 768)
        up_ref[:, j * 1536 : j * 1536 + 768] = first[0:6, part]
        up_ref[:, j * 1536 + 768 : j * 1536 + 1536] = second[0:6, part]
    out_ref[...] = keep_ref[0:6, 2816:]
    sums_ref[...] = (mine[:, 1152:1280] + other[:, 1152:1280]).T[0:16, :]


def halo_kernel(dm_ref, dx_ref, own_ref, near_ref, two_ref, far_ref):
    far_ref[...] = total_of(dm_ref, dx_ref, 0).astype(BF)
    near_ref[0] = total_of(dm_ref, dx_ref, 1).astype(BF)
    near_ref[1] = total_of(dm_ref, dx_ref, 3).astype(BF)
    two_ref[...] = total_of(dm_ref, dx_ref, 2)
    own_ref[...] = total_of(dm_ref, dx_ref, 4)


def relay_kernel(two_ref, got_ref, out_ref):
    out_ref[...] = (two_ref[...] + got_ref[0].astype(F32)).astype(BF)


def input_kernel(own_ref, near_ref, two_ref, far_ref, x_ref, gmid_ref, vec_ref, out_ref):
    total = own_ref[...] + near_ref[1].astype(F32) + two_ref[...].astype(F32)
    total = total + far_ref[...].astype(F32)
    unit, scale = unit_of(x_ref[...].astype(F32))
    out_ref[...] = gmid_ref[...] + norm_backward(total, unit, scale, vec_ref[0:1, :])


def local(
    tokens,
    cotangent,
    segments,
    first_gain,
    first_shift,
    input_weight,
    query_bias,
    value_bias,
    output_weight,
    output_bias,
    second_gain,
    second_shift,
    expand_weight,
    expand_bias,
    reduce_weight,
    reduce_bias,
):
    core = lax.axis_index("c")
    zl, zh = lax.axis_index("zl"), lax.axis_index("zh")
    x, y = lax.axis_index("x"), lax.axis_index("y")
    chip = ((x * 2 + zh) * 4 + y) * 2 + zl
    s = jnp.stack([core, x, zh * 2 + zl, y, chip]).astype(I32)
    seg_own = lax.dynamic_slice_in_dim(segments, (zl * 2 + core) * 128, 128).astype(BF)
    ext = jnp.concatenate([tokens, jnp.pad(seg_own[None], ((0, 7), (0, 640)))], 0)
    grad_other = swap(cotangent)
    far = chip_shift(ext, 4)
    down_z = around(reduce_weight, "z")
    small = [
        first_gain,
        first_shift,
        query_bias,
        value_bias,
        output_bias,
        second_gain,
        second_shift,
        reduce_bias,
        expand_bias,
    ]
    mine, send = run(
        halves_kernel,
        [shape((8, 2816), BF)] * 2,
        [SMEM] + [HBM] * 11,
        [s, *[pltpu.with_memory_space_constraint(v, pltpu.HBM) for v in (input_weight, expand_weight, *[v[None] for v in small])]],
        [pltpu.VMEM((6, 2304), BF), pltpu.VMEM((6, 3072), BF)]
        + [pltpu.VMEM((1, 6), BF)] * 8
        + [pltpu.VMEM((1, 24), BF), pltpu.SemaphoreType.DMA((11,))],
    )
    other = swap(send)
    (pack,) = run(
        pack_kernel, [shape((8, 6400), BF)], [VMEM] * 3, [mine, other, output_weight], us=0.7
    )
    part_a, part_b, up_part = run(
        rows_kernel,
        [shape((24, 1664), BF), shape((24, 1664), BF), shape((24, 3072), BF)],
        [SMEM] + [VMEM] * 4,
        [s, *around_once(pack, "y")],
        us=1.5,
    )
    down_x = around(jnp.concatenate(down_z, 0), "x")
    near = chip_shift(after(ext, part_a), 1)
    pair_a = jnp.stack([part_a, trade(part_a, "z", 0)])
    pair_b = jnp.stack([part_b, trade(part_b, "x", 0)])
    up_pair = jnp.stack([up_part, trade(up_part, "z", 0)])
    all_a = jnp.concatenate([pair_a, trade(pair_a, "z", 1)], 0)
    all_b = jnp.concatenate([pair_b, trade(pair_b, "x", 1)], 0)
    up_z = jnp.concatenate([up_pair, trade(up_pair, "z", 1)], 0)
    down_pieces = around(jnp.concatenate(down_x, 0), "y")
    middle_two = chip_shift(jnp.stack([after(near, all_a), ext]), 2)
    chunks = [far, middle_two, near, ext]
    pair_a = jnp.stack([all_a, trade(all_a, "x", 0)])
    pair_b = jnp.stack([all_b, trade(all_b, "z", 0)])
    in_a = (pair_a, trade(pair_a, "x", 1))
    in_b = (pair_b, trade(pair_b, "z", 1))
    chunks_other = swap(jnp.concatenate([far[None], middle_two, near[None], ext[None]], 0))
    up_pair = jnp.stack([up_z, trade(up_z, "x", 0)])
    up_pair = after(up_pair, in_a[1], in_b[1])
    up_pieces = (up_pair, trade(up_pair, "x", 1))

    low, win, wout, vec, query, pair, mask, bias_up = project(
        s, chunks, chunks_other, in_a + in_b
    )
    att, lse, part_m, part_o = attend([query, pair, mask, wout])
    middle, low_two = run(
        middle_kernel,
        [shape((128, 768), F32), shape((128, 768), BF)],
        [VMEM] * 4,
        [tokens, part_m, swap(part_o), vec],
    )
    (out_m, out_o, da_m, da_o, ups, up_keep, up_send, down_keep, down_send) = forward(
        [s, low_two, swap(low_two), cotangent, grad_other, bias_up, *up_pieces, *down_pieces]
    )
    layer_out, grad_middle, grad_branch, sums = run(
        middle_back_kernel,
        [shape((128, 768), BF), shape((128, 768), F32), shape((128, 768), BF), shape((8, 768), F32)],
        [VMEM] * 7,
        [middle, out_m, swap(out_o), da_m, swap(da_o), cotangent, vec],
        us=2.0,
    )
    up_got = trade(up_send, "x", 1)
    down_got = trade(down_send, "z", 1)
    dq, dkv, dwout = attend_back(
        [grad_branch, swap(grad_branch), att, wout, query, pair, lse, mask]
    )
    up_got = after(up_got, dq)
    up_keep, up_send, down_keep, down_send = run(
        two_pairs_kernel,
        [shape((4, 24, 3072), BF)] * 2 + [shape((4, 4, 24, 768), BF)] * 2,
        [VMEM] * 4,
        [up_keep, up_got, down_keep, down_got],
        us=2.0,
    )
    up_got, down_got = trade(up_send, "x", 0), trade(down_send, "z", 0)
    da_mine, da_other, more = early_back(
        [s, after(dq, up_keep), dkv, win, *chunks, chunks_other]
    )
    a_keep, a_send, b_keep, b_send = weight_back([s, dq, dkv, dwout, low, sums, more, ups])
    up_got = after(up_got, a_keep)
    a_got, b_got = trade(a_send, "x", 1), trade(b_send, "z", 1)
    up_keep, up_send, down_keep, down_send = run(
        up_down_kernel,
        [shape((2, 24, 3072), BF)] * 2 + [shape((2, 4, 24, 768), BF)] * 2,
        [SMEM] + [VMEM] * 4,
        [s, up_keep, up_got, down_keep, down_got],
        us=1.5,
    )
    own, near, two, far = run(
        halo_kernel,
        [
            shape((128, 768), F32),
            shape((2, 128, 768), BF),
            shape((128, 768), F32),
            shape((128, 768), BF),
        ],
        [VMEM] * 2,
        [after(da_mine, up_keep), swap(da_other)],
    )
    near, far = chip_shift(near, -1), chip_shift(far, -4)
    (two,) = run(relay_kernel, [shape((128, 768), BF)], [VMEM] * 2, [two, near], us=0.5)
    relayed = two
    two = chip_shift(two, -2)
    a_keep = after(a_keep, own)
    up_got, down_got = trade(up_send, "z", 1), trade(down_send, "x", 1)
    a_keep, a_send, b_keep, b_send = run(
        two_pairs_kernel,
        [shape((4, 24, 1664), BF)] * 4,
        [VMEM] * 4,
        [a_keep, a_got, b_keep, b_got],
        us=1.5,
    )
    a_keep, a_send, b_keep, b_send = run(
        in_kernel,
        [shape((2, 24, 1664), BF)] * 4,
        [SMEM] + [VMEM] * 4,
        [s, a_keep, trade(a_send, "x", 0), b_keep, trade(b_send, "z", 0)],
    )
    up_keep, up_send, down_keep, down_send = run(
        two_pairs_kernel,
        [shape((24, 3072), BF)] * 2 + [shape((4, 24, 768), BF)] * 2,
        [VMEM] * 4,
        [up_keep, after(up_got, a_keep), down_keep, down_got],
    )
    up_got, down_got = trade(up_send, "z", 0), trade(down_send, "x", 0)
    a_keep = after(a_keep, relayed)
    a_keep, a_send, b_keep, b_send = run(
        two_pairs_kernel,
        [shape((24, 1664), BF)] * 4,
        [VMEM] * 4,
        [a_keep, trade(a_send, "z", 1), b_keep, trade(b_send, "x", 1)],
    )
    pack_sends = run(
        in_again_kernel,
        [shape((8, 8704), BF)] * 4,
        [SMEM] + [VMEM] * 8,
        [s, a_keep, trade(a_send, "z", 0), b_keep, trade(b_send, "x", 0), up_keep, up_got, down_keep, down_got],
        us=1.5,
    )
    keep, send, reduce_weight_grad = run(
        last_kernel,
        [shape((8, 3584), F32), shape((8, 2816), BF), shape((24, 768), F32)],
        [VMEM] * 4,
        spread_once(pack_sends, "y"),
    )
    input_weight_grad, expand_weight_grad, output_weight_grad, table = run(
        owned_kernel,
        [shape((6, 2304), F32), shape((6, 3072), F32), shape((6, 768), F32), shape((16, 8), F32)],
        [SMEM] + [VMEM] * 2,
        [s, keep, swap(send)],
    )
    (grad_input,) = run(
        input_kernel,
        [shape((128, 768), F32)],
        [VMEM] * 7,
        [own, near, two, far, tokens, grad_middle, vec],
    )
    vectors = [table[k, 0:6] for k in range(12)]
    return (
        layer_out,
        grad_input,
        vectors[0],
        vectors[1],
        input_weight_grad,
        vectors[2],
        vectors[3],
        output_weight_grad,
        vectors[4],
        vectors[5],
        vectors[6],
        expand_weight_grad,
        table[8:12, 0:6].reshape(24),
        reduce_weight_grad,
        vectors[7],
    )


def solution(mesh):
    fine = Mesh(mesh.devices.reshape(2, 2, 4, 2, 4), ("zl", "c", "x", "zh", "y"))
    token = P(("x", "zh", "y", "zl", "c"))
    param = P(("zl", "c", "x", "zh", "y"))
    return jax.shard_map(
        local,
        mesh=fine,
        in_specs=(token, token, P(("x", "zh", "y"))) + (param,) * 13,
        out_specs=(token, token) + (param,) * 13,
        check_vma=False,
    )
```
